256 devices in a mesh: tile: 16 (over z, core), bank: 16 (over y, x).
Axes of the slice: x: 4, y: 4, z: 8, core: 2. Of those that a mesh axis runs over, the one named last changes fastest.
Arguments:
- volume: bfloat16 [1024, 1024, 128], P('tile', 'bank'), may hold values from -6 to 6
- pick_list: int32 [3, 16, 16, 16], P(None, 'tile', 'bank'), may hold values from 0 to 1023, as said below
- box_counts: int32 [16, 16], P('tile', 'bank'), may hold values from 1 to 16, as said below
- orientations: int32 [16, 16, 16, 128], P('tile', 'bank'), may hold values from 0 to 255, all different within a row
- orient_weight: int32 [16, 16, 16, 128], P('tile', 'bank'), may hold values from 1 to 4
- reference_bank: bfloat16 [256, 20, 4096], P('bank'), may hold values from -6 to 6
Outputs:
- class_sums: float32 [256, 20, 4096], P('bank')
- weight_sums: float32 [256, 20], P('bank')
The draws below stay inside these ranges and needn't reach their ends.
Inputs may be any that keep to these rules, and one draw needn't show every extreme that they name: pick_list[0, t, b, s] lies in [t * 64, (t + 1) * 64), pick_list[1, t, b, s] in [b * 64, (b + 1) * 64), and pick_list[2, t, b, s] in [0, 32]. `box_counts`: every device has at least one live slot and some device has all 16. The 128 orientations of a slot are distinct.
All inputs are finite; a program needn't handle non-finite values.
Results may differ from the reference program's by a relative error of at most 0.012.
Values may be sent and summed in bfloat16 or wider, within the bound.
A program may use at most 128 MiB of HBM per device.

```python
import jax
import jax.numpy as jnp
from jax import lax

CX = 64
CY = 64
Z = 128
MAXB = 16
B = 96
L = 16
C = 20
R = 256
KO = 128
F = 4096
NX = 1024
NY = 1024
N_TILE = 16
N_BANK = 16


def draw_pick_list(key, part):
    tiles = NX // CX
    banks = NY // CY
    key_x, key_y, key_z = jax.random.split(key, 3)
    grid_shape = (tiles, banks, MAXB)
    pos_x = jax.random.randint(key_x, grid_shape, 0, CX) + (jnp.arange(tiles) * CX)[:, None, None]
    pos_y = jax.random.randint(key_y, grid_shape, 0, CY) + (jnp.arange(banks) * CY)[None, :, None]
    pos_z = jax.random.randint(key_z, grid_shape, 0, Z - B + 1)
    pos_x = pos_x.at[0, 0, 0].set(0).at[tiles - 1, banks - 1, 0].set(NX - 1)
    pos_y = pos_y.at[0, 0, 0].set(0).at[tiles - 1, banks - 1, 0].set(NY - 1)
    pos_z = pos_z.at[0, 0, 0].set(0).at[tiles - 1, banks - 1, 0].set(Z - B)
    return jnp.stack([pos_x, pos_y, pos_z]).astype(jnp.int32)


def draw_box_counts(key, part):
    tiles = NX // CX
    banks = NY // CY
    key_a, key_b = jax.random.split(key, 2)
    drawn = jax.random.randint(key_a, (tiles * banks,), 1, MAXB + 1)
    chosen = jax.random.randint(key_b, (), 0, tiles * banks)
    drawn = jnp.where(jnp.arange(tiles * banks) == chosen, MAXB, drawn)
    return drawn.reshape(tiles, banks).astype(jnp.int32)


def place_ends(array, key, low, largest):
    index_at = [jax.random.randint(jax.random.fold_in(key, axis), (), 0, length) for axis, length in enumerate(array.shape)]
    main_axis = array.shape.index(max(array.shape))
    next_to = index_at[:main_axis] + [(index_at[main_axis] + 1) % array.shape[main_axis]] + index_at[main_axis + 1:]
    return array.at[tuple(index_at)].set(low).at[tuple(next_to)].set(largest)


def level_of(key, shape, cuts, low, largest):
    loudness = 1.0
    for axis_at, parts in cuts:
        draws = jax.random.uniform(jax.random.fold_in(jax.random.fold_in(key, 6), axis_at), (parts,), jnp.float32, low / len(cuts), largest / len(cuts))
        loudness = loudness * jnp.repeat(jnp.exp(draws), shape[axis_at] // parts).reshape((-1,) + (1,) * (len(shape) - 1 - axis_at))
    return loudness


def picks_of(own_key, rows, count, top, lift):
    ranking = jax.random.permutation(jax.random.fold_in(own_key, 1), count)
    boost = ranking
    for power in range(3):
        boost = boost * boost // count
    boost = boost * lift // count
    tickets = jax.random.randint(jax.random.fold_in(own_key, 2), (rows, count), 0, 4096) + boost
    fixed_rows = jax.random.permutation(jax.random.fold_in(own_key, 3), rows)[jnp.arange(count) % rows]
    tickets = jnp.where(jnp.arange(rows)[:, None] == fixed_rows[None, :], 1 << 14, tickets)
    merit = tickets * count + jnp.arange(count)
    return lax.top_k(merit.astype(jnp.int32), top)[1].astype(jnp.int32)


def centred(key, extent, spread, most, shards=(), dtype=jnp.bfloat16):
    result = jax.random.normal(key, extent, jnp.float32) * spread
    if len(shards) > 0:
        result = level_of(key, extent, shards, -0.22, 0.18) * result
    return jnp.clip(result, min=-most, max=most).astype(dtype)


def setup_inputs(seed: int = 0) -> dict:
    key_of = jax.random.split(jax.random.key(seed), 7)
    return {
        "volume": centred(key_of[0], (NX, NY, Z), 1.0, 6.0, ((0, 16), (1, 16))),
        "pick_list": draw_pick_list(jax.random.fold_in(key_of[6], 71), 0),
        "box_counts": draw_box_counts(jax.random.fold_in(key_of[6], 71), 0),
        "orientations": picks_of(key_of[3], N_TILE * N_BANK * MAXB, R, KO, 0).reshape((N_TILE, N_BANK, MAXB, KO)),
        "orient_weight": place_ends(jax.random.randint(key_of[4], (N_TILE, N_BANK, MAXB, KO), 1, 5), jax.random.fold_in(key_of[4], 1), 1, 4).astype(jnp.int32),
        "reference_bank": centred(key_of[5], (R, C, F), 1.0, 6.0, ((0, 16),)),
    }


EPSILON = 1e-06

def fourier_table():
    samples = jnp.arange(B).astype(jnp.float32)
    terms = jnp.arange(L)
    frequency = jnp.where(terms <= L // 2, terms, terms - L // 2).astype(jnp.float32)
    angles = 2.0 * jnp.pi * frequency[:, None] * samples[None, :] / B
    table = jnp.where((terms <= L // 2)[:, None], jnp.cos(angles), jnp.sin(angles)) / jnp.sqrt(jnp.float32(B))
    table_half = table.astype(jnp.bfloat16)
    return (table_half, table_half.astype(jnp.float32))

def box_features(box_cube, table_half, table_full):
    first = jnp.dot(box_cube.reshape(B * B, B), table_half.T, preferred_element_type=jnp.float32).reshape(B, B, L)
    second = jnp.einsum('xyc,by->xbc', first, table_full, precision=lax.Precision.HIGHEST)
    third = jnp.einsum('xbc,ax->abc', second, table_full, precision=lax.Precision.HIGHEST)
    return third.reshape(L * L * L).astype(jnp.bfloat16)

def reference(volume, pick_list, box_counts, orientations, orient_weight, reference_bank):
    table_half, table_full = fourier_table()
    half_box = B // 2
    padded = jnp.pad(volume, ((half_box, half_box), (half_box, half_box), (0, 0)))
    coords = jnp.stack([pick_list[0].reshape(-1), pick_list[1].reshape(-1), pick_list[2].reshape(-1)], axis=1).astype(jnp.int32)

    def extract_one(corner):
        box_cube = lax.dynamic_slice(padded, (corner[0], corner[1], corner[2]), (B, B, B))
        return box_features(box_cube, table_half, table_full)
    features = lax.map(extract_one, coords)
    box_total = coords.shape[0]
    slot_index = jnp.arange(MAXB).astype(jnp.int32)
    live_slots = (slot_index[None, None, :] < box_counts[:, :, None]).reshape(-1)
    orient_rows = orientations.reshape(box_total, KO)
    weight_rows = orient_weight.reshape(box_total, KO).astype(jnp.float32)
    multiplicity = jnp.zeros((box_total, R), jnp.float32).at[jnp.arange(box_total)[:, None], orient_rows].add(weight_rows)
    multiplicity = jnp.where(live_slots[:, None], multiplicity, jnp.float32(0.0)).astype(jnp.bfloat16)
    feature_wide = features.astype(jnp.float32)
    box_norm = jnp.sqrt(lax.optimization_barrier(jnp.mean(feature_wide * feature_wide, axis=1)) + EPSILON)
    bank_wide = reference_bank.astype(jnp.float32)
    ref_norm = jnp.sqrt(lax.optimization_barrier(jnp.mean(bank_wide * bank_wide, axis=2)) + EPSILON)
    scores = jnp.einsum('if,rcf->irc', feature_wide, bank_wide)
    correl = scores / (F * box_norm[:, None, None] * ref_norm[None])
    weights = (multiplicity.astype(jnp.float32)[:, :, None] * jnp.maximum(correl, 0.0)).astype(jnp.bfloat16)
    weight_wide = weights.astype(jnp.float32)
    class_sums = jnp.einsum('irc,if->rcf', weight_wide, feature_wide)
    weight_sums = lax.optimization_barrier(jnp.sum(weight_wide, axis=0))
    return (class_sums, weight_sums)
```

```python
import functools

import jax
import jax.numpy as jnp
import numpy as np
from jax import lax
from jax.experimental import pallas as pl
from jax.experimental.pallas import tpu as pltpu
from jax.sharding import PartitionSpec as P

B = 96
L = 16
R = 256
F = 4096
C = 20
CX = 64
Z = 128
HALF = 48
EX = CX + 2 * HALF
SLOTS = 16
ROWS = 320
WIDE = F + R
EPSILON = 1e-06
XS = 168
YS = 72
MESH = pl.DeviceIdType.MESH
NT = (((1,), (1,)), ((), ()))
bf16 = jnp.bfloat16
f32 = jnp.float32
VMEM_SPEC = pl.BlockSpec(memory_space=pltpu.VMEM)
SMEM_SPEC = pl.BlockSpec(memory_space=pltpu.SMEM)
LIMIT = 60 * 1024 * 1024


def base_table():
    n = np.arange(B).astype(np.float32)
    terms = np.arange(L)
    freq = np.where(terms <= L // 2, terms, terms - L // 2).astype(np.float32)
    angles = np.float32(2.0 * np.pi) * freq[:, None] * n[None, :] / np.float32(B)
    table = np.where((terms <= L // 2)[:, None], np.cos(angles), np.sin(angles)) / np.sqrt(np.float32(B))
    wide = np.zeros((L, 256), np.float32)
    wide[:, :B] = table
    return jnp.asarray(wide).astype(bf16).astype(f32)


def features_kernel(meta, table_ref, lo_ref, own_ref, hi_ref, out_ref, spread, planes, tables, mixed, rows):
    base = table_ref[...]

    def scatter(ref, first, count):
        def step(i, carry):
            spread[pl.ds(first + i, CX, stride=XS), :] = ref[i].astype(f32)
            return carry

        lax.fori_loop(0, count, step, 0, unroll=8)

    scatter(lo_ref, 0, HALF)
    scatter(own_ref, HALF, CX)
    scatter(hi_ref, HALF + CX, HALF)

    def pack(y, carry):
        planes[y] = spread[pl.ds(pl.multiple_of(y * XS, 8), EX), :].astype(bf16)
        return carry

    lax.fori_loop(0, CX, pack, 0, unroll=4)

    lane = lax.broadcasted_iota(jnp.int32, (L, 256), 1)
    pick_b = (lane // L == lax.broadcasted_iota(jnp.int32, (L, 256), 0)).astype(f32)
    collapse = (lane // L == lax.broadcasted_iota(jnp.int32, (L, 256), 0)).astype(bf16)

    for k in range(3):
        def x_table(s, carry):
            shifted = pltpu.roll(base, meta[0, k * SLOTS + s], axis=1)
            tables[pl.ds(pl.multiple_of(s * L, L), L), :] = shifted.astype(bf16)
            return carry

        lax.fori_loop(0, SLOTS, x_table, 0, unroll=2)
        x_tables = tables[:, :EX]

        def x_step(y2, carry):
            y = y2 * 2
            rhs = jnp.concatenate([planes[y], planes[y + 1]], axis=1)
            out = jnp.dot(x_tables, rhs, preferred_element_type=f32)
            mixed[pl.ds(y, 256, stride=YS), :] = out[:, :Z]
            mixed[pl.ds(y + 1, 256, stride=YS), :] = out[:, Z:]
            return carry

        lax.fori_loop(0, CX // 2, x_step, 0)

        def box(s, carry):
            part = k * SLOTS + s
            active = meta[3, part] > 0

            @pl.when(active)
            def _():
                shift = meta[1, part]
                blocks = []
                for j in range(4):
                    moved = pltpu.roll(base, (shift + CX * j) & 255, axis=1)
                    blocks.append(jnp.where(lane // CX == j, moved, 0.0))
                y_table = jnp.concatenate(blocks, axis=0).astype(bf16)
                z_table = pltpu.roll(base, meta[2, part], axis=1)[:, :Z].astype(bf16)
                z_wide = jnp.concatenate([z_table] * L, axis=0)
                start = s * (L * YS)
                parts = []
                for g in range(4):
                    rhs = jnp.concatenate(
                        [
                            mixed[pl.ds(pl.multiple_of(start + (g * 4 + a) * YS, 8), CX), :].astype(bf16)
                            for a in range(4)
                        ],
                        axis=0,
                    )
                    parts.append(jnp.dot(y_table, rhs, preferred_element_type=f32).astype(bf16))
                second = jnp.concatenate(parts, axis=0)
                third = lax.dot_general(second, z_wide, NT, preferred_element_type=f32)
                kept = (third.reshape(L, L, 256) * pick_b[None]).reshape(256, 256).astype(bf16)
                feature = jnp.dot(collapse, kept, preferred_element_type=f32)
                rows[0, pl.ds(s, L, stride=L), :] = feature[:, :128]
                rows[1, pl.ds(s, L, stride=L), :] = feature[:, 128:]

            @pl.when(jnp.logical_not(active))
            def _():
                rows[0, pl.ds(s, L, stride=L), :] = jnp.zeros((L, 128), f32)
                rows[1, pl.ds(s, L, stride=L), :] = jnp.zeros((L, 128), f32)

            return carry

        lax.fori_loop(0, SLOTS, box, 0)
        for a in range(2 * L):
            out_ref[k, :, a * 128 : (a + 1) * 128] = rows[a % 2, a // 2 * L : (a // 2 + 1) * L, :].astype(bf16)


def features_call(meta, table, lo, own, hi):
    return pl.pallas_call(
        features_kernel,
        out_shape=jax.ShapeDtypeStruct((3, SLOTS, F), bf16),
        in_specs=[SMEM_SPEC] + [VMEM_SPEC] * 4,
        out_specs=VMEM_SPEC,
        scratch_shapes=[
            pltpu.VMEM((CX * XS, Z), f32),
            pltpu.VMEM((CX, EX, Z), bf16),
            pltpu.VMEM((256, 256), bf16),
            pltpu.VMEM((256 * YS, Z), f32),
            pltpu.VMEM((2, 256, 128), f32),
        ],
        compiler_params=pltpu.CompilerParams(vmem_limit_bytes=LIMIT),
        cost_estimate=pl.CostEstimate(flops=4 * 10**9, bytes_accessed=3 * 10**6, transcendentals=0),
        name="features",
    )(meta, table, lo, own, hi)


QUARTER = 1024
HALF_LANES = WIDE // 2


def gather_kernel(own_ref, out_ref, own_sem, send_sem, recv_sem):
    bank = lax.axis_index("bank")
    y, x = bank // 4, bank % 4

    def at(axis, i, j):
        dx, dy = (i, j) if axis == 0 else (j, i)
        return ((y + dy + 4) % 4) * 4 + (x + dx + 4) % 4

    barrier = pltpu.get_barrier_semaphore()
    for axis in (0, 1):
        for d in (1, -1):
            pl.semaphore_signal(barrier, inc=1, device_id={"bank": at(axis, d, 0)}, device_id_type=MESH)
    pl.semaphore_wait(barrier, 4)

    local = pltpu.make_async_copy(own_ref, out_ref.at[bank], own_sem)
    local.start()
    sends = []
    slots = {}

    def lanes(h, q):
        start = h * HALF_LANES
        if q == 0:
            return pl.ds(start, QUARTER)
        if q == 1:
            return pl.ds(start + QUARTER, HALF_LANES - QUARTER)
        return pl.ds(start, HALF_LANES)

    def copy(h, i, j, di, dj, q):
        block = at(h, i, j)
        key = (h, i - di, j - dj, q)
        slot = slots.setdefault(key, len(slots))
        source = own_ref if (i, j) == (0, 0) else out_ref.at[block]
        return pltpu.make_async_remote_copy(
            src_ref=source.at[:, lanes(h, q)],
            dst_ref=out_ref.at[block, :, lanes(h, q)],
            send_sem=send_sem.at[slot],
            recv_sem=recv_sem.at[slot],
            device_id={"bank": at(h, di, dj)},
            device_id_type=MESH,
        )

    pending = {}

    def send(h, i, j, di, dj, q):
        c = copy(h, i, j, di, dj, q)
        c.start()
        sends.append(c)
        pending[(h, i - di, j - dj, q)] = c

    def arrive(h, i, j, q):
        pending.pop((h, i, j, q)).wait_recv()

    for h in (0, 1):
        send(h, 0, 0, 1, 0, 2)
        send(h, 0, 0, -1, 0, 2)
    for h in (0, 1):
        send(h, 0, 0, 0, 1, 2)
        send(h, 0, 0, 0, -1, 2)
    for h in (0, 1):
        arrive(h, -1, 0, 2)
        send(h, -1, 0, 1, 0, 0)
        arrive(h, 1, 0, 2)
        send(h, 1, 0, -1, 0, 1)
    for h in (0, 1):
        for i in (-1, 1):
            send(h, i, 0, 0, 1, 2)
            send(h, i, 0, 0, -1, 2)
    for h in (0, 1):
        arrive(h, 0, -1, 2)
        send(h, 0, -1, 0, 1, 0)
        arrive(h, 0, 1, 2)
        send(h, 0, 1, 0, -1, 1)
    for h in (0, 1):
        arrive(h, -2, 0, 0)
        arrive(h, 2, 0, 1)
        send(h, 2, 0, 0, 1, 2)
        send(h, 2, 0, 0, -1, 2)
    for i in (-1, 1, 2):
        for h in (0, 1):
            arrive(h, i, -1, 2)
            send(h, i, -1, 0, 1, 0)
            arrive(h, i, 1, 2)
            send(h, i, 1, 0, -1, 1)
    for key in list(pending):
        arrive(*key)
    for c in sends:
        c.wait_send()
    local.wait()


def gather_call(own):
    return pl.pallas_call(
        gather_kernel,
        out_shape=jax.ShapeDtypeStruct((16, SLOTS, WIDE), bf16),
        in_specs=[VMEM_SPEC],
        out_specs=VMEM_SPEC,
        scratch_shapes=[pltpu.SemaphoreType.DMA, pltpu.SemaphoreType.DMA((40,)), pltpu.SemaphoreType.DMA((40,))],
        compiler_params=pltpu.CompilerParams(collective_id=0, has_side_effects=True),
        name="gather",
    )(own)


SLICE_ROWS = 656
STEP = 512


def norm_kernel(bank_ref, out_ref):
    ones = jnp.ones((128, STEP), bf16)
    total = jnp.zeros((ROWS, 128), f32)
    for k in range(F // STEP):
        wide = bank_ref[:, k * STEP : (k + 1) * STEP].astype(f32)
        total += lax.dot_general((wide * wide).astype(bf16), ones, NT, preferred_element_type=f32)
    out_ref[...] = 1.0 / (F * jnp.sqrt(total * (1.0 / F) + EPSILON))


def norm_call(bank_rows):
    return pl.pallas_call(
        norm_kernel,
        out_shape=jax.ShapeDtypeStruct((ROWS, 128), f32),
        in_specs=[VMEM_SPEC],
        out_specs=VMEM_SPEC,
        compiler_params=pltpu.CompilerParams(vmem_limit_bytes=LIMIT),
        cost_estimate=pl.CostEstimate(flops=3 * 10**8, bytes_accessed=3 * 10**6, transcendentals=0),
        name="norms",
    )(bank_rows)


def score_kernel(row_start, feat_ref, bank_ref, norm_ref, out_ref, scores, squares, weights):
    scores[...] = jnp.zeros_like(scores)
    squares[...] = jnp.zeros_like(squares)
    ones = jnp.ones((8, STEP), bf16)

    def step(k, carry):
        cols = pl.ds(pl.multiple_of(k * STEP, STEP), STEP)
        feat = feat_ref[:, cols]
        scores[...] += lax.dot_general(bank_ref[:, cols], feat, NT, preferred_element_type=f32)
        wide = feat.astype(f32)
        squares[...] += lax.dot_general(ones, (wide * wide).astype(bf16), NT, preferred_element_type=f32)
        return carry

    lax.fori_loop(0, F // STEP, step, 0)
    box = 1.0 / jnp.sqrt(squares[0:1, :] * (1.0 / F) + EPSILON)
    row = lax.broadcasted_iota(jnp.int32, (ROWS, R), 0)
    orient = lax.broadcasted_iota(jnp.int32, (ROWS, R), 1)
    select = (orient == row_start[0] + (row & 15)).astype(bf16)
    times = lax.dot_general(select, feat_ref[:, F:], NT, preferred_element_type=f32)
    correl = scores[...] * norm_ref[:, 0:1] * box
    weights[...] = (times * jnp.maximum(correl, 0.0)).astype(bf16)

    def sums(n, carry):
        h, j = n // 8, n % 8
        mine = weights[pl.ds(pl.multiple_of(h * 160, 32), 160), :]
        out = jnp.dot(
            mine, feat_ref[:, pl.ds(pl.multiple_of(j * STEP, STEP), STEP)], preferred_element_type=f32
        )
        for c in range(4):
            out_ref[h, j, c * 160 : (c + 1) * 160, :] = out[:, c * 128 : (c + 1) * 128].astype(bf16)
        total = lax.dot_general(
            jnp.ones((16, R), bf16),
            jnp.concatenate([mine, jnp.zeros((96, R), bf16)], axis=0),
            NT,
            preferred_element_type=f32,
        )
        upper = lax.broadcasted_iota(jnp.int32, (16, 128), 0) < 8
        out_ref[h, j, 640:656, :] = jnp.where(upper, total[:, :128], total[:, 128:]).astype(bf16)
        return carry

    lax.fori_loop(0, 16, sums, 0)


def score_call(row_start, gathered, bank_rows, norms):
    return pl.pallas_call(
        score_kernel,
        out_shape=jax.ShapeDtypeStruct((2, 8, SLICE_ROWS, 128), bf16),
        in_specs=[SMEM_SPEC] + [VMEM_SPEC] * 3,
        out_specs=VMEM_SPEC,
        scratch_shapes=[pltpu.VMEM((ROWS, R), f32), pltpu.VMEM((8, R), f32), pltpu.VMEM((ROWS, R), bf16)],
        compiler_params=pltpu.CompilerParams(vmem_limit_bytes=LIMIT),
        cost_estimate=pl.CostEstimate(flops=14 * 10**8, bytes_accessed=8 * 10**6, transcendentals=0),
        name="score",
    )(row_start, gathered, bank_rows, norms)


TOP = 320
ORDER = (4, 3, -3, 2, -2, 1, -1, 0)


def reduce_kernel(part_ref, out_ref, twin, from_low, from_high, to_high, to_low, total, *sems):
    twin_send, twin_recv, ring_send, ring_recv, out_send, out_recv, back_send, back_recv, own_sem = sems
    tile = lax.axis_index("tile")
    z, core = tile // 2, tile % 2
    sibling = z * 2 + 1 - core
    high = ((z + 1) % 8) * 2 + core
    low = ((z + 7) % 8) * 2 + core
    other = 1 - core

    barrier = pltpu.get_barrier_semaphore()
    for peer in (sibling, high, low):
        pl.semaphore_signal(barrier, inc=1, device_id={"tile": peer}, device_id_type=MESH)
    pl.semaphore_wait(barrier, 3)

    def remote(src, dst, send, recv, peer):
        return pltpu.make_async_remote_copy(
            src_ref=src, dst_ref=dst, send_sem=send, recv_sem=recv, device_id={"tile": peer}, device_id_type=MESH
        )

    def slot(offset):
        return (z + offset + 8) % 8

    sends = []
    twins = {}
    for m, offset in enumerate(ORDER):
        c = remote(part_ref.at[other, slot(offset)], twin.at[m], twin_send.at[m], twin_recv.at[m], sibling)
        c.start()
        sends.append(c)
        twins[offset] = c

    def pair(offset, rows):
        return part_ref[core, slot(offset), rows, :].astype(f32) + twin[ORDER.index(offset), rows, :].astype(f32)

    upper, lower, whole = pl.ds(0, TOP), pl.ds(TOP, SLICE_ROWS - TOP), pl.ds(0, SLICE_ROWS)
    ring = {}

    def pass_on(step, direction, rows):
        stage, landing, peer, n = (
            (to_high, from_low, high, step) if direction > 0 else (to_low, from_high, low, 4 + step)
        )
        c = remote(stage.at[step, rows], landing.at[step, rows], ring_send.at[n], ring_recv.at[n], peer)
        c.start()
        sends.append(c)
        ring[(step, direction)] = c

    twins[4].wait_recv()
    to_high[0, upper, :] = pair(4, upper).astype(bf16)
    pass_on(0, 1, upper)
    to_low[0, lower, :] = pair(4, lower).astype(bf16)
    pass_on(0, -1, lower)
    for step in (1, 2, 3):
        for direction in (1, -1):
            offset = direction * (4 - step)
            stage, landing = (to_high, from_low) if direction > 0 else (to_low, from_high)
            twins[offset].wait_recv()
            ring[(step - 1, direction)].wait_recv()
            for rows in (upper, lower):
                value = pair(offset, rows)
                if step > 1 or (rows is upper) == (direction > 0):
                    value = value + landing[step - 1, rows, :].astype(f32)
                stage[step, rows, :] = value.astype(bf16)
            pass_on(step, direction, whole)
    twins[0].wait_recv()
    ring[(3, 1)].wait_recv()
    ring[(3, -1)].wait_recv()
    for rows in (upper, lower):
        value = pair(0, rows) + from_low[3, rows, :].astype(f32) + from_high[3, rows, :].astype(f32)
        total[rows, :] = value.astype(bf16)

    keep = pltpu.make_async_copy(total, out_ref.at[core, z], own_sem)
    keep.start()
    outs = {}
    backs = []

    def spread(offset, direction, rows, source, n):
        peer = high if direction > 0 else low
        block = slot(offset)
        c = remote(source, out_ref.at[core, block, rows], out_send.at[n], out_recv.at[n], peer)
        c.start()
        sends.append(c)
        outs[(offset - direction, n)] = c

    def hand_over(offset, source):
        m = ORDER.index(offset)
        c = remote(source, out_ref.at[core, slot(offset)], back_send.at[m], back_recv.at[m], sibling)
        c.start()
        sends.append(c)
        backs.append(c)

    spread(0, 1, whole, total, 0)
    spread(0, -1, whole, total, 4)
    hand_over(0, total)
    for hop in (1, 2, 3):
        for direction in (1, -1):
            n = hop - 1 if direction > 0 else 3 + hop
            offset = -hop * direction
            outs[(offset, n)].wait_recv()
            rows = whole if hop < 3 else (upper if direction > 0 else lower)
            spread(offset, direction, rows, out_ref.at[core, slot(offset), rows], n + 1)
            hand_over(offset, out_ref.at[core, slot(offset)])
    outs[(-4, 3)].wait_recv()
    outs[(4, 7)].wait_recv()
    hand_over(4, out_ref.at[core, slot(4)])
    for c in backs:
        c.wait_recv()
    for c in sends:
        c.wait_send()
    keep.wait()


def reduce_call(partial):
    dma = pltpu.SemaphoreType.DMA
    buffer = pltpu.VMEM((4, SLICE_ROWS, 128), bf16)
    return pl.pallas_call(
        reduce_kernel,
        out_shape=jax.ShapeDtypeStruct((2, 8, SLICE_ROWS, 128), bf16),
        in_specs=[VMEM_SPEC],
        out_specs=VMEM_SPEC,
        scratch_shapes=[pltpu.VMEM((8, SLICE_ROWS, 128), bf16)]
        + [buffer] * 4
        + [pltpu.VMEM((SLICE_ROWS, 128), bf16)]
        + [dma((8,))] * 8
        + [dma],
        compiler_params=pltpu.CompilerParams(collective_id=1, has_side_effects=True, vmem_limit_bytes=LIMIT),
        name="reduce",
    )(partial)


def widen_kernel(in_ref, out_ref):
    for c in range(4):
        out_ref[:, c * 128 : (c + 1) * 128] = in_ref[0, 0, c * 160 : (c + 1) * 160, :].astype(f32)


def widen_call(total):
    return pl.pallas_call(
        widen_kernel,
        out_shape=jax.ShapeDtypeStruct((ROWS, F), f32),
        grid=(2, 8),
        in_specs=[pl.BlockSpec((1, 1, SLICE_ROWS, 128), lambda h, j: (h, j, 0, 0))],
        out_specs=pl.BlockSpec((160, STEP), lambda h, j: (h, j)),
        compiler_params=pltpu.CompilerParams(vmem_limit_bytes=32 * 1024 * 1024),
        name="widen",
    )(total)


def neighbours(value, axis):
    count = lax.axis_size(axis)
    forward = [(i, i + 1) for i in range(count - 1)]
    backward = [(i + 1, i) for i in range(count - 1)]
    return forward, backward


def feature_stage(volume, pick_list, box_counts):
    forward, backward = neighbours(volume, "tile")
    low = lax.ppermute(volume[CX - HALF :], "tile", forward)
    high = lax.ppermute(volume[:HALF], "tile", backward)
    picks = jnp.concatenate(
        [pick_list[:, 0, 0], jnp.broadcast_to(box_counts[0, 0], (1, SLOTS)).astype(jnp.int32)], axis=0
    )
    forward, backward = neighbours(volume, "bank")
    before = lax.ppermute(picks, "bank", forward)
    after = lax.ppermute(picks, "bank", backward)
    every = jnp.concatenate([picks, before, after], axis=1)
    slot = jnp.arange(3 * SLOTS) % SLOTS
    shift_x = every[0] - lax.axis_index("tile") * CX
    shift_y = every[1] - HALF - lax.axis_index("bank") * CX
    active = (slot < every[3]) & (shift_y > -B) & (shift_y < CX)
    meta = jnp.stack([shift_x & 255, shift_y & 255, every[2], active.astype(jnp.int32)])
    partial = features_call(meta, base_table(), low, volume, high)
    from_before = lax.ppermute(partial[2], "bank", forward)
    from_after = lax.ppermute(partial[1], "bank", backward)
    total = partial[0].astype(f32) + from_before.astype(f32) + from_after.astype(f32)
    return total.astype(bf16)


def body(volume, pick_list, box_counts, orientations, orient_weight, reference_bank):
    bank_rows = jnp.transpose(reference_bank, (1, 0, 2)).reshape(ROWS, F)
    norms = norm_call(bank_rows)
    features = feature_stage(volume, pick_list, box_counts)
    live = jnp.arange(SLOTS) < box_counts[0, 0]
    matches = orientations[0, 0][:, :, None] == jnp.arange(R)[None, None, :]
    multiplicity = jnp.sum(jnp.where(matches, orient_weight[0, 0][:, :, None].astype(f32), 0.0), axis=1)
    multiplicity = jnp.where(live[:, None], multiplicity, 0.0).astype(bf16)
    gathered = gather_call(jnp.concatenate([features, multiplicity], axis=1))
    row_start = (lax.axis_index("bank") * 16).astype(jnp.int32).reshape(1)
    partial = score_call(row_start, gathered.reshape(R, WIDE), bank_rows, norms)
    total = reduce_call(partial)
    sums = widen_call(total).reshape(C, 16, F)
    ends = jnp.concatenate([total[:, 0, 640, :], total[:, 0, 648, :32]], axis=1)
    counts = ends.astype(f32).reshape(C, 16)
    return jnp.transpose(sums, (1, 0, 2)), counts.T


def solution(mesh):
    in_specs = (
        P("tile", "bank", None),
        P(None, "tile", "bank", None),
        P("tile", "bank"),
        P("tile", "bank", None, None),
        P("tile", "bank", None, None),
        P("bank", None, None),
    )
    out_specs = (P("bank", None, None), P("bank", None))
    return jax.shard_map(body, mesh=mesh, in_specs=in_specs, out_specs=out_specs, check_vma=False)
```

```python
import functools

import jax
import jax.numpy as jnp
import numpy as np
from jax import lax
from jax.experimental import pallas as pl
from jax.experimental.pallas import tpu as pltpu
from jax.sharding import PartitionSpec as P

B = 96
L = 16
R = 256
F = 4096
C = 20
CX = 64
Z = 128
HALF = 48
EX = CX + 2 * HALF
SLOTS = 16
ROWS = 320
WIDE = F + R
EPSILON = 1e-06
PARTS = 3 * SLOTS
GROUP = 4
X_UNROLL = 4
XS = 161
YS = 65
MESH = pl.DeviceIdType.MESH
NT = (((1,), (1,)), ((), ()))
bf16 = jnp.bfloat16
f32 = jnp.float32
VMEM_SPEC = pl.BlockSpec(memory_space=pltpu.VMEM)
SMEM_SPEC = pl.BlockSpec(memory_space=pltpu.SMEM)
ANY_SPEC = pl.BlockSpec(memory_space=pl.ANY)
MIB = 1024 * 1024


def base_table():
    n = np.arange(B).astype(np.float32)
    terms = np.arange(L)
    freq = np.where(terms <= L // 2, terms, terms - L // 2).astype(np.float32)
    angles = np.float32(2.0 * np.pi) * freq[:, None] * n[None, :] / np.float32(B)
    table = np.where((terms <= L // 2)[:, None], np.cos(angles), np.sin(angles)) / np.sqrt(np.float32(B))
    wide = np.zeros((L, 256), np.float32)
    wide[:, :B] = table
    return jnp.asarray(wide).astype(bf16).astype(f32)


def features_kernel(meta, table_ref, lo_ref, own_ref, hi_ref, out_ref, spread, planes, tables, mixed, rows, order):
    base = table_ref[...]

    def scatter(ref, first, count):
        def step(i, carry):
            spread[pl.ds(first + i, CX, stride=XS), :] = ref[i].astype(f32)
            return carry

        lax.fori_loop(0, count, step, 0, unroll=8)

    scatter(lo_ref, 0, HALF)
    scatter(own_ref, HALF, CX)
    scatter(hi_ref, HALF + CX, HALF)

    def pack(y, carry):
        planes[y] = spread[pl.ds(y * XS, EX), :].astype(bf16)
        return carry

    lax.fori_loop(0, CX, pack, 0, unroll=4)

    lane = lax.broadcasted_iota(jnp.int32, (L, 256), 1)
    inside = (lane >= meta[4, 0]) & (lane < meta[4, 1])

    def x_table(s, carry):
        shifted = jnp.where(inside, pltpu.roll(base, meta[0, s], axis=1), 0.0)
        tables[pl.ds(pl.multiple_of(s * L, L), L), :] = shifted.astype(bf16)
        return carry

    lax.fori_loop(0, PARTS, x_table, 0, unroll=4)

    def x_step(y2, carry):
        y = y2 * 2
        rhs = jnp.concatenate([planes[y], planes[y + 1]], axis=1)
        for k in range(3):
            out = jnp.dot(tables[k * 256 : (k + 1) * 256, :EX], rhs, preferred_element_type=f32)
            mixed[pl.ds(k * 256 * YS + y, 256, stride=YS), :] = out[:, :Z]
            mixed[pl.ds(k * 256 * YS + y + 1, 256, stride=YS), :] = out[:, Z:]
        return carry

    lax.fori_loop(0, CX // 2, x_step, 0, unroll=X_UNROLL)

    order[0] = 0
    count = jnp.int32(0)
    for s in range(PARTS):
        order[count] = s
        count = count + meta[3, s]
    for g in range(GROUP):
        order[count + g] = order[0]
    rows[...] = jnp.zeros_like(rows)

    pick_b = (lane // L == lax.broadcasted_iota(jnp.int32, (L, 256), 0)).astype(f32)
    collapse = pick_b.astype(bf16)

    def boxes(i, carry):
        for g in range(GROUP):
            part = order[i * GROUP + g]
            shift = meta[1, part]
            blocks = []
            for j in range(4):
                moved = pltpu.roll(base, (shift + CX * j) & 255, axis=1)
                blocks.append(jnp.where(lane // CX == j, moved, 0.0))
            y_table = jnp.concatenate(blocks, axis=0).astype(bf16)
            z_table = pltpu.roll(base, meta[2, part], axis=1)[:, :Z].astype(bf16)
            z_wide = jnp.concatenate([z_table] * L, axis=0)
            start = part * (L * YS)
            pieces = []
            for q in range(4):
                rhs = jnp.concatenate(
                    [mixed[pl.ds(start + (q * 4 + a) * YS, CX), :].astype(bf16) for a in range(4)], axis=0
                )
                pieces.append(jnp.dot(y_table, rhs, preferred_element_type=f32).astype(bf16))
            second = jnp.concatenate(pieces, axis=0)
            third = lax.dot_general(second, z_wide, NT, preferred_element_type=f32)
            kept = (third.reshape(L, L, 256) * pick_b[None]).reshape(256, 256).astype(bf16)
            feature = jnp.dot(collapse, kept, preferred_element_type=f32)
            at = (part // SLOTS) * 256 + part % SLOTS
            rows[0, pl.ds(at, L, stride=L), :] = feature[:, :128]
            rows[1, pl.ds(at, L, stride=L), :] = feature[:, 128:]
        return carry

    lax.fori_loop(0, (count + GROUP - 1) // GROUP, boxes, 0)
    for k in range(3):
        for a in range(2 * L):
            first = k * 256 + a // 2 * L
            out_ref[k, :, a * 128 : (a + 1) * 128] = rows[a % 2, first : first + L, :].astype(bf16)


def features_call(meta, table, lo, own, hi):
    return pl.pallas_call(
        features_kernel,
        out_shape=jax.ShapeDtypeStruct((3, SLOTS, F), bf16),
        in_specs=[SMEM_SPEC] + [VMEM_SPEC] * 4,
        out_specs=VMEM_SPEC,
        scratch_shapes=[
            pltpu.VMEM((CX * XS, Z), f32),
            pltpu.VMEM((CX, EX, Z), bf16),
            pltpu.VMEM((PARTS * L, 256), bf16),
            pltpu.VMEM((PARTS * L * YS, Z), f32),
            pltpu.VMEM((2, PARTS * L, 128), f32),
            pltpu.SMEM((PARTS + GROUP,), jnp.int32),
        ],
        compiler_params=pltpu.CompilerParams(vmem_limit_bytes=44 * MIB),
        cost_estimate=pl.CostEstimate(flops=4 * 10**9, bytes_accessed=3 * 10**6, transcendentals=0),
        name="features",
    )(meta, table, lo, own, hi)


STEP = 512


def halo_kernel(volume, picks, bank_hbm, lo, hi, before, after, norms, bank_rows, bank_sem, send_sem, recv_sem):
    tile, bank = lax.axis_index("tile"), lax.axis_index("bank")
    up, down = {"tile": (tile + 1) % 16}, {"tile": (tile + 15) % 16}
    right, left = {"bank": (bank + 1) % 16}, {"bank": (bank + 15) % 16}
    load = pltpu.make_async_copy(bank_hbm, bank_rows, bank_sem)
    load.start()
    barrier = pltpu.get_barrier_semaphore()
    for peer in (up, down, right, left):
        pl.semaphore_signal(barrier, inc=1, device_id=peer, device_id_type=MESH)
    pl.semaphore_wait(barrier, 4)
    copies = []
    for n, (source, target, peer) in enumerate(
        (
            (volume.at[pl.ds(CX - HALF, HALF)], lo, up),
            (volume.at[pl.ds(0, HALF)], hi, down),
            (picks, before, right),
            (picks, after, left),
        )
    ):
        c = pltpu.make_async_remote_copy(
            src_ref=source,
            dst_ref=target,
            send_sem=send_sem.at[n],
            recv_sem=recv_sem.at[n],
            device_id=peer,
            device_id_type=MESH,
        )
        c.start()
        copies.append(c)
    load.wait()
    ones = jnp.ones((128, STEP), bf16)
    total = jnp.zeros((ROWS, 128), f32)
    for k in range(F // STEP):
        wide = bank_rows[:, k * STEP : (k + 1) * STEP].astype(f32)
        total += lax.dot_general((wide * wide).astype(bf16), ones, NT, preferred_element_type=f32)
    norms[...] = 1.0 / (F * jnp.sqrt(total * (1.0 / F) + EPSILON))
    for c in copies:
        c.wait()


def halo_call(volume, picks, bank_rows):
    return pl.pallas_call(
        halo_kernel,
        out_shape=(
            jax.ShapeDtypeStruct((HALF, CX, Z), bf16),
            jax.ShapeDtypeStruct((HALF, CX, Z), bf16),
            jax.ShapeDtypeStruct((8, 128), jnp.int32),
            jax.ShapeDtypeStruct((8, 128), jnp.int32),
            jax.ShapeDtypeStruct((ROWS, 128), f32),
        ),
        in_specs=[ANY_SPEC, VMEM_SPEC, ANY_SPEC],
        out_specs=(VMEM_SPEC,) * 5,
        scratch_shapes=[
            pltpu.VMEM((ROWS, F), bf16),
            pltpu.SemaphoreType.DMA,
            pltpu.SemaphoreType.DMA((4,)),
            pltpu.SemaphoreType.DMA((4,)),
        ],
        compiler_params=pltpu.CompilerParams(collective_id=2, has_side_effects=True, vmem_limit_bytes=16 * MIB),
        name="halo",
    )(volume, picks, bank_rows)


QUARTER = 1024
HALF_LANES = WIDE // 2


def gather_kernel(part_ref, times_ref, out_ref, low, high, pair_send, pair_recv, send_sem, recv_sem):
    bank = lax.axis_index("bank")
    y, x = bank // 4, bank % 4

    def at(axis, i, j):
        dx, dy = (i, j) if axis == 0 else (j, i)
        return ((y + dy + 4) % 4) * 4 + (x + dx + 4) % 4

    right, left = (bank + 1) % 16, (bank + 15) % 16
    barrier = pltpu.get_barrier_semaphore()
    for peer in (right, left, at(0, 1, 0), at(0, -1, 0), at(1, 1, 0), at(1, -1, 0)):
        pl.semaphore_signal(barrier, inc=1, device_id={"bank": peer}, device_id_type=MESH)
    pl.semaphore_wait(barrier, 6)

    sends = []
    pairs = []
    pieces = (pl.ds(0, HALF_LANES), pl.ds(HALF_LANES, F - HALF_LANES))
    for h, cols in enumerate(pieces):
        for n, (source, target, peer) in enumerate(((2, low, right), (1, high, left))):
            c = pltpu.make_async_remote_copy(
                src_ref=part_ref.at[source, :, cols],
                dst_ref=target.at[:, cols],
                send_sem=pair_send.at[2 * h + n],
                recv_sem=pair_recv.at[2 * h + n],
                device_id={"bank": peer},
                device_id_type=MESH,
            )
            c.start()
            sends.append(c)
            pairs.append(c)
    out_ref[bank, :, F:] = times_ref[...]
    slots = {}

    def lanes(h, q):
        start = h * HALF_LANES
        if q == 0:
            return pl.ds(start, QUARTER)
        if q == 1:
            return pl.ds(start + QUARTER, HALF_LANES - QUARTER)
        return pl.ds(start, HALF_LANES)

    pending = {}

    def send(h, i, j, di, dj, q):
        block = at(h, i, j)
        key = (h, i - di, j - dj, q)
        slot = slots.setdefault(key, len(slots))
        c = pltpu.make_async_remote_copy(
            src_ref=out_ref.at[block, :, lanes(h, q)],
            dst_ref=out_ref.at[block, :, lanes(h, q)],
            send_sem=send_sem.at[slot],
            recv_sem=recv_sem.at[slot],
            device_id={"bank": at(h, di, dj)},
            device_id_type=MESH,
        )
        c.start()
        sends.append(c)
        pending[key] = c

    def arrive(h, i, j, q):
        pending.pop((h, i, j, q)).wait_recv()

    for h, cols in enumerate(pieces):
        pairs[2 * h].wait_recv()
        pairs[2 * h + 1].wait_recv()
        total = part_ref[0, :, cols].astype(f32) + low[:, cols].astype(f32) + high[:, cols].astype(f32)
        out_ref[bank, :, cols] = total.astype(bf16)
        send(h, 0, 0, 1, 0, 2)
        send(h, 0, 0, -1, 0, 2)
    for h in (0, 1):
        send(h, 0, 0, 0, 1, 2)
        send(h, 0, 0, 0, -1, 2)
    for h in (0, 1):
        arrive(h, -1, 0, 2)
        send(h, -1, 0, 1, 0, 0)
        arrive(h, 1, 0, 2)
        send(h, 1, 0, -1, 0, 1)
    for h in (0, 1):
        for i in (-1, 1):
            send(h, i, 0, 0, 1, 2)
            send(h, i, 0, 0, -1, 2)
    for h in (0, 1):
        arrive(h, 0, -1, 2)
        send(h, 0, -1, 0, 1, 0)
        arrive(h, 0, 1, 2)
        send(h, 0, 1, 0, -1, 1)
    for h in (0, 1):
        arrive(h, -2, 0, 0)
        arrive(h, 2, 0, 1)
        send(h, 2, 0, 0, 1, 2)
        send(h, 2, 0, 0, -1, 2)
    for i in (-1, 1, 2):
        for h in (0, 1):
            arrive(h, i, -1, 2)
            send(h, i, -1, 0, 1, 0)
            arrive(h, i, 1, 2)
            send(h, i, 1, 0, -1, 1)
    for key in list(pending):
        arrive(*key)
    for c in sends:
        c.wait_send()


def gather_call(partial, times):
    dma = pltpu.SemaphoreType.DMA
    return pl.pallas_call(
        gather_kernel,
        out_shape=jax.ShapeDtypeStruct((16, SLOTS, WIDE), bf16),
        in_specs=[VMEM_SPEC] * 2,
        out_specs=VMEM_SPEC,
        scratch_shapes=[pltpu.VMEM((SLOTS, F), bf16)] * 2 + [dma((4,))] * 2 + [dma((40,))] * 2,
        compiler_params=pltpu.CompilerParams(collective_id=0, has_side_effects=True, vmem_limit_bytes=16 * MIB),
        name="gather",
    )(partial, times)


SLICE_ROWS = 656
PIECES = ((0, 160), (160, 160), (320, 160), (480, 176))
ORDER = (4, 3, -3, 2, -2, 1, -1, 0)


def reduce_kernel(feat_ref, bank_ref, norm_ref, out_ref, weights, mine, theirs, twin, from_low, from_high, to_high, to_low, *sems):
    twin_send, twin_recv, ring_send, ring_recv, out_send, out_recv, back_send, back_recv = sems
    bank, tile = lax.axis_index("bank"), lax.axis_index("tile")
    z, core = tile // 2, tile % 2
    sibling = z * 2 + 1 - core
    high = ((z + 1) % 8) * 2 + core
    low = ((z + 7) % 8) * 2 + core
    other = 1 - core

    barrier = pltpu.get_barrier_semaphore()
    for peer in (sibling, high, low):
        pl.semaphore_signal(barrier, inc=1, device_id={"tile": peer}, device_id_type=MESH)

    scores = jnp.zeros((ROWS, R), f32)
    squares = jnp.zeros((8, R), f32)
    ones = jnp.ones((8, STEP), bf16)
    for k in range(F // STEP):
        cols = pl.ds(k * STEP, STEP)
        feat = feat_ref[:, cols]
        scores += lax.dot_general(bank_ref[:, cols], feat, NT, preferred_element_type=f32)
        wide = feat.astype(f32)
        squares += lax.dot_general(ones, (wide * wide).astype(bf16), NT, preferred_element_type=f32)
    box = 1.0 / jnp.sqrt(squares[0:1, :] * (1.0 / F) + EPSILON)
    row = lax.broadcasted_iota(jnp.int32, (ROWS, R), 0)
    orient = lax.broadcasted_iota(jnp.int32, (ROWS, R), 1)
    select = (orient == bank * 16 + (row & 15)).astype(bf16)
    times = lax.dot_general(select, feat_ref[:, F:], NT, preferred_element_type=f32)
    correl = scores * norm_ref[:, 0:1] * box
    weights[...] = (times * jnp.maximum(correl, 0.0)).astype(bf16)
    pl.semaphore_wait(barrier, 3)

    def remote(src, dst, send, recv, peer):
        return pltpu.make_async_remote_copy(
            src_ref=src, dst_ref=dst, send_sem=send, recv_sem=recv, device_id={"tile": peer}, device_id_type=MESH
        )

    def slot(offset):
        return (z + offset + 8) % 8

    def class_sums(h, offset, target):
        rows = weights[pl.ds(pl.multiple_of(h * 160, 32), 160), :]
        cols = pl.ds(pl.multiple_of(slot(offset) * STEP, STEP), STEP)
        out = jnp.dot(rows, feat_ref[:, cols], preferred_element_type=f32)
        for c in range(4):
            target[c * 160 : (c + 1) * 160, :] = out[:, c * 128 : (c + 1) * 128].astype(bf16)

    def weight_sums(h):
        rows = weights[pl.ds(pl.multiple_of(h * 160, 32), 160), :]
        total = lax.dot_general(
            jnp.ones((16, R), bf16),
            jnp.concatenate([rows, jnp.zeros((96, R), bf16)], axis=0),
            NT,
            preferred_element_type=f32,
        )
        upper = lax.broadcasted_iota(jnp.int32, (16, 128), 0) < 8
        return jnp.where(upper, total[:, :128], total[:, 128:]).astype(bf16)

    sends = []
    twins = {}
    ends = weight_sums(other)
    for m, offset in enumerate(ORDER):
        class_sums(other, offset, theirs.at[m])
        theirs[m, 640:656, :] = ends
        c = remote(theirs.at[m], twin.at[m], twin_send.at[m], twin_recv.at[m], sibling)
        c.start()
        sends.append(c)
        twins[offset] = c
    ends = weight_sums(core)
    for m, offset in enumerate(ORDER):
        class_sums(core, offset, mine.at[m])
        mine[m, 640:656, :] = ends

    def pair(offset, rows):
        m = ORDER.index(offset)
        return mine[m, rows, :].astype(f32) + twin[m, rows, :].astype(f32)

    pieces = [pl.ds(*p) for p in PIECES]
    ring = {}

    def pass_on(step, direction, p):
        stage, landing, peer = (to_high, from_low, high) if direction > 0 else (to_low, from_high, low)
        n = (step * 2 + (direction > 0)) * 4 + p
        c = remote(stage.at[step, pieces[p]], landing.at[step, pieces[p]], ring_send.at[n], ring_recv.at[n], peer)
        c.start()
        sends.append(c)
        ring[(step, direction, p)] = c

    twins[4].wait_recv()
    for p in (0, 1):
        to_high[0, pieces[p], :] = pair(4, pieces[p]).astype(bf16)
        pass_on(0, 1, p)
        to_low[0, pieces[p + 2], :] = pair(4, pieces[p + 2]).astype(bf16)
        pass_on(0, -1, p + 2)
    for step in (1, 2, 3):
        twins[4 - step].wait_recv()
        twins[step - 4].wait_recv()
        orders = {1: (2, 3, 0, 1), -1: (0, 1, 2, 3)}
        for q in range(4):
            for direction in (1, -1):
                stage, landing = (to_high, from_low) if direction > 0 else (to_low, from_high)
                p = orders[direction][q]
                value = pair(direction * (4 - step), pieces[p])
                if (step - 1, direction, p) in ring:
                    ring[(step - 1, direction, p)].wait_recv()
                    value = value + landing[step - 1, pieces[p], :].astype(f32)
                stage[step, pieces[p], :] = value.astype(bf16)
                pass_on(step, direction, p)
    twins[0].wait_recv()
    outs = {}
    backs = []

    def spread(offset, direction, p, n):
        where = out_ref.at[core, slot(offset), pieces[p]]
        c = remote(where, where, out_send.at[n * 4 + p], out_recv.at[n * 4 + p], high if direction > 0 else low)
        c.start()
        sends.append(c)
        outs[(offset - direction, direction, p)] = c

    def hand_over(offset, p):
        where = out_ref.at[core, slot(offset), pieces[p]]
        n = ORDER.index(offset) * 4 + p
        c = remote(where, where, back_send.at[n], back_recv.at[n], sibling)
        c.start()
        sends.append(c)
        backs.append(c)

    for q in range(4):
        for direction in (1, -1):
            ring[(3, direction, orders[direction][q])].wait_recv()
        if q < 2:
            continue
        for p in ((0, 2) if q == 2 else (1, 3)):
            value = pair(0, pieces[p]) + from_low[3, pieces[p], :].astype(f32) + from_high[3, pieces[p], :].astype(f32)
            out_ref[core, z, pieces[p], :] = value.astype(bf16)
            spread(0, 1, p, 0)
            spread(0, -1, p, 4)
            hand_over(0, p)
    for hop in (1, 2, 3):
        for p in (0, 2, 1, 3):
            for direction in (1, -1):
                n = hop if direction > 0 else 4 + hop
                offset = -hop * direction
                outs[(offset, direction, p)].wait_recv()
                if hop < 3 or (p < 2) == (direction > 0):
                    spread(offset, direction, p, n)
                hand_over(offset, p)
    for p in range(4):
        outs[(-4, 1, p) if p < 2 else (4, -1, p)].wait_recv()
        hand_over(4, p)
    for c in backs:
        c.wait_recv()
    for c in sends:
        c.wait_send()


def reduce_call(gathered, bank_rows, norms):
    dma = pltpu.SemaphoreType.DMA
    slices = pltpu.VMEM((8, SLICE_ROWS, 128), bf16)
    buffer = pltpu.VMEM((4, SLICE_ROWS, 128), bf16)
    return pl.pallas_call(
        reduce_kernel,
        out_shape=jax.ShapeDtypeStruct((2, 8, SLICE_ROWS, 128), bf16),
        in_specs=[VMEM_SPEC] * 3,
        out_specs=VMEM_SPEC,
        scratch_shapes=[pltpu.VMEM((ROWS, R), bf16)]
        + [slices] * 3
        + [buffer] * 4
        + [dma((8,))] * 2
        + [dma((32,))] * 6,
        compiler_params=pltpu.CompilerParams(collective_id=1, has_side_effects=True, vmem_limit_bytes=32 * MIB),
        name="reduce",
    )(gathered, bank_rows, norms)


def widen_kernel(in_ref, out_ref, wide, sem):
    copies = []
    for j in range(8):
        for h in range(2):
            rows, cols = pl.ds(h * 160, 160), pl.ds(j * STEP, STEP)
            for c in range(4):
                start = j * STEP + c * 128
                wide[rows, start : start + 128] = in_ref[h, j, c * 160 : (c + 1) * 160, :].astype(f32)
            c = pltpu.make_async_copy(wide.at[rows, cols], out_ref.at[rows, cols], sem.at[j * 2 + h])
            c.start()
            copies.append(c)
    for c in copies:
        c.wait()


def widen_call(total):
    return pl.pallas_call(
        widen_kernel,
        out_shape=jax.ShapeDtypeStruct((ROWS, F), f32),
        in_specs=[VMEM_SPEC],
        out_specs=ANY_SPEC,
        scratch_shapes=[pltpu.VMEM((ROWS, F), f32), pltpu.SemaphoreType.DMA((16,))],
        compiler_params=pltpu.CompilerParams(vmem_limit_bytes=16 * MIB),
        name="widen",
    )(total)


def body(volume, pick_list, box_counts, orientations, orient_weight, reference_bank):
    tile, bank = lax.axis_index("tile"), lax.axis_index("bank")
    bank_rows = jnp.transpose(reference_bank, (1, 0, 2)).reshape(ROWS, F)
    counts = jnp.broadcast_to(box_counts[0, 0], (1, SLOTS)).astype(jnp.int32)
    picks = jnp.pad(jnp.concatenate([pick_list[:, 0, 0], counts], axis=0), ((0, 4), (0, 128 - SLOTS)))
    low, high, before, after, norms = halo_call(volume, picks, bank_rows)
    every = jnp.concatenate([p[:4, :SLOTS] for p in (picks, before, after)], axis=1)
    slot = jnp.arange(PARTS) % SLOTS
    shift_x = every[0] - tile * CX
    shift_y = every[1] - HALF - bank * CX
    active = (slot < every[3]) & (shift_y > -B) & (shift_y < CX)
    ends = jnp.where(
        slot == 0, jnp.where(tile == 0, HALF, 0), jnp.where(tile == lax.axis_size("tile") - 1, HALF + CX, EX)
    )
    meta = jnp.stack([shift_x & 255, shift_y & 255, every[2], active.astype(jnp.int32), ends.astype(jnp.int32)])
    partial = features_call(meta, base_table(), low, volume, high)

    live = jnp.arange(SLOTS) < box_counts[0, 0]
    matches = orientations[0, 0][:, :, None] == jnp.arange(R)[None, None, :]
    multiplicity = jnp.sum(jnp.where(matches, orient_weight[0, 0][:, :, None].astype(f32), 0.0), axis=1)
    multiplicity = jnp.where(live[:, None], multiplicity, 0.0).astype(bf16)
    gathered = gather_call(partial, multiplicity)
    total = reduce_call(gathered.reshape(R, WIDE), bank_rows, norms)
    sums = widen_call(total).reshape(C, 16, F)
    ends = jnp.concatenate([total[:, 0, 640, :], total[:, 0, 648, :32]], axis=1)
    counts = ends.astype(f32).reshape(C, 16)
    return jnp.transpose(sums, (1, 0, 2)), counts.T


def solution(mesh):
    in_specs = (
        P("tile", "bank", None),
        P(None, "tile", "bank", None),
        P("tile", "bank"),
        P("tile", "bank", None, None),
        P("tile", "bank", None, None),
        P("bank", None, None),
    )
    out_specs = (P("bank", None, None), P("bank", None))
    return jax.shard_map(body, mesh=mesh, in_specs=in_specs, out_specs=out_specs, check_vma=False)
```

```python
import functools

import jax
import jax.numpy as jnp
import numpy as np
from jax import lax
from jax.experimental import pallas as pl
from jax.experimental.pallas import tpu as pltpu
from jax.sharding import PartitionSpec as P

B = 96
L = 16
R = 256
F = 4096
C = 20
CX = 64
Z = 128
HALF = 48
EX = CX + 2 * HALF
SLOTS = 16
ROWS = 320
WIDE = F + R
EPSILON = 1e-06
PARTS = 3 * SLOTS
GROUP = 4
X_UNROLL = 4
XS = 161
YS = 65
MESH = pl.DeviceIdType.MESH
NT = (((1,), (1,)), ((), ()))
bf16 = jnp.bfloat16
f32 = jnp.float32
VMEM_SPEC = pl.BlockSpec(memory_space=pltpu.VMEM)
SMEM_SPEC = pl.BlockSpec(memory_space=pltpu.SMEM)
ANY_SPEC = pl.BlockSpec(memory_space=pl.ANY)
HBM_SPEC = pl.BlockSpec(memory_space=pltpu.MemorySpace.HBM)
MIB = 1024 * 1024
FULL = 247 * MIB // 4


def base_table():
    n = np.arange(B).astype(np.float32)
    terms = np.arange(L)
    freq = np.where(terms <= L // 2, terms, terms - L // 2).astype(np.float32)
    angles = np.float32(2.0 * np.pi) * freq[:, None] * n[None, :] / np.float32(B)
    table = np.where((terms <= L // 2)[:, None], np.cos(angles), np.sin(angles)) / np.sqrt(np.float32(B))
    wide = np.zeros((L, 256), np.float32)
    wide[:, :B] = table
    return jnp.asarray(wide).astype(bf16).astype(f32)


def features_kernel(
    picks, counts, table_ref, lo_ref, own_ref, hi_ref, out_ref,
    block, spread, planes, tables, mixed, rows, order, shift_y, shift_z, load_sem,
):
    tile, bank = lax.axis_index("tile"), lax.axis_index("bank")
    base = table_ref[...]
    lane = lax.broadcasted_iota(jnp.int32, (L, 256), 1)

    loads = []
    for n, (ref, first, count) in enumerate(((own_ref, HALF, CX), (lo_ref, 0, HALF), (hi_ref, HALF + CX, HALF))):
        copy = pltpu.make_async_copy(ref, block.at[pl.ds(first, count)], load_sem.at[n])
        copy.start()
        loads.append((copy, first, count))

    begin = jnp.where(tile == 0, HALF, 0)
    end = jnp.where(tile == 15, HALF + CX, EX)
    inside = (lane >= begin) & (lane < end)

    def x_table(p, carry):
        shift = (picks[p // SLOTS, 0, 0, 0, p % SLOTS] - tile * CX) & 255
        shifted = jnp.where(inside, pltpu.roll(base, shift, axis=1), 0.0)
        tables[pl.ds(pl.multiple_of(p * L, L), L), :] = shifted.astype(bf16)
        return carry

    lax.fori_loop(0, PARTS, x_table, 0, unroll=4)

    for copy, first, count in loads:
        copy.wait()

        def scatter(i, carry):
            spread[pl.ds(i, CX, stride=XS), :] = block[i].astype(f32)
            return carry

        lax.fori_loop(first, first + count, scatter, 0, unroll=8)

    def pack(y, carry):
        planes[y] = spread[pl.ds(y * XS, EX), :].astype(bf16)
        return carry

    lax.fori_loop(0, CX, pack, 0, unroll=4)

    def note(p, count):
        k, s = p // SLOTS, p % SLOTS
        shift = picks[k, 1, 0, 0, s] - HALF - bank * CX
        order[count] = p
        shift_y[count] = shift & 255
        shift_z[count] = picks[k, 2, 0, 0, s]
        active = (s < counts[k, 0, 0]) & (shift > -B) & (shift < CX)
        return count + active.astype(jnp.int32)

    def x_step(i, count):
        for n in range(3):
            count = note(i * 3 + n, count)
        for n in range(2):
            y = i * 4 + n * 2
            rhs = jnp.concatenate([planes[y], planes[y + 1]], axis=1)
            for k in range(3):
                out = jnp.dot(tables[k * 256 : (k + 1) * 256, :EX], rhs, preferred_element_type=f32)
                mixed[pl.ds(k * 256 * YS + y, 256, stride=YS), :] = out[:, :Z]
                mixed[pl.ds(k * 256 * YS + y + 1, 256, stride=YS), :] = out[:, Z:]
        return count

    count = lax.fori_loop(0, PARTS // 3, x_step, jnp.int32(0), unroll=X_UNROLL)
    for g in range(GROUP):
        order[count + g] = order[0]
        shift_y[count + g] = shift_y[0]
        shift_z[count + g] = shift_z[0]
    rows[...] = jnp.zeros_like(rows)

    pick_b = (lane % 128 // L == lax.broadcasted_iota(jnp.int32, (L, 256), 0) % 8).astype(f32)
    out_row = lax.broadcasted_iota(jnp.int32, (2 * L, 256), 0)
    source = lax.broadcasted_iota(jnp.int32, (2 * L, 256), 1)
    collapse = ((source // L == out_row % L) & (source % L // 8 == out_row // L)).astype(bf16)

    def pair(first):
        which = (first, first + 1)
        starts = [order[n] * (L * YS) for n in which]
        y_table = jnp.concatenate(
            [
                jnp.where(lane // CX == j, pltpu.roll(base, (shift_y[n] + CX * j) & 255, axis=1), 0.0)
                for n in which
                for j in range(4)
            ],
            axis=0,
        ).astype(bf16)
        z_tables = [pltpu.roll(base, shift_z[n] + 128 * i, axis=1).astype(bf16) for i, n in enumerate(which)]
        z_wide = jnp.concatenate([z_tables[0]] * 8 + [z_tables[1]] * 8, axis=0)
        pieces = []
        for q in range(4):
            halves = [
                jnp.concatenate(
                    [mixed[pl.ds(start + (q * 4 + a) * YS, CX), :].astype(bf16) for a in range(4)], axis=0
                )
                for start in starts
            ]
            out = jnp.dot(y_table, jnp.concatenate(halves, axis=1), preferred_element_type=f32)
            pieces.append(jnp.concatenate([out[:CX, :Z], out[CX:, Z:]], axis=1).astype(bf16))
        second = jnp.concatenate(pieces, axis=0)
        third = lax.dot_general(second, z_wide, NT, preferred_element_type=f32)
        kept = (third.reshape(L, L, 256) * pick_b[None]).reshape(256, 256).astype(bf16)
        feature = jnp.dot(collapse, kept, preferred_element_type=f32)
        for i, n in enumerate(which):
            part = order[n]
            at = (part // SLOTS) * 256 + part % SLOTS
            cols = slice(i * 128, (i + 1) * 128)
            rows[0, pl.ds(at, L, stride=L), :] = feature[:L, cols]
            rows[1, pl.ds(at, L, stride=L), :] = feature[L:, cols]

    def boxes(i, carry):
        for g in range(GROUP // 2):
            pair(i * GROUP + g * 2)
        return carry

    lax.fori_loop(0, (count + GROUP - 1) // GROUP, boxes, 0)
    for k in range(3):
        for a in range(2 * L):
            first_row = k * 256 + a // 2 * L
            out_ref[k, :, a * 128 : (a + 1) * 128] = rows[a % 2, first_row : first_row + L, :].astype(bf16)


def features_call(picks, counts, table, lo, own, hi):
    return pl.pallas_call(
        features_kernel,
        out_shape=jax.ShapeDtypeStruct((3, SLOTS, F), bf16),
        in_specs=[SMEM_SPEC] * 2 + [VMEM_SPEC] + [HBM_SPEC] * 3,
        out_specs=VMEM_SPEC,
        scratch_shapes=[
            pltpu.VMEM((EX, CX, Z), bf16),
            pltpu.VMEM((CX * XS, Z), f32),
            pltpu.VMEM((CX, EX, Z), bf16),
            pltpu.VMEM((PARTS * L, 256), bf16),
            pltpu.VMEM((PARTS * L * YS, Z), f32),
            pltpu.VMEM((2, PARTS * L, 128), f32),
        ]
        + [pltpu.SMEM((PARTS + GROUP,), jnp.int32)] * 3
        + [pltpu.SemaphoreType.DMA((3,))],
        compiler_params=pltpu.CompilerParams(vmem_limit_bytes=FULL),
        cost_estimate=pl.CostEstimate(flops=4 * 10**9, bytes_accessed=3 * 10**6, transcendentals=0),
        name="features",
    )(picks, counts, table, lo, own, hi)


STEP = 512


def halo_kernel(
    volume, pick_ref, count_ref, orient, orient_weight, bank_hbm,
    lo, hi, picks, counts, times, norms, bank_rows, bank_sem, own_sem, send_sem, recv_sem,
):
    tile, bank = lax.axis_index("tile"), lax.axis_index("bank")
    up, down = {"tile": (tile + 1) % 16}, {"tile": (tile + 15) % 16}
    right, left = {"bank": (bank + 1) % 16}, {"bank": (bank + 15) % 16}
    load = pltpu.make_async_copy(bank_hbm, bank_rows, bank_sem)
    load.start()
    own = [
        pltpu.make_async_copy(pick_ref, picks.at[0], own_sem.at[0]),
        pltpu.make_async_copy(count_ref, counts.at[0], own_sem.at[1]),
    ]
    for c in own:
        c.start()
    barrier = pltpu.get_barrier_semaphore()
    for peer in (up, down, right, left):
        pl.semaphore_signal(barrier, inc=1, device_id=peer, device_id_type=MESH)
    pl.semaphore_wait(barrier, 4)
    copies = []
    for n, (source, target, peer) in enumerate(
        (
            (volume.at[pl.ds(CX - HALF, HALF)], lo, up),
            (volume.at[pl.ds(0, HALF)], hi, down),
            (pick_ref, picks.at[1], right),
            (pick_ref, picks.at[2], left),
            (count_ref, counts.at[1], right),
            (count_ref, counts.at[2], left),
        )
    ):
        c = pltpu.make_async_remote_copy(
            src_ref=source,
            dst_ref=target,
            send_sem=send_sem.at[n],
            recv_sem=recv_sem.at[n],
            device_id=peer,
            device_id_type=MESH,
        )
        c.start()
        copies.append(c)

    columns = orient[0, 0].astype(f32).T
    weight = orient_weight[0, 0].astype(f32).astype(bf16)
    choice = lax.broadcasted_iota(jnp.int32, (128, R), 1).astype(f32)
    row = lax.broadcasted_iota(jnp.int32, (SLOTS, R), 0)
    sums = jnp.zeros((SLOTS, R), f32)
    for s in range(SLOTS):
        hot = (columns[:, s : s + 1] == choice).astype(f32).astype(bf16)
        sums += jnp.where(row == s, jnp.dot(weight, hot, preferred_element_type=f32), 0.0)
    times[...] = jnp.where(row < count_ref[...], sums, 0.0).astype(bf16)

    load.wait()
    ones = jnp.ones((128, STEP), bf16)
    total = jnp.zeros((ROWS, 128), f32)
    for k in range(F // STEP):
        wide = bank_rows[:, k * STEP : (k + 1) * STEP].astype(f32)
        total += lax.dot_general((wide * wide).astype(bf16), ones, NT, preferred_element_type=f32)
    norms[...] = 1.0 / (F * jnp.sqrt(total * (1.0 / F) + EPSILON))
    for c in own + copies:
        c.wait()


def halo_call(volume, pick_list, box_counts, orientations, orient_weight, bank_rows):
    dma = pltpu.SemaphoreType.DMA
    return pl.pallas_call(
        halo_kernel,
        out_shape=(
            jax.ShapeDtypeStruct((HALF, CX, Z), bf16),
            jax.ShapeDtypeStruct((HALF, CX, Z), bf16),
            jax.ShapeDtypeStruct((3,) + pick_list.shape, jnp.int32),
            jax.ShapeDtypeStruct((3,) + box_counts.shape, jnp.int32),
            jax.ShapeDtypeStruct((SLOTS, R), bf16),
            jax.ShapeDtypeStruct((ROWS, 128), f32),
        ),
        in_specs=[HBM_SPEC] + [VMEM_SPEC] * 4 + [HBM_SPEC],
        out_specs=(HBM_SPEC,) * 2 + (VMEM_SPEC,) * 4,
        scratch_shapes=[pltpu.VMEM((ROWS, F), bf16), dma, dma((2,)), dma((6,)), dma((6,))],
        compiler_params=pltpu.CompilerParams(collective_id=2, has_side_effects=True, vmem_limit_bytes=FULL),
        name="halo",
    )(volume, pick_list, box_counts, orientations, orient_weight, bank_rows)


QUARTER = 1024
HALF_LANES = WIDE // 2


def gather_kernel(part_ref, times_ref, out_ref, low, high, pair_send, pair_recv, send_sem, recv_sem):
    bank = lax.axis_index("bank")
    y, x = bank // 4, bank % 4

    def at(axis, i, j):
        dx, dy = (i, j) if axis == 0 else (j, i)
        return ((y + dy + 4) % 4) * 4 + (x + dx + 4) % 4

    right, left = (bank + 1) % 16, (bank + 15) % 16
    barrier = pltpu.get_barrier_semaphore()
    for peer in (right, left, at(0, 1, 0), at(0, -1, 0), at(1, 1, 0), at(1, -1, 0)):
        pl.semaphore_signal(barrier, inc=1, device_id={"bank": peer}, device_id_type=MESH)
    pl.semaphore_wait(barrier, 6)

    sends = []
    pairs = []
    pieces = (pl.ds(0, HALF_LANES), pl.ds(HALF_LANES, F - HALF_LANES))
    for h, cols in enumerate(pieces):
        for n, (source, target, peer) in enumerate(((2, low, right), (1, high, left))):
            c = pltpu.make_async_remote_copy(
                src_ref=part_ref.at[source, :, cols],
                dst_ref=target.at[:, cols],
                send_sem=pair_send.at[2 * h + n],
                recv_sem=pair_recv.at[2 * h + n],
                device_id={"bank": peer},
                device_id_type=MESH,
            )
            c.start()
            sends.append(c)
            pairs.append(c)
    out_ref[bank, :, F:] = times_ref[...]
    slots = {}

    def lanes(h, q):
        start = h * HALF_LANES
        if q == 0:
            return pl.ds(start, QUARTER)
        if q == 1:
            return pl.ds(start + QUARTER, HALF_LANES - QUARTER)
        return pl.ds(start, HALF_LANES)

    pending = {}

    def send(h, i, j, di, dj, q):
        block = at(h, i, j)
        key = (h, i - di, j - dj, q)
        slot = slots.setdefault(key, len(slots))
        c = pltpu.make_async_remote_copy(
            src_ref=out_ref.at[block, :, lanes(h, q)],
            dst_ref=out_ref.at[block, :, lanes(h, q)],
            send_sem=send_sem.at[slot],
            recv_sem=recv_sem.at[slot],
            device_id={"bank": at(h, di, dj)},
            device_id_type=MESH,
        )
        c.start()
        sends.append(c)
        pending[key] = c

    def arrive(h, i, j, q):
        pending.pop((h, i, j, q)).wait_recv()

    for h, cols in enumerate(pieces):
        pairs[2 * h].wait_recv()
        pairs[2 * h + 1].wait_recv()
        total = part_ref[0, :, cols].astype(f32) + low[:, cols].astype(f32) + high[:, cols].astype(f32)
        out_ref[bank, :, cols] = total.astype(bf16)
        send(h, 0, 0, 1, 0, 2)
        send(h, 0, 0, -1, 0, 2)
    for h in (0, 1):
        send(h, 0, 0, 0, 1, 2)
        send(h, 0, 0, 0, -1, 2)
    for h in (0, 1):
        arrive(h, -1, 0, 2)
        send(h, -1, 0, 1, 0, 0)
        arrive(h, 1, 0, 2)
        send(h, 1, 0, -1, 0, 1)
    for h in (0, 1):
        for i in (-1, 1):
            send(h, i, 0, 0, 1, 2)
            send(h, i, 0, 0, -1, 2)
    for h in (0, 1):
        arrive(h, 0, -1, 2)
        send(h, 0, -1, 0, 1, 0)
        arrive(h, 0, 1, 2)
        send(h, 0, 1, 0, -1, 1)
    for h in (0, 1):
        arrive(h, -2, 0, 0)
        arrive(h, 2, 0, 1)
        send(h, 2, 0, 0, 1, 2)
        send(h, 2, 0, 0, -1, 2)
    for i in (-1, 1, 2):
        for h in (0, 1):
            arrive(h, i, -1, 2)
            send(h, i, -1, 0, 1, 0)
            arrive(h, i, 1, 2)
            send(h, i, 1, 0, -1, 1)
    for key in list(pending):
        arrive(*key)
    for c in sends:
        c.wait_send()


def gather_call(partial, times):
    dma = pltpu.SemaphoreType.DMA
    return pl.pallas_call(
        gather_kernel,
        out_shape=jax.ShapeDtypeStruct((16, SLOTS, WIDE), bf16),
        in_specs=[VMEM_SPEC] * 2,
        out_specs=VMEM_SPEC,
        scratch_shapes=[pltpu.VMEM((SLOTS, F), bf16)] * 2 + [dma((4,))] * 2 + [dma((40,))] * 2,
        compiler_params=pltpu.CompilerParams(collective_id=0, has_side_effects=True, vmem_limit_bytes=16 * MIB),
        name="gather",
    )(partial, times)


SLICE_ROWS = 656
PIECES = ((0, 160), (160, 160), (320, 160), (480, 176))
ORDER = (4, 3, -3, 2, -2, 1, -1, 0)


def reduce_kernel(feat_ref, bank_ref, norm_ref, out_ref, weights, mine, theirs, twin, from_low, from_high, to_high, to_low, *sems):
    twin_send, twin_recv, ring_send, ring_recv, out_send, out_recv, back_send, back_recv = sems
    bank, tile = lax.axis_index("bank"), lax.axis_index("tile")
    z, core = tile // 2, tile % 2
    sibling = z * 2 + 1 - core
    high = ((z + 1) % 8) * 2 + core
    low = ((z + 7) % 8) * 2 + core
    other = 1 - core

    barrier = pltpu.get_barrier_semaphore()
    for peer in (sibling, high, low):
        pl.semaphore_signal(barrier, inc=1, device_id={"tile": peer}, device_id_type=MESH)

    scores = jnp.zeros((ROWS, R), f32)
    squares = jnp.zeros((8, R), f32)
    ones = jnp.ones((8, STEP), bf16)
    for k in range(F // STEP):
        cols = pl.ds(k * STEP, STEP)
        feat = feat_ref[:, cols]
        scores += lax.dot_general(bank_ref[:, cols], feat, NT, preferred_element_type=f32)
        wide = feat.astype(f32)
        squares += lax.dot_general(ones, (wide * wide).astype(bf16), NT, preferred_element_type=f32)
    box = 1.0 / jnp.sqrt(squares[0:1, :] * (1.0 / F) + EPSILON)
    row = lax.broadcasted_iota(jnp.int32, (ROWS, R), 0)
    orient = lax.broadcasted_iota(jnp.int32, (ROWS, R), 1)
    select = (orient == bank * 16 + (row & 15)).astype(bf16)
    times = lax.dot_general(select, feat_ref[:, F:], NT, preferred_element_type=f32)
    correl = scores * norm_ref[:, 0:1] * box
    weights[...] = (times * jnp.maximum(correl, 0.0)).astype(bf16)
    pl.semaphore_wait(barrier, 3)

    def remote(src, dst, send, recv, peer):
        return pltpu.make_async_remote_copy(
            src_ref=src, dst_ref=dst, send_sem=send, recv_sem=recv, device_id={"tile": peer}, device_id_type=MESH
        )

    def slot(offset):
        return (z + offset + 8) % 8

    def class_sums(h, offset, target):
        rows = weights[pl.ds(pl.multiple_of(h * 160, 32), 160), :]
        cols = pl.ds(pl.multiple_of(slot(offset) * STEP, STEP), STEP)
        out = jnp.dot(rows, feat_ref[:, cols], preferred_element_type=f32)
        for c in range(4):
            target[c * 160 : (c + 1) * 160, :] = out[:, c * 128 : (c + 1) * 128].astype(bf16)

    def weight_sums(h):
        rows = weights[pl.ds(pl.multiple_of(h * 160, 32), 160), :]
        total = lax.dot_general(
            jnp.ones((16, R), bf16),
            jnp.concatenate([rows, jnp.zeros((96, R), bf16)], axis=0),
            NT,
            preferred_element_type=f32,
        )
        upper = lax.broadcasted_iota(jnp.int32, (16, 128), 0) < 8
        return jnp.where(upper, total[:, :128], total[:, 128:]).astype(bf16)

    sends = []
    twins = {}
    ends = weight_sums(other), weight_sums(core)

    def to_twin(offset):
        m = ORDER.index(offset)
        class_sums(other, offset, theirs.at[m])
        theirs[m, 640:656, :] = ends[0]
        c = remote(theirs.at[m], twin.at[m], twin_send.at[m], twin_recv.at[m], sibling)
        c.start()
        sends.append(c)
        twins[offset] = c

    def keep(offset):
        m = ORDER.index(offset)
        class_sums(core, offset, mine.at[m])
        mine[m, 640:656, :] = ends[1]

    to_twin(4)
    keep(4)
    for offset in (3, -3):
        to_twin(offset)
        keep(offset)

    def pair(offset, rows):
        m = ORDER.index(offset)
        return mine[m, rows, :].astype(f32) + twin[m, rows, :].astype(f32)

    pieces = [pl.ds(*p) for p in PIECES]
    ring = {}

    def pass_on(step, direction, p):
        stage, landing, peer = (to_high, from_low, high) if direction > 0 else (to_low, from_high, low)
        n = (step * 2 + (direction > 0)) * 4 + p
        c = remote(stage.at[step, pieces[p]], landing.at[step, pieces[p]], ring_send.at[n], ring_recv.at[n], peer)
        c.start()
        sends.append(c)
        ring[(step, direction, p)] = c

    twins[4].wait_recv()
    for p in (0, 1):
        to_high[0, pieces[p], :] = pair(4, pieces[p]).astype(bf16)
        pass_on(0, 1, p)
        to_low[0, pieces[p + 2], :] = pair(4, pieces[p + 2]).astype(bf16)
        pass_on(0, -1, p + 2)
    for step in (1, 2, 3):
        for offset in (3 - step, step - 3)[: 1 if step == 3 else 2]:
            to_twin(offset)
            keep(offset)
        twins[4 - step].wait_recv()
        twins[step - 4].wait_recv()
        orders = {1: (2, 3, 0, 1), -1: (0, 1, 2, 3)}
        for q in range(4):
            for direction in (1, -1):
                stage, landing = (to_high, from_low) if direction > 0 else (to_low, from_high)
                p = orders[direction][q]
                value = pair(direction * (4 - step), pieces[p])
                if (step - 1, direction, p) in ring:
                    ring[(step - 1, direction, p)].wait_recv()
                    value = value + landing[step - 1, pieces[p], :].astype(f32)
                stage[step, pieces[p], :] = value.astype(bf16)
                pass_on(step, direction, p)
    twins[0].wait_recv()
    outs = {}
    backs = []

    def spread(offset, direction, p, n):
        where = out_ref.at[core, slot(offset), pieces[p]]
        c = remote(where, where, out_send.at[n * 4 + p], out_recv.at[n * 4 + p], high if direction > 0 else low)
        c.start()
        sends.append(c)
        outs[(offset - direction, direction, p)] = c

    def hand_over(offset, p):
        where = out_ref.at[core, slot(offset), pieces[p]]
        n = ORDER.index(offset) * 4 + p
        c = remote(where, where, back_send.at[n], back_recv.at[n], sibling)
        c.start()
        sends.append(c)
        backs.append(c)

    for q in range(4):
        for direction in (1, -1):
            ring[(3, direction, orders[direction][q])].wait_recv()
        if q < 2:
            continue
        for p in ((0, 2) if q == 2 else (1, 3)):
            value = pair(0, pieces[p]) + from_low[3, pieces[p], :].astype(f32) + from_high[3, pieces[p], :].astype(f32)
            out_ref[core, z, pieces[p], :] = value.astype(bf16)
            spread(0, 1, p, 0)
            spread(0, -1, p, 4)
            hand_over(0, p)
    for hop in (1, 2, 3):
        for p in (0, 2, 1, 3):
            for direction in (1, -1):
                n = hop if direction > 0 else 4 + hop
                offset = -hop * direction
                outs[(offset, direction, p)].wait_recv()
                if hop < 3 or (p < 2) == (direction > 0):
                    spread(offset, direction, p, n)
                hand_over(offset, p)
    for p in range(4):
        outs[(-4, 1, p) if p < 2 else (4, -1, p)].wait_recv()
        hand_over(4, p)
    for c in backs:
        c.wait_recv()
    for c in sends:
        c.wait_send()


def reduce_call(gathered, bank_rows, norms):
    dma = pltpu.SemaphoreType.DMA
    slices = pltpu.VMEM((8, SLICE_ROWS, 128), bf16)
    buffer = pltpu.VMEM((4, SLICE_ROWS, 128), bf16)
    return pl.pallas_call(
        reduce_kernel,
        out_shape=jax.ShapeDtypeStruct((2, 8, SLICE_ROWS, 128), bf16),
        in_specs=[VMEM_SPEC] * 3,
        out_specs=VMEM_SPEC,
        scratch_shapes=[pltpu.VMEM((ROWS, R), bf16)]
        + [slices] * 3
        + [buffer] * 4
        + [dma((8,))] * 2
        + [dma((32,))] * 6,
        compiler_params=pltpu.CompilerParams(collective_id=1, has_side_effects=True, vmem_limit_bytes=32 * MIB),
        name="reduce",
    )(gathered, bank_rows, norms)


def widen_kernel(in_ref, out_ref, counts_ref, wide, sem):
    copies = []
    for j in range(8):
        for h in range(2):
            rows, cols = pl.ds(h * 160, 160), pl.ds(j * STEP, STEP)
            for c in range(4):
                start = j * STEP + c * 128
                wide[rows, start : start + 128] = in_ref[h, j, c * 160 : (c + 1) * 160, :].astype(f32)
            c = pltpu.make_async_copy(wide.at[rows, cols], out_ref.at[rows, cols], sem.at[j * 2 + h])
            c.start()
            copies.append(c)
    orient = lax.broadcasted_iota(jnp.int32, (16, 128), 0)
    lane = lax.broadcasted_iota(jnp.int32, (16, 128), 1)
    entry = lax.broadcasted_iota(jnp.int32, (128, 128), 0)
    group = lax.broadcasted_iota(jnp.int32, (128, 128), 1)
    counts = jnp.zeros((16, 128), f32)
    for h in range(2):
        ends = in_ref[h, 0, 640:656, :].astype(f32)
        for first, line, valid in ((0, 0, 128), (128, 8, 32)):
            mine = jnp.where((lane % 16 == orient) & (lane < valid), ends[line : line + 1, :], 0.0).astype(bf16)
            place = (h * 160 + first + entry) // 16 == group
            counts += jnp.dot(mine, place.astype(f32).astype(bf16), preferred_element_type=f32)
    counts_ref[...] = counts[:, :C]
    for c in copies:
        c.wait()


def widen_call(total):
    return pl.pallas_call(
        widen_kernel,
        out_shape=(jax.ShapeDtypeStruct((ROWS, F), f32), jax.ShapeDtypeStruct((16, C), f32)),
        in_specs=[VMEM_SPEC],
        out_specs=(ANY_SPEC, VMEM_SPEC),
        scratch_shapes=[pltpu.VMEM((ROWS, F), f32), pltpu.SemaphoreType.DMA((16,))],
        compiler_params=pltpu.CompilerParams(vmem_limit_bytes=16 * MIB),
        name="widen",
    )(total)


def body(volume, pick_list, box_counts, orientations, orient_weight, reference_bank):
    bank_rows = jnp.transpose(reference_bank, (1, 0, 2)).reshape(ROWS, F)
    low, high, picks, counts, times, norms = halo_call(
        volume, pick_list, box_counts, orientations, orient_weight, bank_rows
    )
    partial = features_call(picks, counts, base_table(), low, volume, high)
    gathered = gather_call(partial, times)
    total = reduce_call(gathered.reshape(R, WIDE), bank_rows, norms)
    sums, weight_sums = widen_call(total)
    return jnp.transpose(sums.reshape(C, 16, F), (1, 0, 2)), weight_sums


def solution(mesh):
    in_specs = (
        P("tile", "bank", None),
        P(None, "tile", "bank", None),
        P("tile", "bank"),
        P("tile", "bank", None, None),
        P("tile", "bank", None, None),
        P("bank", None, None),
    )
    out_specs = (P("bank", None, None), P("bank", None))
    return jax.shard_map(body, mesh=mesh, in_specs=in_specs, out_specs=out_specs, check_vma=False)
```

```python
import functools

import jax
import jax.numpy as jnp
import numpy as np
from jax import lax
from jax.experimental import pallas as pl
from jax.experimental.pallas import tpu as pltpu
from jax.sharding import PartitionSpec as P

B = 96
L = 16
R = 256
F = 4096
C = 20
CX = 64
Z = 128
HALF = 48
EX = CX + 2 * HALF
SLOTS = 16
ROWS = 320
WIDE = F + R
EPSILON = 1e-06
PARTS = 3 * SLOTS
GROUP = 4
X_UNROLL = 4
XS = 161
YS = 65
MESH = pl.DeviceIdType.MESH
NT = (((1,), (1,)), ((), ()))
bf16 = jnp.bfloat16
f32 = jnp.float32
VMEM_SPEC = pl.BlockSpec(memory_space=pltpu.VMEM)
SMEM_SPEC = pl.BlockSpec(memory_space=pltpu.SMEM)
ANY_SPEC = pl.BlockSpec(memory_space=pl.ANY)
HBM_SPEC = pl.BlockSpec(memory_space=pltpu.MemorySpace.HBM)
MIB = 1024 * 1024


def in_hbm(value):
    return pltpu.with_memory_space_constraint(value, memory_space=pltpu.MemorySpace.HBM)


def base_table():
    n = np.arange(B).astype(np.float32)
    terms = np.arange(L)
    freq = np.where(terms <= L // 2, terms, terms - L // 2).astype(np.float32)
    angles = np.float32(2.0 * np.pi) * freq[:, None] * n[None, :] / np.float32(B)
    table = np.where((terms <= L // 2)[:, None], np.cos(angles), np.sin(angles)) / np.sqrt(np.float32(B))
    wide = np.zeros((L, 256), np.float32)
    wide[:, :B] = table
    return jnp.asarray(wide).astype(bf16).astype(f32)


def features_kernel(
    picks, counts, table_ref, lo_ref, own_ref, hi_ref, out_ref,
    block, spread, planes, tables, mixed, rows, order, shift_y, shift_z, load_sem,
):
    tile, bank = lax.axis_index("tile"), lax.axis_index("bank")
    base = table_ref[...]
    lane = lax.broadcasted_iota(jnp.int32, (L, 256), 1)

    load = pltpu.make_async_copy(own_ref, block, load_sem)
    load.start()

    begin = jnp.where(tile == 0, HALF, 0)
    end = jnp.where(tile == 15, HALF + CX, EX)
    inside = (lane >= begin) & (lane < end)

    def x_table(p, carry):
        shift = (picks[p // SLOTS, 0, 0, 0, p % SLOTS] - tile * CX) & 255
        shifted = jnp.where(inside, pltpu.roll(base, shift, axis=1), 0.0)
        tables[pl.ds(pl.multiple_of(p * L, L), L), :] = shifted.astype(bf16)
        return carry

    lax.fori_loop(0, PARTS, x_table, 0, unroll=4)

    def scatter(ref, first, count):
        def step(i, carry):
            spread[pl.ds(first + i, CX, stride=XS), :] = ref[i].astype(f32)
            return carry

        lax.fori_loop(0, count, step, 0, unroll=8)

    scatter(lo_ref, 0, HALF)
    scatter(hi_ref, HALF + CX, HALF)
    load.wait()
    scatter(block, HALF, CX)

    def pack(y, carry):
        planes[y] = spread[pl.ds(y * XS, EX), :].astype(bf16)
        return carry

    lax.fori_loop(0, CX, pack, 0, unroll=4)

    def note(p, count):
        k, s = p // SLOTS, p % SLOTS
        shift = picks[k, 1, 0, 0, s] - HALF - bank * CX
        order[count] = p
        shift_y[count] = shift & 255
        shift_z[count] = picks[k, 2, 0, 0, s]
        active = (s < counts[k, 0, 0]) & (shift > -B) & (shift < CX)
        return count + active.astype(jnp.int32)

    def x_step(i, count):
        for n in range(3):
            count = note(i * 3 + n, count)
        for n in range(2):
            y = i * 4 + n * 2
            rhs = jnp.concatenate([planes[y], planes[y + 1]], axis=1)
            for k in range(3):
                out = jnp.dot(tables[k * 256 : (k + 1) * 256, :EX], rhs, preferred_element_type=f32)
                mixed[pl.ds(k * 256 * YS + y, 256, stride=YS), :] = out[:, :Z]
                mixed[pl.ds(k * 256 * YS + y + 1, 256, stride=YS), :] = out[:, Z:]
        return count

    count = lax.fori_loop(0, PARTS // 3, x_step, jnp.int32(0), unroll=X_UNROLL)
    for g in range(GROUP):
        order[count + g] = order[0]
        shift_y[count + g] = shift_y[0]
        shift_z[count + g] = shift_z[0]
    rows[...] = jnp.zeros_like(rows)

    pick_b = (lane % 128 // L == lax.broadcasted_iota(jnp.int32, (L, 256), 0) % 8).astype(f32)
    out_row = lax.broadcasted_iota(jnp.int32, (2 * L, 256), 0)
    source = lax.broadcasted_iota(jnp.int32, (2 * L, 256), 1)
    collapse = ((source // L == out_row % L) & (source % L // 8 == out_row // L)).astype(bf16)

    def pair(first):
        which = (first, first + 1)
        starts = [order[n] * (L * YS) for n in which]
        y_table = jnp.concatenate(
            [
                jnp.where(lane // CX == j, pltpu.roll(base, (shift_y[n] + CX * j) & 255, axis=1), 0.0)
                for n in which
                for j in range(4)
            ],
            axis=0,
        ).astype(bf16)
        z_tables = [pltpu.roll(base, shift_z[n] + 128 * i, axis=1).astype(bf16) for i, n in enumerate(which)]
        z_wide = jnp.concatenate([z_tables[0]] * 8 + [z_tables[1]] * 8, axis=0)
        pieces = []
        for q in range(4):
            halves = [
                jnp.concatenate(
                    [mixed[pl.ds(start + (q * 4 + a) * YS, CX), :].astype(bf16) for a in range(4)], axis=0
                )
                for start in starts
            ]
            out = jnp.dot(y_table, jnp.concatenate(halves, axis=1), preferred_element_type=f32)
            pieces.append(jnp.concatenate([out[:CX, :Z], out[CX:, Z:]], axis=1).astype(bf16))
        second = jnp.concatenate(pieces, axis=0)
        third = lax.dot_general(second, z_wide, NT, preferred_element_type=f32)
        kept = (third.reshape(L, L, 256) * pick_b[None]).reshape(256, 256).astype(bf16)
        feature = jnp.dot(collapse, kept, preferred_element_type=f32)
        for i, n in enumerate(which):
            part = order[n]
            at = (part // SLOTS) * 256 + part % SLOTS
            cols = slice(i * 128, (i + 1) * 128)
            rows[0, pl.ds(at, L, stride=L), :] = feature[:L, cols]
            rows[1, pl.ds(at, L, stride=L), :] = feature[L:, cols]

    def boxes(i, carry):
        for g in range(GROUP // 2):
            pair(i * GROUP + g * 2)
        return carry

    lax.fori_loop(0, (count + GROUP - 1) // GROUP, boxes, 0)
    for k in range(3):
        for a in range(2 * L):
            first_row = k * 256 + a // 2 * L
            out_ref[k, :, a * 128 : (a + 1) * 128] = rows[a % 2, first_row : first_row + L, :].astype(bf16)


def features_call(picks, counts, table, lo, own, hi):
    return pl.pallas_call(
        features_kernel,
        out_shape=jax.ShapeDtypeStruct((3, SLOTS, F), bf16),
        in_specs=[SMEM_SPEC] * 2 + [VMEM_SPEC] * 2 + [HBM_SPEC, VMEM_SPEC],
        out_specs=VMEM_SPEC,
        scratch_shapes=[
            pltpu.VMEM((CX, CX, Z), bf16),
            pltpu.VMEM((CX * XS, Z), f32),
            pltpu.VMEM((CX, EX, Z), bf16),
            pltpu.VMEM((PARTS * L, 256), bf16),
            pltpu.VMEM((PARTS * L * YS, Z), f32),
            pltpu.VMEM((2, PARTS * L, 128), f32),
        ]
        + [pltpu.SMEM((PARTS + GROUP,), jnp.int32)] * 3
        + [pltpu.SemaphoreType.DMA],
        compiler_params=pltpu.CompilerParams(vmem_limit_bytes=44 * MIB),
        cost_estimate=pl.CostEstimate(flops=4 * 10**9, bytes_accessed=3 * 10**6, transcendentals=0),
        name="features",
    )(picks, counts, table, lo, in_hbm(own), hi)


STEP = 512


def halo_kernel(
    volume, pick_ref, count, orient_hbm, orient_weight_hbm, bank_hbm,
    lo, hi, picks, counts, times, norms,
    bank_rows, orient, orient_weight, bank_sem, own_sem, send_sem, recv_sem,
):
    tile, bank = lax.axis_index("tile"), lax.axis_index("bank")
    up, down = {"tile": (tile + 1) % 16}, {"tile": (tile + 15) % 16}
    right, left = {"bank": (bank + 1) % 16}, {"bank": (bank + 15) % 16}
    barrier = pltpu.get_barrier_semaphore()
    for peer in (up, down, right, left):
        pl.semaphore_signal(barrier, inc=1, device_id=peer, device_id_type=MESH)
    own = [
        pltpu.make_async_copy(pick_ref, picks.at[0], own_sem.at[0]),
        pltpu.make_async_copy(count, counts.at[0], own_sem.at[1]),
    ]
    loads = [
        pltpu.make_async_copy(orient_hbm, orient, own_sem.at[2]),
        pltpu.make_async_copy(orient_weight_hbm, orient_weight, own_sem.at[3]),
    ]
    load = pltpu.make_async_copy(bank_hbm, bank_rows, bank_sem)
    for c in own + loads + [load]:
        c.start()
    pl.semaphore_wait(barrier, 4)
    copies = []
    for n, (source, target, peer) in enumerate(
        (
            (volume.at[pl.ds(CX - HALF, HALF)], lo, up),
            (volume.at[pl.ds(0, HALF)], hi, down),
            (pick_ref, picks.at[1], right),
            (pick_ref, picks.at[2], left),
            (count, counts.at[1], right),
            (count, counts.at[2], left),
        )
    ):
        c = pltpu.make_async_remote_copy(
            src_ref=source,
            dst_ref=target,
            send_sem=send_sem.at[n],
            recv_sem=recv_sem.at[n],
            device_id=peer,
            device_id_type=MESH,
        )
        c.start()
        copies.append(c)

    for c in loads:
        c.wait()
    columns = orient[0, 0].astype(f32).T
    weight = orient_weight[0, 0].astype(f32).astype(bf16)
    choice = lax.broadcasted_iota(jnp.int32, (128, R), 1).astype(f32)
    row = lax.broadcasted_iota(jnp.int32, (SLOTS, R), 0)
    sums = jnp.zeros((SLOTS, R), f32)
    for s in range(SLOTS):
        hot = (columns[:, s : s + 1] == choice).astype(f32).astype(bf16)
        sums += jnp.where(row == s, jnp.dot(weight, hot, preferred_element_type=f32), 0.0)
    times[...] = jnp.where(row < count[...], sums, 0.0).astype(bf16)

    load.wait()
    ones = jnp.ones((128, STEP), bf16)
    total = jnp.zeros((ROWS, 128), f32)
    for k in range(F // STEP):
        wide = bank_rows[:, k * STEP : (k + 1) * STEP].astype(f32)
        total += lax.dot_general((wide * wide).astype(bf16), ones, NT, preferred_element_type=f32)
    norms[...] = 1.0 / (F * jnp.sqrt(total * (1.0 / F) + EPSILON))
    for c in own + copies:
        c.wait()


def halo_call(volume, pick_list, box_counts, orientations, orient_weight, bank_rows):
    dma = pltpu.SemaphoreType.DMA
    return pl.pallas_call(
        halo_kernel,
        out_shape=(
            jax.ShapeDtypeStruct((HALF, CX, Z), bf16),
            jax.ShapeDtypeStruct((HALF, CX, Z), bf16),
            jax.ShapeDtypeStruct((3,) + pick_list.shape, jnp.int32),
            jax.ShapeDtypeStruct((3,) + box_counts.shape, jnp.int32),
            jax.ShapeDtypeStruct((SLOTS, R), bf16),
            jax.ShapeDtypeStruct((ROWS, 128), f32),
        ),
        in_specs=[HBM_SPEC] * 2 + [VMEM_SPEC] + [HBM_SPEC] * 3,
        out_specs=(VMEM_SPEC,) * 6,
        scratch_shapes=[
            pltpu.VMEM((ROWS, F), bf16),
            pltpu.VMEM(orientations.shape, jnp.int32),
            pltpu.VMEM(orient_weight.shape, jnp.int32),
            dma,
            dma((4,)),
            dma((6,)),
            dma((6,)),
        ],
        compiler_params=pltpu.CompilerParams(collective_id=2, has_side_effects=True, vmem_limit_bytes=16 * MIB),
        name="halo",
    )(in_hbm(volume), in_hbm(pick_list), box_counts, *map(in_hbm, (orientations, orient_weight, bank_rows)))


QUARTER = 1024
HALF_LANES = WIDE // 2


def gather_kernel(part_ref, times_ref, out_ref, low, high, pair_send, pair_recv, send_sem, recv_sem):
    bank = lax.axis_index("bank")
    y, x = bank // 4, bank % 4

    def at(axis, i, j):
        dx, dy = (i, j) if axis == 0 else (j, i)
        return ((y + dy + 4) % 4) * 4 + (x + dx + 4) % 4

    right, left = (bank + 1) % 16, (bank + 15) % 16
    barrier = pltpu.get_barrier_semaphore()
    for peer in (right, left, at(0, 1, 0), at(0, -1, 0), at(1, 1, 0), at(1, -1, 0)):
        pl.semaphore_signal(barrier, inc=1, device_id={"bank": peer}, device_id_type=MESH)
    pl.semaphore_wait(barrier, 6)

    sends = []
    pairs = []
    pieces = (pl.ds(0, HALF_LANES), pl.ds(HALF_LANES, F - HALF_LANES))
    for h, cols in enumerate(pieces):
        for n, (source, target, peer) in enumerate(((2, low, right), (1, high, left))):
            c = pltpu.make_async_remote_copy(
                src_ref=part_ref.at[source, :, cols],
                dst_ref=target.at[:, cols],
                send_sem=pair_send.at[2 * h + n],
                recv_sem=pair_recv.at[2 * h + n],
                device_id={"bank": peer},
                device_id_type=MESH,
            )
            c.start()
            sends.append(c)
            pairs.append(c)
    out_ref[bank, :, F:] = times_ref[...]
    slots = {}

    def lanes(h, q):
        start = h * HALF_LANES
        if q == 0:
            return pl.ds(start, QUARTER)
        if q == 1:
            return pl.ds(start + QUARTER, HALF_LANES - QUARTER)
        return pl.ds(start, HALF_LANES)

    pending = {}

    def send(h, i, j, di, dj, q):
        block = at(h, i, j)
        key = (h, i - di, j - dj, q)
        slot = slots.setdefault(key, len(slots))
        c = pltpu.make_async_remote_copy(
            src_ref=out_ref.at[block, :, lanes(h, q)],
            dst_ref=out_ref.at[block, :, lanes(h, q)],
            send_sem=send_sem.at[slot],
            recv_sem=recv_sem.at[slot],
            device_id={"bank": at(h, di, dj)},
            device_id_type=MESH,
        )
        c.start()
        sends.append(c)
        pending[key] = c

    def arrive(h, i, j, q):
        pending.pop((h, i, j, q)).wait_recv()

    for h, cols in enumerate(pieces):
        pairs[2 * h].wait_recv()
        pairs[2 * h + 1].wait_recv()
        total = part_ref[0, :, cols].astype(f32) + low[:, cols].astype(f32) + high[:, cols].astype(f32)
        out_ref[bank, :, cols] = total.astype(bf16)
        send(h, 0, 0, 1, 0, 2)
        send(h, 0, 0, -1, 0, 2)
    for h in (0, 1):
        send(h, 0, 0, 0, 1, 2)
        send(h, 0, 0, 0, -1, 2)
    for h in (0, 1):
        arrive(h, -1, 0, 2)
        send(h, -1, 0, 1, 0, 0)
        arrive(h, 1, 0, 2)
        send(h, 1, 0, -1, 0, 1)
    for h in (0, 1):
        for i in (-1, 1):
            send(h, i, 0, 0, 1, 2)
            send(h, i, 0, 0, -1, 2)
    for h in (0, 1):
        arrive(h, 0, -1, 2)
        send(h, 0, -1, 0, 1, 0)
        arrive(h, 0, 1, 2)
        send(h, 0, 1, 0, -1, 1)
    for h in (0, 1):
        arrive(h, -2, 0, 0)
        arrive(h, 2, 0, 1)
        send(h, 2, 0, 0, 1, 2)
        send(h, 2, 0, 0, -1, 2)
    for i in (-1, 1, 2):
        for h in (0, 1):
            arrive(h, i, -1, 2)
            send(h, i, -1, 0, 1, 0)
            arrive(h, i, 1, 2)
            send(h, i, 1, 0, -1, 1)
    for key in list(pending):
        arrive(*key)
    for c in sends:
        c.wait_send()


def gather_call(partial, times):
    dma = pltpu.SemaphoreType.DMA
    return pl.pallas_call(
        gather_kernel,
        out_shape=jax.ShapeDtypeStruct((16, SLOTS, WIDE), bf16),
        in_specs=[VMEM_SPEC] * 2,
        out_specs=VMEM_SPEC,
        scratch_shapes=[pltpu.VMEM((SLOTS, F), bf16)] * 2 + [dma((4,))] * 2 + [dma((40,))] * 2,
        compiler_params=pltpu.CompilerParams(collective_id=0, has_side_effects=True, vmem_limit_bytes=16 * MIB),
        name="gather",
    )(partial, times)


SLICE_ROWS = 656
PIECES = ((0, 160), (160, 160), (320, 160), (480, 176))
ORDER = (4, 3, -3, 2, -2, 1, -1, 0)


def reduce_kernel(feat_ref, bank_ref, norm_ref, out_ref, weights, mine, theirs, twin, from_low, from_high, to_high, to_low, *sems):
    twin_send, twin_recv, ring_send, ring_recv, out_send, out_recv, back_send, back_recv = sems
    bank, tile = lax.axis_index("bank"), lax.axis_index("tile")
    z, core = tile // 2, tile % 2
    sibling = z * 2 + 1 - core
    high = ((z + 1) % 8) * 2 + core
    low = ((z + 7) % 8) * 2 + core
    other = 1 - core

    barrier = pltpu.get_barrier_semaphore()
    for peer in (sibling, high, low):
        pl.semaphore_signal(barrier, inc=1, device_id={"tile": peer}, device_id_type=MESH)

    scores = jnp.zeros((ROWS, R), f32)
    squares = jnp.zeros((8, R), f32)
    ones = jnp.ones((8, STEP), bf16)
    for k in range(F // STEP):
        cols = pl.ds(k * STEP, STEP)
        feat = feat_ref[:, cols]
        scores += lax.dot_general(bank_ref[:, cols], feat, NT, preferred_element_type=f32)
        wide = feat.astype(f32)
        squares += lax.dot_general(ones, (wide * wide).astype(bf16), NT, preferred_element_type=f32)
    box = 1.0 / jnp.sqrt(squares[0:1, :] * (1.0 / F) + EPSILON)
    row = lax.broadcasted_iota(jnp.int32, (ROWS, R), 0)
    orient = lax.broadcasted_iota(jnp.int32, (ROWS, R), 1)
    select = (orient == bank * 16 + (row & 15)).astype(bf16)
    times = lax.dot_general(select, feat_ref[:, F:], NT, preferred_element_type=f32)
    correl = scores * norm_ref[:, 0:1] * box
    weights[...] = (times * jnp.maximum(correl, 0.0)).astype(bf16)
    pl.semaphore_wait(barrier, 3)

    def remote(src, dst, send, recv, peer):
        return pltpu.make_async_remote_copy(
            src_ref=src, dst_ref=dst, send_sem=send, recv_sem=recv, device_id={"tile": peer}, device_id_type=MESH
        )

    def slot(offset):
        return (z + offset + 8) % 8

    def class_sums(h, offset, target):
        rows = weights[pl.ds(pl.multiple_of(h * 160, 32), 160), :]
        cols = pl.ds(pl.multiple_of(slot(offset) * STEP, STEP), STEP)
        out = jnp.dot(rows, feat_ref[:, cols], preferred_element_type=f32)
        for c in range(4):
            target[c * 160 : (c + 1) * 160, :] = out[:, c * 128 : (c + 1) * 128].astype(bf16)

    def weight_sums(h):
        rows = weights[pl.ds(pl.multiple_of(h * 160, 32), 160), :]
        total = lax.dot_general(
            jnp.ones((16, R), bf16),
            jnp.concatenate([rows, jnp.zeros((96, R), bf16)], axis=0),
            NT,
            preferred_element_type=f32,
        )
        upper = lax.broadcasted_iota(jnp.int32, (16, 128), 0) < 8
        return jnp.where(upper, total[:, :128], total[:, 128:]).astype(bf16)

    sends = []
    twins = {}
    ends = weight_sums(other), weight_sums(core)

    def to_twin(offset):
        m = ORDER.index(offset)
        class_sums(other, offset, theirs.at[m])
        theirs[m, 640:656, :] = ends[0]
        c = remote(theirs.at[m], twin.at[m], twin_send.at[m], twin_recv.at[m], sibling)
        c.start()
        sends.append(c)
        twins[offset] = c

    def keep(offset):
        m = ORDER.index(offset)
        class_sums(core, offset, mine.at[m])
        mine[m, 640:656, :] = ends[1]

    to_twin(4)
    keep(4)
    for offset in (3, -3):
        to_twin(offset)
        keep(offset)

    def pair(offset, rows):
        m = ORDER.index(offset)
        return mine[m, rows, :].astype(f32) + twin[m, rows, :].astype(f32)

    pieces = [pl.ds(*p) for p in PIECES]
    ring = {}

    def pass_on(step, direction, p):
        stage, landing, peer = (to_high, from_low, high) if direction > 0 else (to_low, from_high, low)
        n = (step * 2 + (direction > 0)) * 4 + p
        c = remote(stage.at[step, pieces[p]], landing.at[step, pieces[p]], ring_send.at[n], ring_recv.at[n], peer)
        c.start()
        sends.append(c)
        ring[(step, direction, p)] = c

    twins[4].wait_recv()
    for p in (0, 1):
        to_high[0, pieces[p], :] = pair(4, pieces[p]).astype(bf16)
        pass_on(0, 1, p)
        to_low[0, pieces[p + 2], :] = pair(4, pieces[p + 2]).astype(bf16)
        pass_on(0, -1, p + 2)
    for step in (1, 2, 3):
        for offset in (3 - step, step - 3)[: 1 if step == 3 else 2]:
            to_twin(offset)
            keep(offset)
        twins[4 - step].wait_recv()
        twins[step - 4].wait_recv()
        orders = {1: (2, 3, 0, 1), -1: (0, 1, 2, 3)}
        for q in range(4):
            for direction in (1, -1):
                stage, landing = (to_high, from_low) if direction > 0 else (to_low, from_high)
                p = orders[direction][q]
                value = pair(direction * (4 - step), pieces[p])
                if (step - 1, direction, p) in ring:
                    ring[(step - 1, direction, p)].wait_recv()
                    value = value + landing[step - 1, pieces[p], :].astype(f32)
                stage[step, pieces[p], :] = value.astype(bf16)
                pass_on(step, direction, p)
    twins[0].wait_recv()
    outs = {}
    backs = []

    def spread(offset, direction, p, n):
        where = out_ref.at[core, slot(offset), pieces[p]]
        c = remote(where, where, out_send.at[n * 4 + p], out_recv.at[n * 4 + p], high if direction > 0 else low)
        c.start()
        sends.append(c)
        outs[(offset - direction, direction, p)] = c

    def hand_over(offset, p):
        where = out_ref.at[core, slot(offset), pieces[p]]
        n = ORDER.index(offset) * 4 + p
        c = remote(where, where, back_send.at[n], back_recv.at[n], sibling)
        c.start()
        sends.append(c)
        backs.append(c)

    for q in range(4):
        for direction in (1, -1):
            ring[(3, direction, orders[direction][q])].wait_recv()
        if q < 2:
            continue
        for p in ((0, 2) if q == 2 else (1, 3)):
            value = pair(0, pieces[p]) + from_low[3, pieces[p], :].astype(f32) + from_high[3, pieces[p], :].astype(f32)
            out_ref[core, z, pieces[p], :] = value.astype(bf16)
            spread(0, 1, p, 0)
            spread(0, -1, p, 4)
            hand_over(0, p)
    for hop in (1, 2, 3):
        for p in (0, 2, 1, 3):
            for direction in (1, -1):
                n = hop if direction > 0 else 4 + hop
                offset = -hop * direction
                outs[(offset, direction, p)].wait_recv()
                if hop < 3 or (p < 2) == (direction > 0):
                    spread(offset, direction, p, n)
                hand_over(offset, p)
    for p in range(4):
        outs[(-4, 1, p) if p < 2 else (4, -1, p)].wait_recv()
        hand_over(4, p)
    for c in backs:
        c.wait_recv()
    for c in sends:
        c.wait_send()


def reduce_call(gathered, bank_rows, norms):
    dma = pltpu.SemaphoreType.DMA
    slices = pltpu.VMEM((8, SLICE_ROWS, 128), bf16)
    buffer = pltpu.VMEM((4, SLICE_ROWS, 128), bf16)
    return pl.pallas_call(
        reduce_kernel,
        out_shape=jax.ShapeDtypeStruct((2, 8, SLICE_ROWS, 128), bf16),
        in_specs=[VMEM_SPEC] * 3,
        out_specs=VMEM_SPEC,
        scratch_shapes=[pltpu.VMEM((ROWS, R), bf16)]
        + [slices] * 3
        + [buffer] * 4
        + [dma((8,))] * 2
        + [dma((32,))] * 6,
        compiler_params=pltpu.CompilerParams(collective_id=1, has_side_effects=True, vmem_limit_bytes=32 * MIB),
        name="reduce",
    )(gathered, bank_rows, norms)


def widen_kernel(in_ref, out_ref, counts_ref, wide, small, sem):
    copies = []
    for j in range(8):
        for h in range(2):
            rows, cols = pl.ds(h * 160, 160), pl.ds(j * STEP, STEP)
            for c in range(4):
                start = j * STEP + c * 128
                wide[rows, start : start + 128] = in_ref[h, j, c * 160 : (c + 1) * 160, :].astype(f32)
            c = pltpu.make_async_copy(wide.at[rows, cols], out_ref.at[rows, cols], sem.at[j * 2 + h])
            c.start()
            copies.append(c)
    orient = lax.broadcasted_iota(jnp.int32, (16, 128), 0)
    lane = lax.broadcasted_iota(jnp.int32, (16, 128), 1)
    entry = lax.broadcasted_iota(jnp.int32, (128, 128), 0)
    group = lax.broadcasted_iota(jnp.int32, (128, 128), 1)
    counts = jnp.zeros((16, 128), f32)
    for h in range(2):
        ends = in_ref[h, 0, 640:656, :].astype(f32)
        for first, line, valid in ((0, 0, 128), (128, 8, 32)):
            mine = jnp.where((lane % 16 == orient) & (lane < valid), ends[line : line + 1, :], 0.0).astype(bf16)
            place = (h * 160 + first + entry) // 16 == group
            counts += jnp.dot(mine, place.astype(f32).astype(bf16), preferred_element_type=f32)
    small[...] = counts[:, :C]
    c = pltpu.make_async_copy(small, counts_ref, sem.at[16])
    c.start()
    copies.append(c)
    for c in copies:
        c.wait()


def widen_call(total):
    return pl.pallas_call(
        widen_kernel,
        out_shape=(jax.ShapeDtypeStruct((ROWS, F), f32), jax.ShapeDtypeStruct((16, C), f32)),
        in_specs=[VMEM_SPEC],
        out_specs=(ANY_SPEC, ANY_SPEC),
        scratch_shapes=[pltpu.VMEM((ROWS, F), f32), pltpu.VMEM((16, C), f32), pltpu.SemaphoreType.DMA((17,))],
        compiler_params=pltpu.CompilerParams(vmem_limit_bytes=16 * MIB),
        name="widen",
    )(total)


def body(volume, pick_list, box_counts, orientations, orient_weight, reference_bank):
    bank_rows = jnp.transpose(reference_bank, (1, 0, 2)).reshape(ROWS, F)
    low, high, picks, counts, times, norms = halo_call(
        volume, pick_list, box_counts, orientations, orient_weight, bank_rows
    )
    partial = features_call(picks, counts, base_table(), low, volume, high)
    gathered = gather_call(partial, times)
    total = reduce_call(gathered.reshape(R, WIDE), bank_rows, norms)
    sums, weight_sums = widen_call(total)
    return jnp.transpose(sums.reshape(C, 16, F), (1, 0, 2)), weight_sums


def solution(mesh):
    in_specs = (
        P("tile", "bank", None),
        P(None, "tile", "bank", None),
        P("tile", "bank"),
        P("tile", "bank", None, None),
        P("tile", "bank", None, None),
        P("bank", None, None),
    )
    out_specs = (P("bank", None, None), P("bank", None))
    return jax.shard_map(body, mesh=mesh, in_specs=in_specs, out_specs=out_specs, check_vma=False)
```

```python
import functools

import jax
import jax.numpy as jnp
import numpy as np
from jax import lax
from jax.experimental import pallas as pl
from jax.experimental.pallas import tpu as pltpu
from jax.sharding import PartitionSpec as P

B = 96
L = 16
R = 256
F = 4096
C = 20
CX = 64
Z = 128
HALF = 48
EX = CX + 2 * HALF
SLOTS = 16
ROWS = 320
WIDE = F + R
EPSILON = 1e-06
PARTS = 3 * SLOTS
GROUP = 6
X_UNROLL = 16
XS = 161
YS = 65
MESH = pl.DeviceIdType.MESH
NT = (((1,), (1,)), ((), ()))
bf16 = jnp.bfloat16
f32 = jnp.float32
VMEM_SPEC = pl.BlockSpec(memory_space=pltpu.VMEM)
SMEM_SPEC = pl.BlockSpec(memory_space=pltpu.SMEM)
ANY_SPEC = pl.BlockSpec(memory_space=pl.ANY)
HBM_SPEC = pl.BlockSpec(memory_space=pltpu.MemorySpace.HBM)
MIB = 1024 * 1024


def in_hbm(value):
    return pltpu.with_memory_space_constraint(value, memory_space=pltpu.MemorySpace.HBM)


def base_table():
    n = np.arange(B).astype(np.float32)
    terms = np.arange(L)
    freq = np.where(terms <= L // 2, terms, terms - L // 2).astype(np.float32)
    angles = np.float32(2.0 * np.pi) * freq[:, None] * n[None, :] / np.float32(B)
    table = np.where((terms <= L // 2)[:, None], np.cos(angles), np.sin(angles)) / np.sqrt(np.float32(B))
    wide = np.zeros((L, 256), np.float32)
    wide[:, :B] = table
    return jnp.asarray(wide).astype(bf16).astype(f32)


def features_kernel(
    picks, counts, table_ref, lo_ref, own_ref, hi_ref, out_ref,
    block, spread, planes, tables, mixed, rows, order, shift_y, shift_z, load_sem,
):
    tile, bank = lax.axis_index("tile"), lax.axis_index("bank")
    base = table_ref[...]
    lane = lax.broadcasted_iota(jnp.int32, (L, 256), 1)

    load = pltpu.make_async_copy(own_ref, block, load_sem)
    load.start()

    begin = jnp.where(tile == 0, HALF, 0)
    end = jnp.where(tile == 15, HALF + CX, EX)
    inside = (lane >= begin) & (lane < end)

    def x_table(p, carry):
        shift = (picks[p // SLOTS, 0, 0, 0, p % SLOTS] - tile * CX) & 255
        shifted = jnp.where(inside, pltpu.roll(base, shift, axis=1), 0.0)
        tables[pl.ds(pl.multiple_of(p * L, L), L), :] = shifted.astype(bf16)
        return carry

    lax.fori_loop(0, PARTS, x_table, 0, unroll=8)

    def scatter(ref, first, count):
        def step(i, carry):
            spread[pl.ds(first + i, CX, stride=XS), :] = ref[i].astype(f32)
            return carry

        lax.fori_loop(0, count, step, 0, unroll=8)

    scatter(lo_ref, 0, HALF)
    scatter(hi_ref, HALF + CX, HALF)
    load.wait()
    scatter(block, HALF, CX)

    def pack(y, carry):
        planes[y] = spread[pl.ds(y * XS, EX), :].astype(bf16)
        return carry

    lax.fori_loop(0, CX, pack, 0, unroll=4)

    def note(p, count):
        k, s = p // SLOTS, p % SLOTS
        shift = picks[k, 1, 0, 0, s] - HALF - bank * CX
        order[count] = p
        shift_y[count] = shift & 255
        shift_z[count] = picks[k, 2, 0, 0, s]
        active = (s < counts[k, 0, 0]) & (shift > -B) & (shift < CX)
        return count + active.astype(jnp.int32)

    def x_step(i, count):
        for n in range(3):
            count = note(i * 3 + n, count)
        for n in range(2):
            y = i * 4 + n * 2
            rhs = jnp.concatenate([planes[y], planes[y + 1]], axis=1)
            for k in range(3):
                out = jnp.dot(tables[k * 256 : (k + 1) * 256, :EX], rhs, preferred_element_type=f32)
                mixed[pl.ds(k * 256 * YS + y, 256, stride=YS), :] = out[:, :Z]
                mixed[pl.ds(k * 256 * YS + y + 1, 256, stride=YS), :] = out[:, Z:]
        return count

    count = lax.fori_loop(0, PARTS // 3, x_step, jnp.int32(0), unroll=X_UNROLL)
    for g in range(GROUP):
        order[count + g] = order[0]
        shift_y[count + g] = shift_y[0]
        shift_z[count + g] = shift_z[0]
    rows[...] = jnp.zeros_like(rows)

    pick_b = (lane % 128 // L == lax.broadcasted_iota(jnp.int32, (L, 256), 0) % 8).astype(f32)
    out_row = lax.broadcasted_iota(jnp.int32, (2 * L, 256), 0)
    source = lax.broadcasted_iota(jnp.int32, (2 * L, 256), 1)
    collapse = ((source // L == out_row % L) & (source % L // 8 == out_row // L)).astype(bf16)

    def pair(first):
        which = (first, first + 1)
        starts = [order[n] * (L * YS) for n in which]
        y_table = jnp.concatenate(
            [
                jnp.where(lane // CX == j, pltpu.roll(base, (shift_y[n] + CX * j) & 255, axis=1), 0.0)
                for n in which
                for j in range(4)
            ],
            axis=0,
        ).astype(bf16)
        z_tables = [pltpu.roll(base, shift_z[n] + 128 * i, axis=1).astype(bf16) for i, n in enumerate(which)]
        z_wide = jnp.concatenate([z_tables[0]] * 8 + [z_tables[1]] * 8, axis=0)
        pieces = []
        for q in range(4):
            halves = [
                jnp.concatenate(
                    [mixed[pl.ds(start + (q * 4 + a) * YS, CX), :].astype(bf16) for a in range(4)], axis=0
                )
                for start in starts
            ]
            out = jnp.dot(y_table, jnp.concatenate(halves, axis=1), preferred_element_type=f32)
            pieces.append(jnp.concatenate([out[:CX, :Z], out[CX:, Z:]], axis=1).astype(bf16))
        second = jnp.concatenate(pieces, axis=0)
        third = lax.dot_general(second, z_wide, NT, preferred_element_type=f32)
        kept = (third.reshape(L, L, 256) * pick_b[None]).reshape(256, 256).astype(bf16)
        feature = jnp.dot(collapse, kept, preferred_element_type=f32)
        for i, n in enumerate(which):
            part = order[n]
            at = (part // SLOTS) * 256 + part % SLOTS
            cols = slice(i * 128, (i + 1) * 128)
            rows[0, pl.ds(at, L, stride=L), :] = feature[:L, cols]
            rows[1, pl.ds(at, L, stride=L), :] = feature[L:, cols]

    def boxes(i, carry):
        for g in range(GROUP // 2):
            pair(i * GROUP + g * 2)
        return carry

    lax.fori_loop(0, (count + GROUP - 1) // GROUP, boxes, 0)
    for k in range(3):
        for a in range(2 * L):
            first_row = k * 256 + a // 2 * L
            out_ref[k, :, a * 128 : (a + 1) * 128] = rows[a % 2, first_row : first_row + L, :].astype(bf16)


def features_call(picks, counts, table, lo, own, hi):
    return pl.pallas_call(
        features_kernel,
        out_shape=jax.ShapeDtypeStruct((3, SLOTS, F), bf16),
        in_specs=[SMEM_SPEC] * 2 + [VMEM_SPEC] * 2 + [HBM_SPEC, VMEM_SPEC],
        out_specs=VMEM_SPEC,
        scratch_shapes=[
            pltpu.VMEM((CX, CX, Z), bf16),
            pltpu.VMEM((CX * XS, Z), f32),
            pltpu.VMEM((CX, EX, Z), bf16),
            pltpu.VMEM((PARTS * L, 256), bf16),
            pltpu.VMEM((PARTS * L * YS, Z), f32),
            pltpu.VMEM((2, PARTS * L, 128), f32),
        ]
        + [pltpu.SMEM((PARTS + GROUP,), jnp.int32)] * 3
        + [pltpu.SemaphoreType.DMA],
        compiler_params=pltpu.CompilerParams(vmem_limit_bytes=44 * MIB),
        cost_estimate=pl.CostEstimate(flops=4 * 10**9, bytes_accessed=3 * 10**6, transcendentals=0),
        name="features",
    )(picks, counts, table, lo, in_hbm(own), hi)


STEP = 512


def halo_kernel(
    volume, pick_ref, count, orient_hbm, orient_weight_hbm, bank_hbm,
    lo, hi, picks, counts, times, norms,
    bank_rows, orient, orient_weight, bank_sem, own_sem, send_sem, recv_sem,
):
    tile, bank = lax.axis_index("tile"), lax.axis_index("bank")
    up, down = {"tile": (tile + 1) % 16}, {"tile": (tile + 15) % 16}
    right, left = {"bank": (bank + 1) % 16}, {"bank": (bank + 15) % 16}
    barrier = pltpu.get_barrier_semaphore()
    for peer in (up, down, right, left):
        pl.semaphore_signal(barrier, inc=1, device_id=peer, device_id_type=MESH)
    own = [
        pltpu.make_async_copy(pick_ref, picks.at[0], own_sem.at[0]),
        pltpu.make_async_copy(count, counts.at[0], own_sem.at[1]),
    ]
    loads = [
        pltpu.make_async_copy(orient_hbm, orient, own_sem.at[2]),
        pltpu.make_async_copy(orient_weight_hbm, orient_weight, own_sem.at[3]),
    ]
    load = pltpu.make_async_copy(bank_hbm, bank_rows, bank_sem)
    for c in own + loads + [load]:
        c.start()
    pl.semaphore_wait(barrier, 4)
    copies = []
    for n, (source, target, peer) in enumerate(
        (
            (volume.at[pl.ds(CX - HALF, HALF)], lo, up),
            (volume.at[pl.ds(0, HALF)], hi, down),
            (pick_ref, picks.at[1], right),
            (pick_ref, picks.at[2], left),
            (count, counts.at[1], right),
            (count, counts.at[2], left),
        )
    ):
        c = pltpu.make_async_remote_copy(
            src_ref=source,
            dst_ref=target,
            send_sem=send_sem.at[n],
            recv_sem=recv_sem.at[n],
            device_id=peer,
            device_id_type=MESH,
        )
        c.start()
        copies.append(c)

    for c in loads:
        c.wait()
    columns = orient[0, 0].astype(f32).T
    weight = orient_weight[0, 0].astype(f32).astype(bf16)
    choice = lax.broadcasted_iota(jnp.int32, (128, R), 1).astype(f32)
    row = lax.broadcasted_iota(jnp.int32, (SLOTS, R), 0)
    sums = jnp.zeros((SLOTS, R), f32)
    for s in range(SLOTS):
        hot = (columns[:, s : s + 1] == choice).astype(f32).astype(bf16)
        sums += jnp.where(row == s, jnp.dot(weight, hot, preferred_element_type=f32), 0.0)
    times[...] = jnp.where(row < count[...], sums, 0.0).astype(bf16)

    load.wait()
    ones = jnp.ones((128, STEP), bf16)
    total = jnp.zeros((ROWS, 128), f32)
    for k in range(F // STEP):
        wide = bank_rows[:, k * STEP : (k + 1) * STEP].astype(f32)
        total += lax.dot_general((wide * wide).astype(bf16), ones, NT, preferred_element_type=f32)
    norms[...] = 1.0 / (F * jnp.sqrt(total * (1.0 / F) + EPSILON))
    for c in own + copies:
        c.wait()


def halo_call(volume, pick_list, box_counts, orientations, orient_weight, bank_rows):
    dma = pltpu.SemaphoreType.DMA
    return pl.pallas_call(
        halo_kernel,
        out_shape=(
            jax.ShapeDtypeStruct((HALF, CX, Z), bf16),
            jax.ShapeDtypeStruct((HALF, CX, Z), bf16),
            jax.ShapeDtypeStruct((3,) + pick_list.shape, jnp.int32),
            jax.ShapeDtypeStruct((3,) + box_counts.shape, jnp.int32),
            jax.ShapeDtypeStruct((SLOTS, R), bf16),
            jax.ShapeDtypeStruct((ROWS, 128), f32),
        ),
        in_specs=[HBM_SPEC] * 2 + [VMEM_SPEC] + [HBM_SPEC] * 3,
        out_specs=(VMEM_SPEC,) * 6,
        scratch_shapes=[
            pltpu.VMEM((ROWS, F), bf16),
            pltpu.VMEM(orientations.shape, jnp.int32),
            pltpu.VMEM(orient_weight.shape, jnp.int32),
            dma,
            dma((4,)),
            dma((6,)),
            dma((6,)),
        ],
        compiler_params=pltpu.CompilerParams(collective_id=2, has_side_effects=True, vmem_limit_bytes=16 * MIB),
        name="halo",
    )(in_hbm(volume), in_hbm(pick_list), box_counts, *map(in_hbm, (orientations, orient_weight, bank_rows)))


QUARTER = 1024
HALF_LANES = WIDE // 2


def gather_kernel(part_ref, times_ref, out_ref, low, high, pair_send, pair_recv, send_sem, recv_sem):
    bank = lax.axis_index("bank")
    y, x = bank // 4, bank % 4

    def at(axis, i, j):
        dx, dy = (i, j) if axis == 0 else (j, i)
        return ((y + dy + 4) % 4) * 4 + (x + dx + 4) % 4

    right, left = (bank + 1) % 16, (bank + 15) % 16
    barrier = pltpu.get_barrier_semaphore()
    for peer in (right, left, at(0, 1, 0), at(0, -1, 0), at(1, 1, 0), at(1, -1, 0)):
        pl.semaphore_signal(barrier, inc=1, device_id={"bank": peer}, device_id_type=MESH)
    pl.semaphore_wait(barrier, 6)

    sends = []
    pairs = []
    pieces = (pl.ds(0, HALF_LANES), pl.ds(HALF_LANES, F - HALF_LANES))
    for h, cols in enumerate(pieces):
        for n, (source, target, peer) in enumerate(((2, low, right), (1, high, left))):
            c = pltpu.make_async_remote_copy(
                src_ref=part_ref.at[source, :, cols],
                dst_ref=target.at[:, cols],
                send_sem=pair_send.at[2 * h + n],
                recv_sem=pair_recv.at[2 * h + n],
                device_id={"bank": peer},
                device_id_type=MESH,
            )
            c.start()
            sends.append(c)
            pairs.append(c)
    out_ref[bank, :, F:] = times_ref[...]
    slots = {}

    def lanes(h, q):
        start = h * HALF_LANES
        if q == 0:
            return pl.ds(start, QUARTER)
        if q == 1:
            return pl.ds(start + QUARTER, HALF_LANES - QUARTER)
        return pl.ds(start, HALF_LANES)

    pending = {}

    def send(h, i, j, di, dj, q):
        block = at(h, i, j)
        key = (h, i - di, j - dj, q)
        slot = slots.setdefault(key, len(slots))
        c = pltpu.make_async_remote_copy(
            src_ref=out_ref.at[block, :, lanes(h, q)],
            dst_ref=out_ref.at[block, :, lanes(h, q)],
            send_sem=send_sem.at[slot],
            recv_sem=recv_sem.at[slot],
            device_id={"bank": at(h, di, dj)},
            device_id_type=MESH,
        )
        c.start()
        sends.append(c)
        pending[key] = c

    def arrive(h, i, j, q):
        pending.pop((h, i, j, q)).wait_recv()

    for h, cols in enumerate(pieces):
        pairs[2 * h].wait_recv()
        pairs[2 * h + 1].wait_recv()
        total = part_ref[0, :, cols].astype(f32) + low[:, cols].astype(f32) + high[:, cols].astype(f32)
        out_ref[bank, :, cols] = total.astype(bf16)
        send(h, 0, 0, 1, 0, 2)
        send(h, 0, 0, -1, 0, 2)
    for h in (0, 1):
        send(h, 0, 0, 0, 1, 2)
        send(h, 0, 0, 0, -1, 2)
    for h in (0, 1):
        arrive(h, -1, 0, 2)
        send(h, -1, 0, 1, 0, 0)
        arrive(h, 1, 0, 2)
        send(h, 1, 0, -1, 0, 1)
    for h in (0, 1):
        for i in (-1, 1):
            send(h, i, 0, 0, 1, 2)
            send(h, i, 0, 0, -1, 2)
    for h in (0, 1):
        arrive(h, 0, -1, 2)
        send(h, 0, -1, 0, 1, 0)
        arrive(h, 0, 1, 2)
        send(h, 0, 1, 0, -1, 1)
    for h in (0, 1):
        arrive(h, -2, 0, 0)
        arrive(h, 2, 0, 1)
        send(h, 2, 0, 0, 1, 2)
        send(h, 2, 0, 0, -1, 2)
    for i in (-1, 1, 2):
        for h in (0, 1):
            arrive(h, i, -1, 2)
            send(h, i, -1, 0, 1, 0)
            arrive(h, i, 1, 2)
            send(h, i, 1, 0, -1, 1)
    for key in list(pending):
        arrive(*key)
    for c in sends:
        c.wait_send()


def gather_call(partial, times):
    dma = pltpu.SemaphoreType.DMA
    return pl.pallas_call(
        gather_kernel,
        out_shape=jax.ShapeDtypeStruct((16, SLOTS, WIDE), bf16),
        in_specs=[VMEM_SPEC] * 2,
        out_specs=VMEM_SPEC,
        scratch_shapes=[pltpu.VMEM((SLOTS, F), bf16)] * 2 + [dma((4,))] * 2 + [dma((40,))] * 2,
        compiler_params=pltpu.CompilerParams(collective_id=0, has_side_effects=True, vmem_limit_bytes=16 * MIB),
        name="gather",
    )(partial, times)


SLICE_ROWS = 656
PIECES = ((0, 160), (160, 160), (320, 160), (480, 176))
ORDER = (4, 3, -3, 2, -2, 1, -1, 0)


def reduce_kernel(feat_ref, bank_ref, norm_ref, out_ref, weights, mine, theirs, twin, from_low, from_high, to_high, to_low, *sems):
    twin_send, twin_recv, ring_send, ring_recv, out_send, out_recv, back_send, back_recv = sems
    bank, tile = lax.axis_index("bank"), lax.axis_index("tile")
    z, core = tile // 2, tile % 2
    sibling = z * 2 + 1 - core
    high = ((z + 1) % 8) * 2 + core
    low = ((z + 7) % 8) * 2 + core
    other = 1 - core

    barrier = pltpu.get_barrier_semaphore()
    for peer in (sibling, high, low):
        pl.semaphore_signal(barrier, inc=1, device_id={"tile": peer}, device_id_type=MESH)

    scores = jnp.zeros((ROWS, R), f32)
    squares = jnp.zeros((8, R), f32)
    ones = jnp.ones((8, STEP), bf16)
    for k in range(F // STEP):
        cols = pl.ds(k * STEP, STEP)
        feat = feat_ref[:, cols]
        scores += lax.dot_general(bank_ref[:, cols], feat, NT, preferred_element_type=f32)
        wide = feat.astype(f32)
        squares += lax.dot_general(ones, (wide * wide).astype(bf16), NT, preferred_element_type=f32)
    box = 1.0 / jnp.sqrt(squares[0:1, :] * (1.0 / F) + EPSILON)
    row = lax.broadcasted_iota(jnp.int32, (ROWS, R), 0)
    orient = lax.broadcasted_iota(jnp.int32, (ROWS, R), 1)
    select = (orient == bank * 16 + (row & 15)).astype(bf16)
    times = lax.dot_general(select, feat_ref[:, F:], NT, preferred_element_type=f32)
    correl = scores * norm_ref[:, 0:1] * box
    weights[...] = (times * jnp.maximum(correl, 0.0)).astype(bf16)
    pl.semaphore_wait(barrier, 3)

    def remote(src, dst, send, recv, peer):
        return pltpu.make_async_remote_copy(
            src_ref=src, dst_ref=dst, send_sem=send, recv_sem=recv, device_id={"tile": peer}, device_id_type=MESH
        )

    def slot(offset):
        return (z + offset + 8) % 8

    def class_sums(h, offset, target):
        rows = weights[pl.ds(pl.multiple_of(h * 160, 32), 160), :]
        cols = pl.ds(pl.multiple_of(slot(offset) * STEP, STEP), STEP)
        out = jnp.dot(rows, feat_ref[:, cols], preferred_element_type=f32)
        for c in range(4):
            target[c * 160 : (c + 1) * 160, :] = out[:, c * 128 : (c + 1) * 128].astype(bf16)

    def weight_sums(h):
        rows = weights[pl.ds(pl.multiple_of(h * 160, 32), 160), :]
        total = lax.dot_general(
            jnp.ones((16, R), bf16),
            jnp.concatenate([rows, jnp.zeros((96, R), bf16)], axis=0),
            NT,
            preferred_element_type=f32,
        )
        upper = lax.broadcasted_iota(jnp.int32, (16, 128), 0) < 8
        return jnp.where(upper, total[:, :128], total[:, 128:]).astype(bf16)

    sends = []
    twins = {}
    ends = weight_sums(other), weight_sums(core)

    def to_twin(offset):
        m = ORDER.index(offset)
        class_sums(other, offset, theirs.at[m])
        theirs[m, 640:656, :] = ends[0]
        c = remote(theirs.at[m], twin.at[m], twin_send.at[m], twin_recv.at[m], sibling)
        c.start()
        sends.append(c)
        twins[offset] = c

    def keep(offset):
        m = ORDER.index(offset)
        class_sums(core, offset, mine.at[m])
        mine[m, 640:656, :] = ends[1]

    to_twin(4)
    keep(4)
    for offset in (3, -3):
        to_twin(offset)
        keep(offset)

    def pair(offset, rows):
        m = ORDER.index(offset)
        return mine[m, rows, :].astype(f32) + twin[m, rows, :].astype(f32)

    pieces = [pl.ds(*p) for p in PIECES]
    orders = {1: (2, 0, 1, 3), -1: (0, 2, 3, 1)}
    ring = {}

    def pass_on(step, direction, p):
        stage, landing, peer = (to_high, from_low, high) if direction > 0 else (to_low, from_high, low)
        n = (step * 2 + (direction > 0)) * 4 + p
        c = remote(stage.at[step, pieces[p]], landing.at[step, pieces[p]], ring_send.at[n], ring_recv.at[n], peer)
        c.start()
        sends.append(c)
        ring[(step, direction, p)] = c

    twins[4].wait_recv()
    for p in (0, 1):
        to_high[0, pieces[p], :] = pair(4, pieces[p]).astype(bf16)
        pass_on(0, 1, p)
        to_low[0, pieces[p + 2], :] = pair(4, pieces[p + 2]).astype(bf16)
        pass_on(0, -1, p + 2)
    for step in (1, 2, 3):
        for offset in (3 - step, step - 3)[: 1 if step == 3 else 2]:
            to_twin(offset)
            keep(offset)
        twins[4 - step].wait_recv()
        twins[step - 4].wait_recv()
        for q in range(4):
            for direction in (1, -1):
                stage, landing = (to_high, from_low) if direction > 0 else (to_low, from_high)
                p = orders[direction][q]
                value = pair(direction * (4 - step), pieces[p])
                if (step - 1, direction, p) in ring:
                    ring[(step - 1, direction, p)].wait_recv()
                    value = value + landing[step - 1, pieces[p], :].astype(f32)
                stage[step, pieces[p], :] = value.astype(bf16)
                pass_on(step, direction, p)
    twins[0].wait_recv()
    outs = {}
    backs = []

    def spread(offset, direction, p, n):
        where = out_ref.at[core, slot(offset), pieces[p]]
        c = remote(where, where, out_send.at[n * 4 + p], out_recv.at[n * 4 + p], high if direction > 0 else low)
        c.start()
        sends.append(c)
        outs[(offset - direction, direction, p)] = c

    def hand_over(offset, p):
        where = out_ref.at[core, slot(offset), pieces[p]]
        n = ORDER.index(offset) * 4 + p
        c = remote(where, where, back_send.at[n], back_recv.at[n], sibling)
        c.start()
        sends.append(c)
        backs.append(c)

    for q in range(4):
        for direction in (1, -1):
            ring[(3, direction, orders[direction][q])].wait_recv()
        if q % 2 == 0:
            continue
        for p in ((0, 2) if q == 1 else (1, 3)):
            value = pair(0, pieces[p]) + from_low[3, pieces[p], :].astype(f32) + from_high[3, pieces[p], :].astype(f32)
            out_ref[core, z, pieces[p], :] = value.astype(bf16)
            spread(0, 1, p, 0)
            spread(0, -1, p, 4)
            hand_over(0, p)
    for hop in (1, 2, 3):
        for p in (0, 2, 1, 3):
            for direction in (1, -1):
                n = hop if direction > 0 else 4 + hop
                offset = -hop * direction
                outs[(offset, direction, p)].wait_recv()
                if hop < 3 or (p < 2) == (direction > 0):
                    spread(offset, direction, p, n)
                hand_over(offset, p)
    for p in range(4):
        outs[(-4, 1, p) if p < 2 else (4, -1, p)].wait_recv()
        hand_over(4, p)
    for c in backs:
        c.wait_recv()
    for c in sends:
        c.wait_send()


def reduce_call(gathered, bank_rows, norms):
    dma = pltpu.SemaphoreType.DMA
    slices = pltpu.VMEM((8, SLICE_ROWS, 128), bf16)
    buffer = pltpu.VMEM((4, SLICE_ROWS, 128), bf16)
    return pl.pallas_call(
        reduce_kernel,
        out_shape=jax.ShapeDtypeStruct((2, 8, SLICE_ROWS, 128), bf16),
        in_specs=[VMEM_SPEC] * 3,
        out_specs=VMEM_SPEC,
        scratch_shapes=[pltpu.VMEM((ROWS, R), bf16)]
        + [slices] * 3
        + [buffer] * 4
        + [dma((8,))] * 2
        + [dma((32,))] * 6,
        compiler_params=pltpu.CompilerParams(collective_id=1, has_side_effects=True, vmem_limit_bytes=32 * MIB),
        name="reduce",
    )(gathered, bank_rows, norms)


def widen_kernel(in_ref, out_ref, counts_ref, wide, small, sem):
    copies = []
    for j in range(8):
        for h in range(2):
            rows, cols = pl.ds(h * 160, 160), pl.ds(j * STEP, STEP)
            for c in range(4):
                start = j * STEP + c * 128
                wide[rows, start : start + 128] = in_ref[h, j, c * 160 : (c + 1) * 160, :].astype(f32)
            c = pltpu.make_async_copy(wide.at[rows, cols], out_ref.at[rows, cols], sem.at[j * 2 + h])
            c.start()
            copies.append(c)
    orient = lax.broadcasted_iota(jnp.int32, (16, 128), 0)
    lane = lax.broadcasted_iota(jnp.int32, (16, 128), 1)
    entry = lax.broadcasted_iota(jnp.int32, (128, 128), 0)
    group = lax.broadcasted_iota(jnp.int32, (128, 128), 1)
    counts = jnp.zeros((16, 128), f32)
    for h in range(2):
        ends = in_ref[h, 0, 640:656, :].astype(f32)
        for first, line, valid in ((0, 0, 128), (128, 8, 32)):
            mine = jnp.where((lane % 16 == orient) & (lane < valid), ends[line : line + 1, :], 0.0).astype(bf16)
            place = (h * 160 + first + entry) // 16 == group
            counts += jnp.dot(mine, place.astype(f32).astype(bf16), preferred_element_type=f32)
    small[...] = counts[:, :C]
    c = pltpu.make_async_copy(small, counts_ref, sem.at[16])
    c.start()
    copies.append(c)
    for c in copies:
        c.wait()


def widen_call(total):
    return pl.pallas_call(
        widen_kernel,
        out_shape=(jax.ShapeDtypeStruct((ROWS, F), f32), jax.ShapeDtypeStruct((16, C), f32)),
        in_specs=[VMEM_SPEC],
        out_specs=(ANY_SPEC, ANY_SPEC),
        scratch_shapes=[pltpu.VMEM((ROWS, F), f32), pltpu.VMEM((16, C), f32), pltpu.SemaphoreType.DMA((17,))],
        compiler_params=pltpu.CompilerParams(vmem_limit_bytes=16 * MIB),
        name="widen",
    )(total)


def body(volume, pick_list, box_counts, orientations, orient_weight, reference_bank):
    bank_rows = jnp.transpose(reference_bank, (1, 0, 2)).reshape(ROWS, F)
    low, high, picks, counts, times, norms = halo_call(
        volume, pick_list, box_counts, orientations, orient_weight, bank_rows
    )
    partial = features_call(picks, counts, base_table(), low, volume, high)
    gathered = gather_call(partial, times)
    total = reduce_call(gathered.reshape(R, WIDE), bank_rows, norms)
    sums, weight_sums = widen_call(total)
    return jnp.transpose(sums.reshape(C, 16, F), (1, 0, 2)), weight_sums


def solution(mesh):
    in_specs = (
        P("tile", "bank", None),
        P(None, "tile", "bank", None),
        P("tile", "bank"),
        P("tile", "bank", None, None),
        P("tile", "bank", None, None),
        P("bank", None, None),
    )
    out_specs = (P("bank", None, None), P("bank", None))
    return jax.shard_map(body, mesh=mesh, in_specs=in_specs, out_specs=out_specs, check_vma=False)
```

```python
import functools

import jax
import jax.numpy as jnp
import numpy as np
from jax import lax
from jax.experimental import pallas as pl
from jax.experimental.pallas import tpu as pltpu
from jax.sharding import PartitionSpec as P

B = 96
L = 16
R = 256
F = 4096
C = 20
CX = 64
Z = 128
HALF = 48
EX = CX + 2 * HALF
SLOTS = 16
ROWS = 320
WIDE = F + R
EPSILON = 1e-06
PARTS = 3 * SLOTS
GROUP = 6
X_UNROLL = 16
XS = 161
YS = 65
MESH = pl.DeviceIdType.MESH
NT = (((1,), (1,)), ((), ()))
bf16 = jnp.bfloat16
f32 = jnp.float32
VMEM_SPEC = pl.BlockSpec(memory_space=pltpu.VMEM)
SMEM_SPEC = pl.BlockSpec(memory_space=pltpu.SMEM)
ANY_SPEC = pl.BlockSpec(memory_space=pl.ANY)
HBM_SPEC = pl.BlockSpec(memory_space=pltpu.MemorySpace.HBM)
MIB = 1024 * 1024


def in_hbm(value):
    return pltpu.with_memory_space_constraint(value, memory_space=pltpu.MemorySpace.HBM)


def base_table():
    n = np.arange(B).astype(np.float32)
    terms = np.arange(L)
    freq = np.where(terms <= L // 2, terms, terms - L // 2).astype(np.float32)
    angles = np.float32(2.0 * np.pi) * freq[:, None] * n[None, :] / np.float32(B)
    table = np.where((terms <= L // 2)[:, None], np.cos(angles), np.sin(angles)) / np.sqrt(np.float32(B))
    wide = np.zeros((L, 256), np.float32)
    wide[:, :B] = table
    return jnp.asarray(wide).astype(bf16).astype(f32)


def features_kernel(
    picks, counts, table_ref, lo_ref, own_ref, hi_ref, out_ref,
    block, spread, planes, tables, mixed, rows, order, shift_y, shift_z, load_sem,
):
    tile, bank = lax.axis_index("tile"), lax.axis_index("bank")
    base = table_ref[...]
    lane = lax.broadcasted_iota(jnp.int32, (L, 256), 1)

    load = pltpu.make_async_copy(own_ref, block, load_sem)
    load.start()

    begin = jnp.where(tile == 0, HALF, 0)
    end = jnp.where(tile == 15, HALF + CX, EX)
    inside = (lane >= begin) & (lane < end)

    def x_table(p, carry):
        shift = (picks[p // SLOTS, 0, 0, 0, p % SLOTS] - tile * CX) & 255
        shifted = jnp.where(inside, pltpu.roll(base, shift, axis=1), 0.0)
        tables[pl.ds(pl.multiple_of(p * L, L), L), :] = shifted.astype(bf16)
        return carry

    lax.fori_loop(0, PARTS, x_table, 0, unroll=8)

    def scatter(ref, first, count):
        def step(i, carry):
            spread[pl.ds(first + i, CX, stride=XS), :] = ref[i].astype(f32)
            return carry

        lax.fori_loop(0, count, step, 0, unroll=8)

    scatter(lo_ref, 0, HALF)
    scatter(hi_ref, HALF + CX, HALF)
    load.wait()
    scatter(block, HALF, CX)

    def pack(y, carry):
        planes[y] = spread[pl.ds(y * XS, EX), :].astype(bf16)
        return carry

    lax.fori_loop(0, CX, pack, 0, unroll=4)

    def note(p, count):
        k, s = p // SLOTS, p % SLOTS
        shift = picks[k, 1, 0, 0, s] - HALF - bank * CX
        order[count] = p
        shift_y[count] = shift & 255
        shift_z[count] = picks[k, 2, 0, 0, s]
        active = (s < counts[k, 0, 0]) & (shift > -B) & (shift < CX)
        return count + active.astype(jnp.int32)

    def x_step(i, count):
        for n in range(3):
            count = note(i * 3 + n, count)
        for n in range(2):
            y = i * 4 + n * 2
            rhs = jnp.concatenate([planes[y], planes[y + 1]], axis=1)
            for k in range(3):
                out = jnp.dot(tables[k * 256 : (k + 1) * 256, :EX], rhs, preferred_element_type=f32)
                mixed[pl.ds(k * 256 * YS + y, 256, stride=YS), :] = out[:, :Z]
                mixed[pl.ds(k * 256 * YS + y + 1, 256, stride=YS), :] = out[:, Z:]
        return count

    count = lax.fori_loop(0, PARTS // 3, x_step, jnp.int32(0), unroll=X_UNROLL)
    for g in range(GROUP):
        order[count + g] = order[0]
        shift_y[count + g] = shift_y[0]
        shift_z[count + g] = shift_z[0]
    rows[...] = jnp.zeros_like(rows)

    pick_b = (lane % 128 // L == lax.broadcasted_iota(jnp.int32, (L, 256), 0) % 8).astype(f32)
    out_row = lax.broadcasted_iota(jnp.int32, (2 * L, 256), 0)
    source = lax.broadcasted_iota(jnp.int32, (2 * L, 256), 1)
    collapse = ((source // L == out_row % L) & (source % L // 8 == out_row // L)).astype(bf16)

    def pair(first):
        which = (first, first + 1)
        starts = [order[n] * (L * YS) for n in which]
        y_table = jnp.concatenate(
            [
                jnp.where(lane // CX == j, pltpu.roll(base, (shift_y[n] + CX * j) & 255, axis=1), 0.0)
                for n in which
                for j in range(4)
            ],
            axis=0,
        ).astype(bf16)
        z_tables = [pltpu.roll(base, shift_z[n] + 128 * i, axis=1).astype(bf16) for i, n in enumerate(which)]
        z_wide = jnp.concatenate([z_tables[0]] * 8 + [z_tables[1]] * 8, axis=0)
        pieces = []
        for q in range(4):
            halves = [
                jnp.concatenate(
                    [mixed[pl.ds(start + (q * 4 + a) * YS, CX), :].astype(bf16) for a in range(4)], axis=0
                )
                for start in starts
            ]
            out = jnp.dot(y_table, jnp.concatenate(halves, axis=1), preferred_element_type=f32)
            pieces.append(jnp.concatenate([out[:CX, :Z], out[CX:, Z:]], axis=1).astype(bf16))
        second = jnp.concatenate(pieces, axis=0)
        third = lax.dot_general(second, z_wide, NT, preferred_element_type=f32)
        kept = (third.reshape(L, L, 256) * pick_b[None]).reshape(256, 256).astype(bf16)
        feature = jnp.dot(collapse, kept, preferred_element_type=f32)
        for i, n in enumerate(which):
            part = order[n]
            at = (part // SLOTS) * 256 + part % SLOTS
            cols = slice(i * 128, (i + 1) * 128)
            rows[0, pl.ds(at, L, stride=L), :] = feature[:L, cols]
            rows[1, pl.ds(at, L, stride=L), :] = feature[L:, cols]

    def boxes(i, carry):
        for g in range(GROUP // 2):
            pair(i * GROUP + g * 2)
        return carry

    lax.fori_loop(0, (count + GROUP - 1) // GROUP, boxes, 0)
    for k in range(3):
        for a in range(2 * L):
            first_row = k * 256 + a // 2 * L
            out_ref[k, :, a * 128 : (a + 1) * 128] = rows[a % 2, first_row : first_row + L, :].astype(bf16)


def features_call(picks, counts, table, lo, own, hi):
    return pl.pallas_call(
        features_kernel,
        out_shape=jax.ShapeDtypeStruct((3, SLOTS, F), bf16),
        in_specs=[SMEM_SPEC] * 2 + [VMEM_SPEC] * 2 + [HBM_SPEC, VMEM_SPEC],
        out_specs=VMEM_SPEC,
        scratch_shapes=[
            pltpu.VMEM((CX, CX, Z), bf16),
            pltpu.VMEM((CX * XS, Z), f32),
            pltpu.VMEM((CX, EX, Z), bf16),
            pltpu.VMEM((PARTS * L, 256), bf16),
            pltpu.VMEM((PARTS * L * YS, Z), f32),
            pltpu.VMEM((2, PARTS * L, 128), f32),
        ]
        + [pltpu.SMEM((PARTS + GROUP,), jnp.int32)] * 3
        + [pltpu.SemaphoreType.DMA],
        compiler_params=pltpu.CompilerParams(vmem_limit_bytes=44 * MIB),
        cost_estimate=pl.CostEstimate(flops=4 * 10**9, bytes_accessed=3 * 10**6, transcendentals=0),
        name="features",
    )(picks, counts, table, lo, in_hbm(own), hi)


STEP = 512


def halo_kernel(
    volume, pick_ref, count, orient_hbm, orient_weight_hbm, bank_hbm,
    lo, hi, picks, counts, times, norms,
    bank_rows, orient, orient_weight, bank_sem, own_sem, send_sem, recv_sem,
):
    tile, bank = lax.axis_index("tile"), lax.axis_index("bank")
    up, down = {"tile": (tile + 1) % 16}, {"tile": (tile + 15) % 16}
    right, left = {"bank": (bank + 1) % 16}, {"bank": (bank + 15) % 16}
    barrier = pltpu.get_barrier_semaphore()
    for peer in (up, down, right, left):
        pl.semaphore_signal(barrier, inc=1, device_id=peer, device_id_type=MESH)
    own = [
        pltpu.make_async_copy(pick_ref, picks.at[0], own_sem.at[0]),
        pltpu.make_async_copy(count, counts.at[0], own_sem.at[1]),
    ]
    loads = [
        pltpu.make_async_copy(orient_hbm, orient, own_sem.at[2]),
        pltpu.make_async_copy(orient_weight_hbm, orient_weight, own_sem.at[3]),
    ]
    load = pltpu.make_async_copy(bank_hbm, bank_rows, bank_sem)
    for c in own + loads + [load]:
        c.start()
    pl.semaphore_wait(barrier, 4)
    copies = []
    for n, (source, target, peer) in enumerate(
        (
            (volume.at[pl.ds(CX - HALF, HALF)], lo, up),
            (volume.at[pl.ds(0, HALF)], hi, down),
            (pick_ref, picks.at[1], right),
            (pick_ref, picks.at[2], left),
            (count, counts.at[1], right),
            (count, counts.at[2], left),
        )
    ):
        c = pltpu.make_async_remote_copy(
            src_ref=source,
            dst_ref=target,
            send_sem=send_sem.at[n],
            recv_sem=recv_sem.at[n],
            device_id=peer,
            device_id_type=MESH,
        )
        c.start()
        copies.append(c)

    for c in loads:
        c.wait()
    columns = orient[0, 0].astype(f32).T
    weight = orient_weight[0, 0].astype(f32).astype(bf16)
    choice = lax.broadcasted_iota(jnp.int32, (128, R), 1).astype(f32)
    row = lax.broadcasted_iota(jnp.int32, (SLOTS, R), 0)
    sums = jnp.zeros((SLOTS, R), f32)
    for s in range(SLOTS):
        hot = (columns[:, s : s + 1] == choice).astype(f32).astype(bf16)
        sums += jnp.where(row == s, jnp.dot(weight, hot, preferred_element_type=f32), 0.0)
    times[...] = jnp.where(row < count[...], sums, 0.0).astype(bf16)

    load.wait()
    ones = jnp.ones((128, STEP), bf16)
    total = jnp.zeros((ROWS, 128), f32)
    for k in range(F // STEP):
        wide = bank_rows[:, k * STEP : (k + 1) * STEP].astype(f32)
        total += lax.dot_general((wide * wide).astype(bf16), ones, NT, preferred_element_type=f32)
    norms[...] = 1.0 / (F * jnp.sqrt(total * (1.0 / F) + EPSILON))
    for c in own + copies:
        c.wait()


def halo_call(volume, pick_list, box_counts, orientations, orient_weight, bank_rows):
    dma = pltpu.SemaphoreType.DMA
    return pl.pallas_call(
        halo_kernel,
        out_shape=(
            jax.ShapeDtypeStruct((HALF, CX, Z), bf16),
            jax.ShapeDtypeStruct((HALF, CX, Z), bf16),
            jax.ShapeDtypeStruct((3,) + pick_list.shape, jnp.int32),
            jax.ShapeDtypeStruct((3,) + box_counts.shape, jnp.int32),
            jax.ShapeDtypeStruct((SLOTS, R), bf16),
            jax.ShapeDtypeStruct((ROWS, 128), f32),
        ),
        in_specs=[HBM_SPEC] * 2 + [VMEM_SPEC] + [HBM_SPEC] * 3,
        out_specs=(VMEM_SPEC,) * 6,
        scratch_shapes=[
            pltpu.VMEM((ROWS, F), bf16),
            pltpu.VMEM(orientations.shape, jnp.int32),
            pltpu.VMEM(orient_weight.shape, jnp.int32),
            dma,
            dma((4,)),
            dma((6,)),
            dma((6,)),
        ],
        compiler_params=pltpu.CompilerParams(collective_id=2, has_side_effects=True, vmem_limit_bytes=16 * MIB),
        name="halo",
    )(in_hbm(volume), in_hbm(pick_list), box_counts, *map(in_hbm, (orientations, orient_weight, bank_rows)))


QUARTER = 1024
HALF_LANES = WIDE // 2


def gather_kernel(part_ref, times_ref, out_ref, low, high, pair_send, pair_recv, send_sem, recv_sem):
    bank = lax.axis_index("bank")
    y, x = bank // 4, bank % 4

    def at(axis, i, j):
        dx, dy = (i, j) if axis == 0 else (j, i)
        return ((y + dy + 4) % 4) * 4 + (x + dx + 4) % 4

    right, left = (bank + 1) % 16, (bank + 15) % 16
    barrier = pltpu.get_barrier_semaphore()
    for peer in (right, left, at(0, 1, 0), at(0, -1, 0), at(1, 1, 0), at(1, -1, 0)):
        pl.semaphore_signal(barrier, inc=1, device_id={"bank": peer}, device_id_type=MESH)
    pl.semaphore_wait(barrier, 6)

    sends = []
    pairs = []
    pieces = (pl.ds(0, HALF_LANES), pl.ds(HALF_LANES, F - HALF_LANES))
    for h, cols in enumerate(pieces):
        for n, (source, target, peer) in enumerate(((2, low, right), (1, high, left))):
            c = pltpu.make_async_remote_copy(
                src_ref=part_ref.at[source, :, cols],
                dst_ref=target.at[:, cols],
                send_sem=pair_send.at[2 * h + n],
                recv_sem=pair_recv.at[2 * h + n],
                device_id={"bank": peer},
                device_id_type=MESH,
            )
            c.start()
            sends.append(c)
            pairs.append(c)
    slots = {}

    def lanes(h, q):
        start = h * HALF_LANES
        if q == 0:
            return pl.ds(start, QUARTER)
        if q == 1:
            return pl.ds(start + QUARTER, HALF_LANES - QUARTER)
        return pl.ds(start, HALF_LANES)

    pending = {}

    def send(h, i, j, di, dj, q):
        block = at(h, i, j)
        key = (h, i - di, j - dj, q)
        slot = slots.setdefault(key, len(slots))
        c = pltpu.make_async_remote_copy(
            src_ref=out_ref.at[block, :, lanes(h, q)],
            dst_ref=out_ref.at[block, :, lanes(h, q)],
            send_sem=send_sem.at[slot],
            recv_sem=recv_sem.at[slot],
            device_id={"bank": at(h, di, dj)},
            device_id_type=MESH,
        )
        c.start()
        sends.append(c)
        pending[key] = c

    def arrive(h, i, j, q):
        pending.pop((h, i, j, q)).wait_recv()

    squares = jnp.zeros((SLOTS, 1), f32)
    for h, cols in enumerate(pieces):
        pairs[2 * h].wait_recv()
        pairs[2 * h + 1].wait_recv()
        total = part_ref[0, :, cols].astype(f32) + low[:, cols].astype(f32) + high[:, cols].astype(f32)
        total = total.astype(bf16)
        out_ref[bank, :, cols] = total
        wide = total.astype(f32)
        squares += jnp.sum(wide * wide, axis=1, keepdims=True)
        if h == 1:
            scale = 1.0 / jnp.sqrt(squares * (1.0 / F) + EPSILON)
            out_ref[bank, :, F:] = (times_ref[...].astype(f32) * scale).astype(bf16)
        send(h, 0, 0, 1, 0, 2)
        send(h, 0, 0, -1, 0, 2)
    for h in (0, 1):
        send(h, 0, 0, 0, 1, 2)
        send(h, 0, 0, 0, -1, 2)
    for h in (0, 1):
        arrive(h, -1, 0, 2)
        send(h, -1, 0, 1, 0, 0)
        arrive(h, 1, 0, 2)
        send(h, 1, 0, -1, 0, 1)
    for h in (0, 1):
        for i in (-1, 1):
            send(h, i, 0, 0, 1, 2)
            send(h, i, 0, 0, -1, 2)
    for h in (0, 1):
        arrive(h, 0, -1, 2)
        send(h, 0, -1, 0, 1, 0)
        arrive(h, 0, 1, 2)
        send(h, 0, 1, 0, -1, 1)
    for h in (0, 1):
        arrive(h, -2, 0, 0)
        arrive(h, 2, 0, 1)
        send(h, 2, 0, 0, 1, 2)
        send(h, 2, 0, 0, -1, 2)
    for i in (-1, 1, 2):
        for h in (0, 1):
            arrive(h, i, -1, 2)
            send(h, i, -1, 0, 1, 0)
            arrive(h, i, 1, 2)
            send(h, i, 1, 0, -1, 1)
    for key in list(pending):
        arrive(*key)
    for c in sends:
        c.wait_send()


def gather_call(partial, times):
    dma = pltpu.SemaphoreType.DMA
    return pl.pallas_call(
        gather_kernel,
        out_shape=jax.ShapeDtypeStruct((16, SLOTS, WIDE), bf16),
        in_specs=[VMEM_SPEC] * 2,
        out_specs=VMEM_SPEC,
        scratch_shapes=[pltpu.VMEM((SLOTS, F), bf16)] * 2 + [dma((4,))] * 2 + [dma((40,))] * 2,
        compiler_params=pltpu.CompilerParams(collective_id=0, has_side_effects=True, vmem_limit_bytes=16 * MIB),
        name="gather",
    )(partial, times)


SLICE_ROWS = 656
PIECES = ((0, 160), (160, 160), (320, 160), (480, 176))
ORDER = (4, 3, -3, 2, -2, 1, -1, 0)


def reduce_kernel(feat_ref, bank_ref, norm_ref, out_ref, weights, mine, theirs, twin, from_low, from_high, to_high, to_low, *sems):
    twin_send, twin_recv, ring_send, ring_recv, out_send, out_recv, back_send, back_recv = sems
    bank, tile = lax.axis_index("bank"), lax.axis_index("tile")
    z, core = tile // 2, tile % 2
    sibling = z * 2 + 1 - core
    high = ((z + 1) % 8) * 2 + core
    low = ((z + 7) % 8) * 2 + core
    other = 1 - core

    barrier = pltpu.get_barrier_semaphore()
    for peer in (sibling, high, low):
        pl.semaphore_signal(barrier, inc=1, device_id={"tile": peer}, device_id_type=MESH)

    scores = jnp.zeros((ROWS, R), f32)
    for k in range(F // STEP):
        cols = pl.ds(k * STEP, STEP)
        scores += lax.dot_general(bank_ref[:, cols], feat_ref[:, cols], NT, preferred_element_type=f32)
    row = lax.broadcasted_iota(jnp.int32, (ROWS, R), 0)
    orient = lax.broadcasted_iota(jnp.int32, (ROWS, R), 1)
    select = (orient == bank * 16 + (row & 15)).astype(bf16)
    times = lax.dot_general(select, feat_ref[:, F:], NT, preferred_element_type=f32)
    correl = scores * norm_ref[:, 0:1]
    weights[...] = (times * jnp.maximum(correl, 0.0)).astype(bf16)
    pl.semaphore_wait(barrier, 3)

    def remote(src, dst, send, recv, peer):
        return pltpu.make_async_remote_copy(
            src_ref=src, dst_ref=dst, send_sem=send, recv_sem=recv, device_id={"tile": peer}, device_id_type=MESH
        )

    def slot(offset):
        return (z + offset + 8) % 8

    def class_sums(h, offset, target):
        rows = weights[pl.ds(pl.multiple_of(h * 160, 32), 160), :]
        cols = pl.ds(pl.multiple_of(slot(offset) * STEP, STEP), STEP)
        out = jnp.dot(rows, feat_ref[:, cols], preferred_element_type=f32)
        for c in range(4):
            target[c * 160 : (c + 1) * 160, :] = out[:, c * 128 : (c + 1) * 128].astype(bf16)

    def weight_sums(h):
        rows = weights[pl.ds(pl.multiple_of(h * 160, 32), 160), :]
        total = lax.dot_general(
            jnp.ones((16, R), bf16),
            jnp.concatenate([rows, jnp.zeros((96, R), bf16)], axis=0),
            NT,
            preferred_element_type=f32,
        )
        upper = lax.broadcasted_iota(jnp.int32, (16, 128), 0) < 8
        return jnp.where(upper, total[:, :128], total[:, 128:]).astype(bf16)

    sends = []
    twins = {}
    ends = weight_sums(other), weight_sums(core)

    def to_twin(offset):
        m = ORDER.index(offset)
        class_sums(other, offset, theirs.at[m])
        theirs[m, 640:656, :] = ends[0]
        c = remote(theirs.at[m], twin.at[m], twin_send.at[m], twin_recv.at[m], sibling)
        c.start()
        sends.append(c)
        twins[offset] = c

    def keep(offset):
        m = ORDER.index(offset)
        class_sums(core, offset, mine.at[m])
        mine[m, 640:656, :] = ends[1]

    to_twin(4)
    keep(4)
    for offset in (3, -3):
        to_twin(offset)
        keep(offset)

    def pair(offset, rows):
        m = ORDER.index(offset)
        return mine[m, rows, :].astype(f32) + twin[m, rows, :].astype(f32)

    pieces = [pl.ds(*p) for p in PIECES]
    orders = {1: (2, 3, 0, 1), -1: (0, 1, 2, 3)}
    ring = {}

    def pass_on(step, direction, p):
        stage, landing, peer = (to_high, from_low, high) if direction > 0 else (to_low, from_high, low)
        n = (step * 2 + (direction > 0)) * 4 + p
        c = remote(stage.at[step, pieces[p]], landing.at[step, pieces[p]], ring_send.at[n], ring_recv.at[n], peer)
        c.start()
        sends.append(c)
        ring[(step, direction, p)] = c

    twins[4].wait_recv()
    for p in (0, 1):
        to_high[0, pieces[p], :] = pair(4, pieces[p]).astype(bf16)
        pass_on(0, 1, p)
        to_low[0, pieces[p + 2], :] = pair(4, pieces[p + 2]).astype(bf16)
        pass_on(0, -1, p + 2)
    for step in (1, 2, 3):
        for offset in (3 - step, step - 3)[: 1 if step == 3 else 2]:
            to_twin(offset)
            keep(offset)
        twins[4 - step].wait_recv()
        twins[step - 4].wait_recv()
        for q in range(4):
            for direction in (1, -1):
                stage, landing = (to_high, from_low) if direction > 0 else (to_low, from_high)
                p = orders[direction][q]
                value = pair(direction * (4 - step), pieces[p])
                if (step - 1, direction, p) in ring:
                    ring[(step - 1, direction, p)].wait_recv()
                    value = value + landing[step - 1, pieces[p], :].astype(f32)
                stage[step, pieces[p], :] = value.astype(bf16)
                pass_on(step, direction, p)
    twins[0].wait_recv()
    outs = {}
    backs = []

    def spread(offset, direction, p, n):
        where = out_ref.at[core, slot(offset), pieces[p]]
        c = remote(where, where, out_send.at[n * 4 + p], out_recv.at[n * 4 + p], high if direction > 0 else low)
        c.start()
        sends.append(c)
        outs[(offset - direction, direction, p)] = c

    def hand_over(offset, p):
        where = out_ref.at[core, slot(offset), pieces[p]]
        n = ORDER.index(offset) * 4 + p
        c = remote(where, where, back_send.at[n], back_recv.at[n], sibling)
        c.start()
        sends.append(c)
        backs.append(c)

    for q in range(4):
        for direction in (1, -1):
            ring[(3, direction, orders[direction][q])].wait_recv()
        if q < 2:
            continue
        for p in ((0, 2) if q == 2 else (1, 3)):
            value = pair(0, pieces[p]) + from_low[3, pieces[p], :].astype(f32) + from_high[3, pieces[p], :].astype(f32)
            out_ref[core, z, pieces[p], :] = value.astype(bf16)
            spread(0, 1, p, 0)
            spread(0, -1, p, 4)
            hand_over(0, p)
    for hop in (1, 2, 3):
        for p in (0, 2, 1, 3):
            for direction in (1, -1):
                n = hop if direction > 0 else 4 + hop
                offset = -hop * direction
                outs[(offset, direction, p)].wait_recv()
                if hop < 3 or (p < 2) == (direction > 0):
                    spread(offset, direction, p, n)
                hand_over(offset, p)
    for p in range(4):
        outs[(-4, 1, p) if p < 2 else (4, -1, p)].wait_recv()
        hand_over(4, p)
    for c in backs:
        c.wait_recv()
    for c in sends:
        c.wait_send()


def reduce_call(gathered, bank_rows, norms):
    dma = pltpu.SemaphoreType.DMA
    slices = pltpu.VMEM((8, SLICE_ROWS, 128), bf16)
    buffer = pltpu.VMEM((4, SLICE_ROWS, 128), bf16)
    return pl.pallas_call(
        reduce_kernel,
        out_shape=jax.ShapeDtypeStruct((2, 8, SLICE_ROWS, 128), bf16),
        in_specs=[VMEM_SPEC] * 3,
        out_specs=VMEM_SPEC,
        scratch_shapes=[pltpu.VMEM((ROWS, R), bf16)]
        + [slices] * 3
        + [buffer] * 4
        + [dma((8,))] * 2
        + [dma((32,))] * 6,
        compiler_params=pltpu.CompilerParams(collective_id=1, has_side_effects=True, vmem_limit_bytes=32 * MIB),
        name="reduce",
    )(gathered, bank_rows, norms)


def widen_kernel(in_ref, out_ref, counts_ref, wide, small, sem):
    copies = []
    for j in range(8):
        for h in range(2):
            rows, cols = pl.ds(h * 160, 160), pl.ds(j * STEP, STEP)
            for c in range(4):
                start = j * STEP + c * 128
                wide[rows, start : start + 128] = in_ref[h, j, c * 160 : (c + 1) * 160, :].astype(f32)
            c = pltpu.make_async_copy(wide.at[rows, cols], out_ref.at[rows, cols], sem.at[j * 2 + h])
            c.start()
            copies.append(c)
    orient = lax.broadcasted_iota(jnp.int32, (16, 128), 0)
    lane = lax.broadcasted_iota(jnp.int32, (16, 128), 1)
    entry = lax.broadcasted_iota(jnp.int32, (128, 128), 0)
    group = lax.broadcasted_iota(jnp.int32, (128, 128), 1)
    counts = jnp.zeros((16, 128), f32)
    for h in range(2):
        ends = in_ref[h, 0, 640:656, :].astype(f32)
        for first, line, valid in ((0, 0, 128), (128, 8, 32)):
            mine = jnp.where((lane % 16 == orient) & (lane < valid), ends[line : line + 1, :], 0.0).astype(bf16)
            place = (h * 160 + first + entry) // 16 == group
            counts += jnp.dot(mine, place.astype(f32).astype(bf16), preferred_element_type=f32)
    small[...] = counts[:, :C]
    c = pltpu.make_async_copy(small, counts_ref, sem.at[16])
    c.start()
    copies.append(c)
    for c in copies:
        c.wait()


def widen_call(total):
    return pl.pallas_call(
        widen_kernel,
        out_shape=(jax.ShapeDtypeStruct((ROWS, F), f32), jax.ShapeDtypeStruct((16, C), f32)),
        in_specs=[VMEM_SPEC],
        out_specs=(ANY_SPEC, ANY_SPEC),
        scratch_shapes=[pltpu.VMEM((ROWS, F), f32), pltpu.VMEM((16, C), f32), pltpu.SemaphoreType.DMA((17,))],
        compiler_params=pltpu.CompilerParams(vmem_limit_bytes=16 * MIB),
        name="widen",
    )(total)


def body(volume, pick_list, box_counts, orientations, orient_weight, reference_bank):
    bank_rows = jnp.transpose(reference_bank, (1, 0, 2)).reshape(ROWS, F)
    low, high, picks, counts, times, norms = halo_call(
        volume, pick_list, box_counts, orientations, orient_weight, bank_rows
    )
    partial = features_call(picks, counts, base_table(), low, volume, high)
    gathered = gather_call(partial, times)
    total = reduce_call(gathered.reshape(R, WIDE), bank_rows, norms)
    sums, weight_sums = widen_call(total)
    return jnp.transpose(sums.reshape(C, 16, F), (1, 0, 2)), weight_sums


def solution(mesh):
    in_specs = (
        P("tile", "bank", None),
        P(None, "tile", "bank", None),
        P("tile", "bank"),
        P("tile", "bank", None, None),
        P("tile", "bank", None, None),
        P("bank", None, None),
    )
    out_specs = (P("bank", None, None), P("bank", None))
    return jax.shard_map(body, mesh=mesh, in_specs=in_specs, out_specs=out_specs, check_vma=False)
```

```python
import functools

import jax
import jax.numpy as jnp
import numpy as np
from jax import lax
from jax.experimental import pallas as pl
from jax.experimental.pallas import tpu as pltpu
from jax.sharding import PartitionSpec as P

B = 96
L = 16
R = 256
F = 4096
C = 20
CX = 64
Z = 128
HALF = 48
EX = CX + 2 * HALF
SLOTS = 16
ROWS = 320
WIDE = F + R
EPSILON = 1e-06
PARTS = 3 * SLOTS
GROUP = 6
X_UNROLL = 16
XS = 161
YS = 65
MESH = pl.DeviceIdType.MESH
NT = (((1,), (1,)), ((), ()))
bf16 = jnp.bfloat16
f32 = jnp.float32
VMEM_SPEC = pl.BlockSpec(memory_space=pltpu.VMEM)
SMEM_SPEC = pl.BlockSpec(memory_space=pltpu.SMEM)
ANY_SPEC = pl.BlockSpec(memory_space=pl.ANY)
HBM_SPEC = pl.BlockSpec(memory_space=pltpu.MemorySpace.HBM)
MIB = 1024 * 1024


def in_hbm(value):
    return pltpu.with_memory_space_constraint(value, memory_space=pltpu.MemorySpace.HBM)


def base_table():
    n = np.arange(B).astype(np.float32)
    terms = np.arange(L)
    freq = np.where(terms <= L // 2, terms, terms - L // 2).astype(np.float32)
    angles = np.float32(2.0 * np.pi) * freq[:, None] * n[None, :] / np.float32(B)
    table = np.where((terms <= L // 2)[:, None], np.cos(angles), np.sin(angles)) / np.sqrt(np.float32(B))
    wide = np.zeros((L, 256), np.float32)
    wide[:, :B] = table
    return jnp.asarray(wide).astype(bf16).astype(f32)


def features_kernel(
    picks, counts, table_ref, lo_ref, own_ref, hi_ref, out_ref,
    block, spread, planes, tables, mixed, rows, order, shift_y, shift_z, load_sem,
):
    tile, bank = lax.axis_index("tile"), lax.axis_index("bank")
    base = table_ref[...]
    lane = lax.broadcasted_iota(jnp.int32, (L, 256), 1)

    load = pltpu.make_async_copy(own_ref, block, load_sem)
    load.start()

    begin = jnp.where(tile == 0, HALF, 0)
    end = jnp.where(tile == 15, HALF + CX, EX)
    inside = (lane >= begin) & (lane < end)

    def x_table(p, carry):
        shift = (picks[p // SLOTS, 0, 0, 0, p % SLOTS] - tile * CX) & 255
        shifted = jnp.where(inside, pltpu.roll(base, shift, axis=1), 0.0)
        tables[pl.ds(pl.multiple_of(p * L, L), L), :] = shifted.astype(bf16)
        return carry

    lax.fori_loop(0, PARTS, x_table, 0, unroll=8)

    def scatter(ref, first, count):
        def step(i, carry):
            spread[pl.ds(first + i, CX, stride=XS), :] = ref[i].astype(f32)
            return carry

        lax.fori_loop(0, count, step, 0, unroll=8)

    scatter(lo_ref, 0, HALF)
    scatter(hi_ref, HALF + CX, HALF)
    load.wait()
    scatter(block, HALF, CX)

    def pack(y, carry):
        planes[y] = spread[pl.ds(y * XS, EX), :].astype(bf16)
        return carry

    lax.fori_loop(0, CX, pack, 0, unroll=4)

    def note(p, count):
        k, s = p // SLOTS, p % SLOTS
        shift = picks[k, 1, 0, 0, s] - HALF - bank * CX
        order[count] = p
        shift_y[count] = shift & 255
        shift_z[count] = picks[k, 2, 0, 0, s]
        active = (s < counts[k, 0, 0]) & (shift > -B) & (shift < CX)
        return count + active.astype(jnp.int32)

    def x_step(i, count):
        for n in range(3):
            count = note(i * 3 + n, count)
        for n in range(2):
            y = i * 4 + n * 2
            rhs = jnp.concatenate([planes[y], planes[y + 1]], axis=1)
            for k in range(3):
                out = jnp.dot(tables[k * 256 : (k + 1) * 256, :EX], rhs, preferred_element_type=f32)
                mixed[pl.ds(k * 256 * YS + y, 256, stride=YS), :] = out[:, :Z]
                mixed[pl.ds(k * 256 * YS + y + 1, 256, stride=YS), :] = out[:, Z:]
        return count

    count = lax.fori_loop(0, PARTS // 3, x_step, jnp.int32(0), unroll=X_UNROLL)
    for g in range(GROUP):
        order[count + g] = order[0]
        shift_y[count + g] = shift_y[0]
        shift_z[count + g] = shift_z[0]
    rows[...] = jnp.zeros_like(rows)

    pick_b = (lane % 128 // L == lax.broadcasted_iota(jnp.int32, (L, 256), 0) % 8).astype(f32)
    out_row = lax.broadcasted_iota(jnp.int32, (2 * L, 256), 0)
    source = lax.broadcasted_iota(jnp.int32, (2 * L, 256), 1)
    collapse = ((source // L == out_row % L) & (source % L // 8 == out_row // L)).astype(bf16)

    def pair(first):
        which = (first, first + 1)
        starts = [order[n] * (L * YS) for n in which]
        y_table = jnp.concatenate(
            [
                jnp.where(lane // CX == j, pltpu.roll(base, (shift_y[n] + CX * j) & 255, axis=1), 0.0)
                for n in which
                for j in range(4)
            ],
            axis=0,
        ).astype(bf16)
        z_tables = [pltpu.roll(base, shift_z[n] + 128 * i, axis=1).astype(bf16) for i, n in enumerate(which)]
        z_wide = jnp.concatenate([z_tables[0]] * 8 + [z_tables[1]] * 8, axis=0)
        pieces = []
        for q in range(4):
            halves = [
                jnp.concatenate(
                    [mixed[pl.ds(start + (q * 4 + a) * YS, CX), :].astype(bf16) for a in range(4)], axis=0
                )
                for start in starts
            ]
            out = jnp.dot(y_table, jnp.concatenate(halves, axis=1), preferred_element_type=f32)
            pieces.append(jnp.concatenate([out[:CX, :Z], out[CX:, Z:]], axis=1).astype(bf16))
        second = jnp.concatenate(pieces, axis=0)
        third = lax.dot_general(second, z_wide, NT, preferred_element_type=f32)
        kept = (third.reshape(L, L, 256) * pick_b[None]).reshape(256, 256).astype(bf16)
        feature = jnp.dot(collapse, kept, preferred_element_type=f32)
        for i, n in enumerate(which):
            part = order[n]
            at = (part // SLOTS) * 256 + part % SLOTS
            cols = slice(i * 128, (i + 1) * 128)
            rows[0, pl.ds(at, L, stride=L), :] = feature[:L, cols]
            rows[1, pl.ds(at, L, stride=L), :] = feature[L:, cols]

    def boxes(i, carry):
        for g in range(GROUP // 2):
            pair(i * GROUP + g * 2)
        return carry

    lax.fori_loop(0, (count + GROUP - 1) // GROUP, boxes, 0)
    for k in range(3):
        for a in range(2 * L):
            first_row = k * 256 + a // 2 * L
            out_ref[k, :, a * 128 : (a + 1) * 128] = rows[a % 2, first_row : first_row + L, :].astype(bf16)


def features_call(picks, counts, table, lo, own, hi):
    return pl.pallas_call(
        features_kernel,
        out_shape=jax.ShapeDtypeStruct((3, SLOTS, F), bf16),
        in_specs=[SMEM_SPEC] * 2 + [VMEM_SPEC] * 2 + [HBM_SPEC, VMEM_SPEC],
        out_specs=VMEM_SPEC,
        scratch_shapes=[
            pltpu.VMEM((CX, CX, Z), bf16),
            pltpu.VMEM((CX * XS, Z), f32),
            pltpu.VMEM((CX, EX, Z), bf16),
            pltpu.VMEM((PARTS * L, 256), bf16),
            pltpu.VMEM((PARTS * L * YS, Z), f32),
            pltpu.VMEM((2, PARTS * L, 128), f32),
        ]
        + [pltpu.SMEM((PARTS + GROUP,), jnp.int32)] * 3
        + [pltpu.SemaphoreType.DMA],
        compiler_params=pltpu.CompilerParams(vmem_limit_bytes=44 * MIB),
        cost_estimate=pl.CostEstimate(flops=4 * 10**9, bytes_accessed=3 * 10**6, transcendentals=0),
        name="features",
    )(picks, counts, table, lo, in_hbm(own), hi)


STEP = 512


def halo_kernel(
    volume, pick_ref, count, orient_hbm, orient_weight_hbm, bank_hbm,
    lo, hi, picks, counts, times, norms,
    bank_rows, orient, orient_weight, bank_sem, own_sem, send_sem, recv_sem,
):
    tile, bank = lax.axis_index("tile"), lax.axis_index("bank")
    up, down = {"tile": (tile + 1) % 16}, {"tile": (tile + 15) % 16}
    right, left = {"bank": (bank + 1) % 16}, {"bank": (bank + 15) % 16}
    barrier = pltpu.get_barrier_semaphore()
    for peer in (up, down, right, left):
        pl.semaphore_signal(barrier, inc=1, device_id=peer, device_id_type=MESH)
    own = [
        pltpu.make_async_copy(pick_ref, picks.at[0], own_sem.at[0]),
        pltpu.make_async_copy(count, counts.at[0], own_sem.at[1]),
    ]
    loads = [
        pltpu.make_async_copy(orient_hbm, orient, own_sem.at[2]),
        pltpu.make_async_copy(orient_weight_hbm, orient_weight, own_sem.at[3]),
    ]
    load = pltpu.make_async_copy(bank_hbm, bank_rows, bank_sem)
    for c in own + loads + [load]:
        c.start()
    pl.semaphore_wait(barrier, 4)
    copies = []
    for n, (source, target, peer) in enumerate(
        (
            (volume.at[pl.ds(CX - HALF, HALF)], lo, up),
            (volume.at[pl.ds(0, HALF)], hi, down),
            (pick_ref, picks.at[1], right),
            (pick_ref, picks.at[2], left),
            (count, counts.at[1], right),
            (count, counts.at[2], left),
        )
    ):
        c = pltpu.make_async_remote_copy(
            src_ref=source,
            dst_ref=target,
            send_sem=send_sem.at[n],
            recv_sem=recv_sem.at[n],
            device_id=peer,
            device_id_type=MESH,
        )
        c.start()
        copies.append(c)

    for c in loads:
        c.wait()
    columns = orient[0, 0].astype(f32).T
    weight = orient_weight[0, 0].astype(f32).astype(bf16)
    choice = lax.broadcasted_iota(jnp.int32, (128, R), 1).astype(f32)
    row = lax.broadcasted_iota(jnp.int32, (SLOTS, R), 0)
    sums = jnp.zeros((SLOTS, R), f32)
    for s in range(SLOTS):
        hot = (columns[:, s : s + 1] == choice).astype(f32).astype(bf16)
        sums += jnp.where(row == s, jnp.dot(weight, hot, preferred_element_type=f32), 0.0)
    times[...] = jnp.where(row < count[...], sums, 0.0).astype(bf16)

    load.wait()
    ones = jnp.ones((128, STEP), bf16)
    total = jnp.zeros((ROWS, 128), f32)
    for k in range(F // STEP):
        wide = bank_rows[:, k * STEP : (k + 1) * STEP].astype(f32)
        total += lax.dot_general((wide * wide).astype(bf16), ones, NT, preferred_element_type=f32)
    norms[...] = 1.0 / (F * jnp.sqrt(total * (1.0 / F) + EPSILON))
    for c in own + copies:
        c.wait()


def halo_call(volume, pick_list, box_counts, orientations, orient_weight, bank_rows):
    dma = pltpu.SemaphoreType.DMA
    return pl.pallas_call(
        halo_kernel,
        out_shape=(
            jax.ShapeDtypeStruct((HALF, CX, Z), bf16),
            jax.ShapeDtypeStruct((HALF, CX, Z), bf16),
            jax.ShapeDtypeStruct((3,) + pick_list.shape, jnp.int32),
            jax.ShapeDtypeStruct((3,) + box_counts.shape, jnp.int32),
            jax.ShapeDtypeStruct((SLOTS, R), bf16),
            jax.ShapeDtypeStruct((ROWS, 128), f32),
        ),
        in_specs=[HBM_SPEC] * 2 + [VMEM_SPEC] + [HBM_SPEC] * 3,
        out_specs=(VMEM_SPEC,) * 6,
        scratch_shapes=[
            pltpu.VMEM((ROWS, F), bf16),
            pltpu.VMEM(orientations.shape, jnp.int32),
            pltpu.VMEM(orient_weight.shape, jnp.int32),
            dma,
            dma((4,)),
            dma((6,)),
            dma((6,)),
        ],
        compiler_params=pltpu.CompilerParams(collective_id=2, has_side_effects=True, vmem_limit_bytes=16 * MIB),
        name="halo",
    )(in_hbm(volume), in_hbm(pick_list), box_counts, *map(in_hbm, (orientations, orient_weight, bank_rows)))


QUARTER = 1024
HALF_LANES = WIDE // 2


def gather_kernel(part_ref, times_ref, out_ref, low, high, pair_send, pair_recv, send_sem, recv_sem):
    bank = lax.axis_index("bank")
    y, x = bank // 4, bank % 4

    def at(axis, i, j):
        dx, dy = (i, j) if axis == 0 else (j, i)
        return ((y + dy + 4) % 4) * 4 + (x + dx + 4) % 4

    right, left = (bank + 1) % 16, (bank + 15) % 16
    barrier = pltpu.get_barrier_semaphore()
    for peer in (right, left, at(0, 1, 0), at(0, -1, 0), at(1, 1, 0), at(1, -1, 0)):
        pl.semaphore_signal(barrier, inc=1, device_id={"bank": peer}, device_id_type=MESH)
    pl.semaphore_wait(barrier, 6)

    sends = []
    pairs = []
    pieces = (pl.ds(0, HALF_LANES), pl.ds(HALF_LANES, F - HALF_LANES))
    for h, cols in enumerate(pieces):
        for n, (source, target, peer) in enumerate(((2, low, right), (1, high, left))):
            c = pltpu.make_async_remote_copy(
                src_ref=part_ref.at[source, :, cols],
                dst_ref=target.at[:, cols],
                send_sem=pair_send.at[2 * h + n],
                recv_sem=pair_recv.at[2 * h + n],
                device_id={"bank": peer},
                device_id_type=MESH,
            )
            c.start()
            sends.append(c)
            pairs.append(c)
    slots = {}

    def lanes(h, q):
        start = h * HALF_LANES
        if q == 0:
            return pl.ds(start, QUARTER)
        if q == 1:
            return pl.ds(start + QUARTER, HALF_LANES - QUARTER)
        return pl.ds(start, HALF_LANES)

    pending = {}

    def send(h, i, j, di, dj, q):
        block = at(h, i, j)
        key = (h, i - di, j - dj, q)
        slot = slots.setdefault(key, len(slots))
        c = pltpu.make_async_remote_copy(
            src_ref=out_ref.at[block, :, lanes(h, q)],
            dst_ref=out_ref.at[block, :, lanes(h, q)],
            send_sem=send_sem.at[slot],
            recv_sem=recv_sem.at[slot],
            device_id={"bank": at(h, di, dj)},
            device_id_type=MESH,
        )
        c.start()
        sends.append(c)
        pending[key] = c

    def arrive(h, i, j, q):
        pending.pop((h, i, j, q)).wait_recv()

    squares = jnp.zeros((SLOTS, 1), f32)
    for h, cols in enumerate(pieces):
        pairs[2 * h].wait_recv()
        pairs[2 * h + 1].wait_recv()
        total = part_ref[0, :, cols].astype(f32) + low[:, cols].astype(f32) + high[:, cols].astype(f32)
        total = total.astype(bf16)
        out_ref[bank, :, cols] = total
        wide = total.astype(f32)
        squares += jnp.sum(wide * wide, axis=1, keepdims=True)
        if h == 1:
            scale = 1.0 / jnp.sqrt(squares * (1.0 / F) + EPSILON)
            out_ref[bank, :, F:] = (times_ref[...].astype(f32) * scale).astype(bf16)
        send(h, 0, 0, 1, 0, 2)
        send(h, 0, 0, -1, 0, 2)
    for h in (0, 1):
        send(h, 0, 0, 0, 1, 2)
        send(h, 0, 0, 0, -1, 2)
    for h in (0, 1):
        arrive(h, -1, 0, 2)
        send(h, -1, 0, 1, 0, 0)
        arrive(h, 1, 0, 2)
        send(h, 1, 0, -1, 0, 1)
    for h in (0, 1):
        for i in (-1, 1):
            send(h, i, 0, 0, 1, 2)
            send(h, i, 0, 0, -1, 2)
    for h in (0, 1):
        arrive(h, 0, -1, 2)
        send(h, 0, -1, 0, 1, 0)
        arrive(h, 0, 1, 2)
        send(h, 0, 1, 0, -1, 1)
    for h in (0, 1):
        arrive(h, -2, 0, 0)
        arrive(h, 2, 0, 1)
        send(h, 2, 0, 0, 1, 2)
        send(h, 2, 0, 0, -1, 2)
    for i in (-1, 1, 2):
        for h in (0, 1):
            arrive(h, i, -1, 2)
            send(h, i, -1, 0, 1, 0)
            arrive(h, i, 1, 2)
            send(h, i, 1, 0, -1, 1)
    for key in list(pending):
        arrive(*key)
    for c in sends:
        c.wait_send()


def gather_call(partial, times):
    dma = pltpu.SemaphoreType.DMA
    return pl.pallas_call(
        gather_kernel,
        out_shape=jax.ShapeDtypeStruct((16, SLOTS, WIDE), bf16),
        in_specs=[VMEM_SPEC] * 2,
        out_specs=VMEM_SPEC,
        scratch_shapes=[pltpu.VMEM((SLOTS, F), bf16)] * 2 + [dma((4,))] * 2 + [dma((40,))] * 2,
        compiler_params=pltpu.CompilerParams(collective_id=0, has_side_effects=True, vmem_limit_bytes=16 * MIB),
        name="gather",
    )(partial, times)


SLICE_ROWS = 656
PIECES = ((0, 160), (160, 160), (320, 160), (480, 176))
ORDER = (4, 3, -3, 2, -2, 1, -1, 0)


def reduce_kernel(feat_ref, bank_ref, norm_ref, out_ref, weights, mine, theirs, twin, from_low, from_high, to_high, to_low, *sems):
    twin_send, twin_recv, ring_send, ring_recv, out_send, out_recv, back_send, back_recv = sems
    bank, tile = lax.axis_index("bank"), lax.axis_index("tile")
    z, core = tile // 2, tile % 2
    sibling = z * 2 + 1 - core
    high = ((z + 1) % 8) * 2 + core
    low = ((z + 7) % 8) * 2 + core
    other = 1 - core

    barrier = pltpu.get_barrier_semaphore()
    for peer in (sibling, high, low):
        pl.semaphore_signal(barrier, inc=1, device_id={"tile": peer}, device_id_type=MESH)

    scores = jnp.zeros((ROWS, R), f32)
    for k in range(F // STEP):
        cols = pl.ds(k * STEP, STEP)
        scores += lax.dot_general(bank_ref[:, cols], feat_ref[:, cols], NT, preferred_element_type=f32)
    row = lax.broadcasted_iota(jnp.int32, (ROWS, R), 0)
    orient = lax.broadcasted_iota(jnp.int32, (ROWS, R), 1)
    select = (orient == bank * 16 + (row & 15)).astype(bf16)
    times = lax.dot_general(select, feat_ref[:, F:], NT, preferred_element_type=f32)
    correl = scores * norm_ref[:, 0:1]
    weights[...] = (times * jnp.maximum(correl, 0.0)).astype(bf16)
    pl.semaphore_wait(barrier, 3)

    def remote(src, dst, send, recv, peer):
        return pltpu.make_async_remote_copy(
            src_ref=src, dst_ref=dst, send_sem=send, recv_sem=recv, device_id={"tile": peer}, device_id_type=MESH
        )

    def slot(offset):
        return (z + offset + 8) % 8

    def class_sums(h, offset, target):
        rows = weights[pl.ds(pl.multiple_of(h * 160, 32), 160), :]
        cols = pl.ds(pl.multiple_of(slot(offset) * STEP, STEP), STEP)
        out = jnp.dot(rows, feat_ref[:, cols], preferred_element_type=f32)
        for c in range(4):
            target[c * 160 : (c + 1) * 160, :] = out[:, c * 128 : (c + 1) * 128].astype(bf16)

    def weight_sums(h):
        rows = weights[pl.ds(pl.multiple_of(h * 160, 32), 160), :]
        total = lax.dot_general(
            jnp.ones((16, R), bf16),
            jnp.concatenate([rows, jnp.zeros((96, R), bf16)], axis=0),
            NT,
            preferred_element_type=f32,
        )
        upper = lax.broadcasted_iota(jnp.int32, (16, 128), 0) < 8
        return jnp.where(upper, total[:, :128], total[:, 128:]).astype(bf16)

    sends = []
    twins = {}
    ends = weight_sums(other), weight_sums(core)

    def to_twin(offset):
        m = ORDER.index(offset)
        class_sums(other, offset, theirs.at[m])
        theirs[m, 640:656, :] = ends[0]
        c = remote(theirs.at[m], twin.at[m], twin_send.at[m], twin_recv.at[m], sibling)
        c.start()
        sends.append(c)
        twins[offset] = c

    def keep(offset):
        m = ORDER.index(offset)
        class_sums(core, offset, mine.at[m])
        mine[m, 640:656, :] = ends[1]

    to_twin(4)
    keep(4)
    for offset in (3, -3):
        to_twin(offset)
        keep(offset)

    def pair(offset, rows):
        m = ORDER.index(offset)
        return mine[m, rows, :].astype(f32) + twin[m, rows, :].astype(f32)

    pieces = [pl.ds(*p) for p in PIECES]
    orders = {1: (2, 3, 0, 1), -1: (0, 1, 2, 3)}
    ring = {}

    def pass_on(step, direction, p):
        stage, landing, peer = (to_high, from_low, high) if direction > 0 else (to_low, from_high, low)
        n = (step * 2 + (direction > 0)) * 4 + p
        c = remote(stage.at[step, pieces[p]], landing.at[step, pieces[p]], ring_send.at[n], ring_recv.at[n], peer)
        c.start()
        sends.append(c)
        ring[(step, direction, p)] = c

    twins[4].wait_recv()
    for p in (0, 1):
        to_high[0, pieces[p], :] = pair(4, pieces[p]).astype(bf16)
        pass_on(0, 1, p)
        to_low[0, pieces[p + 2], :] = pair(4, pieces[p + 2]).astype(bf16)
        pass_on(0, -1, p + 2)
    for step in (1, 2, 3):
        twins[4 - step].wait_recv()
        twins[step - 4].wait_recv()
        for q in range(4):
            if q == 1:
                for offset in (3 - step, step - 3)[: 1 if step == 3 else 2]:
                    to_twin(offset)
                    keep(offset)
            for direction in (1, -1):
                stage, landing = (to_high, from_low) if direction > 0 else (to_low, from_high)
                p = orders[direction][q]
                value = pair(direction * (4 - step), pieces[p])
                if (step - 1, direction, p) in ring:
                    ring[(step - 1, direction, p)].wait_recv()
                    value = value + landing[step - 1, pieces[p], :].astype(f32)
                stage[step, pieces[p], :] = value.astype(bf16)
                pass_on(step, direction, p)
    twins[0].wait_recv()
    outs = {}
    backs = []

    def spread(offset, direction, p, n):
        where = out_ref.at[core, slot(offset), pieces[p]]
        c = remote(where, where, out_send.at[n * 4 + p], out_recv.at[n * 4 + p], high if direction > 0 else low)
        c.start()
        sends.append(c)
        outs[(offset - direction, direction, p)] = c

    def hand_over(offset, p):
        where = out_ref.at[core, slot(offset), pieces[p]]
        n = ORDER.index(offset) * 4 + p
        c = remote(where, where, back_send.at[n], back_recv.at[n], sibling)
        c.start()
        sends.append(c)
        backs.append(c)

    for q in range(4):
        for direction in (1, -1):
            ring[(3, direction, orders[direction][q])].wait_recv()
        if q < 2:
            continue
        for p in ((0, 2) if q == 2 else (1, 3)):
            value = pair(0, pieces[p]) + from_low[3, pieces[p], :].astype(f32) + from_high[3, pieces[p], :].astype(f32)
            out_ref[core, z, pieces[p], :] = value.astype(bf16)
            spread(0, 1, p, 0)
            spread(0, -1, p, 4)
            hand_over(0, p)
    for hop in (1, 2, 3):
        for p in (0, 2, 1, 3):
            for direction in (1, -1):
                n = hop if direction > 0 else 4 + hop
                offset = -hop * direction
                outs[(offset, direction, p)].wait_recv()
                if hop < 3 or (p < 2) == (direction > 0):
                    spread(offset, direction, p, n)
                hand_over(offset, p)
    for p in range(4):
        outs[(-4, 1, p) if p < 2 else (4, -1, p)].wait_recv()
        hand_over(4, p)
    for c in backs:
        c.wait_recv()
    for c in sends:
        c.wait_send()


def reduce_call(gathered, bank_rows, norms):
    dma = pltpu.SemaphoreType.DMA
    slices = pltpu.VMEM((8, SLICE_ROWS, 128), bf16)
    buffer = pltpu.VMEM((4, SLICE_ROWS, 128), bf16)
    return pl.pallas_call(
        reduce_kernel,
        out_shape=jax.ShapeDtypeStruct((2, 8, SLICE_ROWS, 128), bf16),
        in_specs=[VMEM_SPEC] * 3,
        out_specs=VMEM_SPEC,
        scratch_shapes=[pltpu.VMEM((ROWS, R), bf16)]
        + [slices] * 3
        + [buffer] * 4
        + [dma((8,))] * 2
        + [dma((32,))] * 6,
        compiler_params=pltpu.CompilerParams(collective_id=1, has_side_effects=True, vmem_limit_bytes=32 * MIB),
        name="reduce",
    )(gathered, bank_rows, norms)


def widen_kernel(in_ref, out_ref, counts_ref, wide, small, sem):
    copies = []
    for j in range(8):
        for h in range(2):
            rows, cols = pl.ds(h * 160, 160), pl.ds(j * STEP, STEP)
            for c in range(4):
                start = j * STEP + c * 128
                wide[rows, start : start + 128] = in_ref[h, j, c * 160 : (c + 1) * 160, :].astype(f32)
            c = pltpu.make_async_copy(wide.at[rows, cols], out_ref.at[rows, cols], sem.at[j * 2 + h])
            c.start()
            copies.append(c)
    orient = lax.broadcasted_iota(jnp.int32, (16, 128), 0)
    lane = lax.broadcasted_iota(jnp.int32, (16, 128), 1)
    entry = lax.broadcasted_iota(jnp.int32, (128, 128), 0)
    group = lax.broadcasted_iota(jnp.int32, (128, 128), 1)
    counts = jnp.zeros((16, 128), f32)
    for h in range(2):
        ends = in_ref[h, 0, 640:656, :].astype(f32)
        for first, line, valid in ((0, 0, 128), (128, 8, 32)):
            mine = jnp.where((lane % 16 == orient) & (lane < valid), ends[line : line + 1, :], 0.0).astype(bf16)
            place = (h * 160 + first + entry) // 16 == group
            counts += jnp.dot(mine, place.astype(f32).astype(bf16), preferred_element_type=f32)
    small[...] = counts[:, :C]
    c = pltpu.make_async_copy(small, counts_ref, sem.at[16])
    c.start()
    copies.append(c)
    for c in copies:
        c.wait()


def widen_call(total):
    return pl.pallas_call(
        widen_kernel,
        out_shape=(jax.ShapeDtypeStruct((ROWS, F), f32), jax.ShapeDtypeStruct((16, C), f32)),
        in_specs=[VMEM_SPEC],
        out_specs=(ANY_SPEC, ANY_SPEC),
        scratch_shapes=[pltpu.VMEM((ROWS, F), f32), pltpu.VMEM((16, C), f32), pltpu.SemaphoreType.DMA((17,))],
        compiler_params=pltpu.CompilerParams(vmem_limit_bytes=16 * MIB),
        name="widen",
    )(total)


def body(volume, pick_list, box_counts, orientations, orient_weight, reference_bank):
    bank_rows = jnp.transpose(reference_bank, (1, 0, 2)).reshape(ROWS, F)
    low, high, picks, counts, times, norms = halo_call(
        volume, pick_list, box_counts, orientations, orient_weight, bank_rows
    )
    partial = features_call(picks, counts, base_table(), low, volume, high)
    gathered = gather_call(partial, times)
    total = reduce_call(gathered.reshape(R, WIDE), bank_rows, norms)
    sums, weight_sums = widen_call(total)
    return jnp.transpose(sums.reshape(C, 16, F), (1, 0, 2)), weight_sums


def solution(mesh):
    in_specs = (
        P("tile", "bank", None),
        P(None, "tile", "bank", None),
        P("tile", "bank"),
        P("tile", "bank", None, None),
        P("tile", "bank", None, None),
        P("bank", None, None),
    )
    out_specs = (P("bank", None, None), P("bank", None))
    return jax.shard_map(body, mesh=mesh, in_specs=in_specs, out_specs=out_specs, check_vma=False)
```
